32 devices in a mesh: day: 2 (over y), tm: 4 (over z), sta: 4 (over x, core).
Axes of the slice: x: 2, y: 2, z: 4, core: 2. Of those that a mesh axis runs over, the one named last changes fastest.
Arguments:
- traces: bfloat16 [2048, 24576], P('sta', ('day', 'tm')), parts along dimension 1, may hold values from -12 to 12
- offsets: int32 [24], P(('day', 'tm')), parts along dimension 0, may hold values from 0 to 3072, as said below
- pair_first: int32 [2048], P('sta'), may hold values from 0 to 511
- pair_slot: int32 [2048], P('sta'), may hold values from 0 to 127, as said below
- send_rows: int32 [4, 128], P('sta'), may hold values from 0 to 511, as said below
Outputs:
- correlations: float32 [2048, 2048], P(('day', 'tm'), 'sta'), parts along dimension 0
The draws below stay inside these ranges and needn't reach their ends.
There are 2 independent parts, one for each index of `day`. The reference program is written for one: setup_inputs(seed, part) draws one part's arguments, and reference() takes and returns one part's arrays. A program takes and returns all parts, laid end to end along the dimension named above; an argument that names none is the same for every part. Nothing has to cross between parts.
Inputs may be any that keep to these rules, and one draw needn't show every extreme that they name: offsets[t * 3 + w] lies between w * 1024 and (w + 1) * 1024. For a pair owned by group g whose src = pair_slot // 32 lies two or more groups from g around the cycle of 4 groups (neither g - 1, g nor g + 1 modulo 4), pair_slot mod 32 is below 8. The 32 entries send_rows[s, g * 32 .. (g + 1) * 32 - 1] are distinct.
All inputs are finite; a program needn't handle non-finite values.
Results may differ from the reference program's by a relative error of at most 0.0039.
Values may be sent and summed in bfloat16 or wider, within the bound.
No kernel may reach another device: no remote copies, remote signals or barrier semaphores. Data moves between devices by JAX's collectives and lax.ppermute only.
A program may use at most 64 MiB of HBM per device.

```python
import math
import jax
import jax.numpy as jnp
from jax import lax

STATIONS = 2048
STA_GROUP = 512
WIN = 2048
NF = 512
STEP = 1024
NWB = 3
TB = 3072
SAMPLES = 12288
WINDOWS = 12
CAP = 32
CAP_FAR = 8
PD = 512
PAIRS = 2048
NL = 1024
N_TM = 4


def draw_traces(key, part):
    noise_key, scale_key = jax.random.split(key, 2)
    station_scale = jnp.exp(jax.random.uniform(scale_key, (STATIONS, 1), jnp.float32, math.log(0.03), math.log(3.0)))
    values = station_scale * jax.random.normal(noise_key, (STATIONS, SAMPLES), jnp.float32)
    return jnp.clip(values, -12.0, 12.0).astype(jnp.bfloat16)


def draw_offsets(key, part):
    jitter_key, low_key, high_key = jax.random.split(key, 3)
    blocks = WINDOWS // NWB
    jitter = jax.random.randint(jitter_key, (blocks, NWB), 0, STEP + 1)
    low_block = jax.random.randint(low_key, (), 0, blocks)
    high_block = jax.random.randint(high_key, (), 0, blocks)
    block_index = jnp.arange(blocks)[:, None]
    window_index = jnp.arange(NWB)[None, :]
    jitter = jnp.where((block_index == low_block) & (window_index == 0), 0, jitter)
    jitter = jnp.where((block_index == high_block) & (window_index == NWB - 1), STEP, jitter)
    return (window_index * STEP + jitter).reshape(WINDOWS).astype(jnp.int32)


def draw_pair_first(key, part):
    groups = PAIRS // PD

    def take_one(subkey):
        shuffled = jax.random.permutation(subkey, STA_GROUP)
        return shuffled[jnp.arange(PD) % STA_GROUP]
    return jax.vmap(take_one)(jax.random.split(key, groups)).reshape(PAIRS).astype(jnp.int32)


def draw_pair_slot(key, part):
    groups = PAIRS // PD
    count_key, full_key, source_key, pick_key = jax.random.split(key, 4)
    owner_index = jnp.arange(groups)[:, None]
    source_index = jnp.arange(groups)[None, :]
    distance = jnp.abs(owner_index - source_index)
    distance = jnp.minimum(distance, groups - distance)
    lowest = jnp.where(distance <= 1, max(CAP // 2, 1), 1)
    highest = jnp.where(distance <= 1, CAP + 1, CAP_FAR + 1)
    counts = jax.random.randint(count_key, (groups, groups), lowest, highest)
    counts = jnp.where(distance == 0, CAP, counts)
    full_owner = jax.random.randint(full_key, (), 0, groups)
    counts = jnp.where((owner_index == full_owner) & (distance <= 1), CAP, counts)
    far_source = (full_owner + 2) % groups
    counts = jnp.where((owner_index == full_owner) & (source_index == far_source), CAP_FAR, counts)
    pair_index = jnp.arange(PD)[None, :]
    pick_source = jnp.where(pair_index < groups * CAP, pair_index // CAP, jax.random.randint(source_key, (groups, PD), 0, groups))
    live_count = jnp.take_along_axis(counts, pick_source, axis=1)
    random_slot = jax.random.randint(pick_key, (groups, PD), 0, live_count)
    direct = pair_index % CAP
    slot_inside = jnp.where((pair_index < groups * CAP) & (direct < live_count), direct, random_slot)
    return (pick_source * CAP + slot_inside).reshape(PAIRS).astype(jnp.int32)


def draw_send_rows(key, part):
    groups = STATIONS // STA_GROUP
    blocks = groups * groups
    subkeys = jax.random.split(key, blocks + 1)

    def take_one(subkey):
        return jax.random.permutation(subkey, STA_GROUP)[:CAP]
    regular = jax.vmap(take_one)(subkeys[:blocks]).astype(jnp.int32)
    inner_rows = 1 + jax.random.permutation(subkeys[blocks], STA_GROUP - 2)[:CAP - 2]
    special = jnp.concatenate([jnp.array([0, STA_GROUP - 1], jnp.int32), inner_rows.astype(jnp.int32)])
    chosen = jax.random.randint(jax.random.fold_in(key, 7), (), 0, blocks)
    rows_all = jnp.where((jnp.arange(blocks) == chosen)[:, None], special[None, :], regular)
    return rows_all.reshape(groups, groups * CAP).astype(jnp.int32)


def setup_inputs(seed: int = 0, part: int = 0) -> dict:
    seeds = jax.random.split(jax.random.key(seed), 6)
    own_keys = jax.random.split(jax.random.fold_in(seeds[5], part), 6)
    traces = draw_traces(jax.random.fold_in(jax.random.fold_in(seeds[5], part), 71), part)
    offsets = draw_offsets(jax.random.fold_in(jax.random.fold_in(seeds[5], part), 71), part)
    pair_first = draw_pair_first(jax.random.fold_in(seeds[5], 71), part)
    pair_slot = draw_pair_slot(jax.random.fold_in(seeds[5], 71), part)
    send_rows = draw_send_rows(jax.random.fold_in(seeds[5], 71), part)
    return dict(traces=traces, offsets=offsets, pair_first=pair_first, pair_slot=pair_slot, send_rows=send_rows)


FLOOR = 0.1

def taper_table(length):
    sample_index = jnp.arange(length, dtype=jnp.float32)
    return 0.5 - 0.5 * jnp.cos(2.0 * math.pi * sample_index / length)

def dft_table(length, bin_count):
    sample_index = jnp.arange(length, dtype=jnp.int32)[:, None]
    bin_index = jnp.arange(bin_count, dtype=jnp.int32)[None, :] + 1
    angles = (sample_index * bin_index % length).astype(jnp.float32) * (2.0 * math.pi / length)
    return jnp.concatenate([jnp.cos(angles), -jnp.sin(angles)], axis=1).astype(jnp.bfloat16)

def lag_table(lag_count, length, bin_count):
    lag_shift = jnp.arange(lag_count, dtype=jnp.int32)[:, None] - lag_count // 2
    bin_index = jnp.arange(bin_count, dtype=jnp.int32)[None, :] + 1
    angles = (lag_shift * bin_index % length).astype(jnp.float32) * (2.0 * math.pi / length)
    return jnp.concatenate([jnp.cos(angles), -jnp.sin(angles)], axis=1)

def segments(block_data, starts, length):

    def take_one(start_at):
        return lax.dynamic_slice_in_dim(block_data, start_at, length, axis=1)
    pieces = jax.vmap(take_one)(starts)
    values = pieces.astype(jnp.float32)
    centred = values - lax.optimization_barrier(jnp.mean(values, axis=2, keepdims=True))
    return (centred * taper_table(length)).astype(jnp.bfloat16)

def whiten(spectrum, bin_count):
    real_part = spectrum[..., :bin_count]
    imag_part = spectrum[..., bin_count:]
    amplitude = jnp.sqrt(real_part * real_part + imag_part * imag_part + 1e-06)
    padded = jnp.pad(amplitude, [(0, 0)] * (amplitude.ndim - 1) + [(2, 2)])
    smooth = (padded[..., 0:bin_count] + padded[..., 1:bin_count + 1] + padded[..., 2:bin_count + 2] + padded[..., 3:bin_count + 3] + padded[..., 4:bin_count + 4]) / 5.0
    inverse = 1.0 / jnp.maximum(smooth, FLOOR)
    return (spectrum * jnp.concatenate([inverse, inverse], axis=-1)).astype(jnp.bfloat16)

def cross_terms(first_spec, second_spec, bin_count):
    first_real = first_spec[..., :bin_count].astype(jnp.float32)
    first_imag = first_spec[..., bin_count:].astype(jnp.float32)
    second_real = second_spec[..., :bin_count].astype(jnp.float32)
    second_imag = second_spec[..., bin_count:].astype(jnp.float32)
    return jnp.concatenate([first_real * second_real + first_imag * second_imag, first_imag * second_real - first_real * second_imag], axis=-1)

def reference(traces, offsets, pair_first, pair_slot, send_rows):
    table = dft_table(WIN, NF)
    padded = jnp.concatenate([traces, jnp.zeros((STATIONS, WIN), jnp.bfloat16)], axis=1)
    owner_group = jnp.arange(PAIRS, dtype=jnp.int32) // PD
    first_station = owner_group * STA_GROUP + pair_first
    source = pair_slot // CAP
    column = owner_group * CAP + pair_slot % CAP
    second_station = source * STA_GROUP + send_rows[source, column]

    def block_step(running, block_number):
        block_data = lax.dynamic_slice_in_dim(padded, block_number * TB, TB + WIN, axis=1)
        starts = lax.dynamic_slice_in_dim(offsets, block_number * NWB, NWB)
        segment = segments(block_data, starts, WIN)
        spectrum = jnp.dot(segment.reshape(NWB * STATIONS, WIN), table, preferred_element_type=jnp.float32) * (1.0 / math.sqrt(WIN))
        whitened = whiten(spectrum.reshape(NWB, STATIONS, 2 * NF), NF)
        terms = cross_terms(whitened[:, first_station, :], whitened[:, second_station, :], NF)
        return (running + lax.optimization_barrier(jnp.sum(terms, axis=0)), None)
    cross_sum, _ = lax.scan(block_step, jnp.zeros((PAIRS, 2 * NF), jnp.float32), jnp.arange(N_TM, dtype=jnp.int32))
    lag_rows = lag_table(NL, WIN, NF)
    stacked = jnp.dot(lag_rows, cross_sum.T, precision=lax.Precision.HIGHEST, preferred_element_type=jnp.float32)
    return stacked * (1.0 / math.sqrt(NF * WINDOWS))
```

```python
import functools
import math

import jax
import jax.numpy as jnp
from jax import lax
from jax.experimental import pallas as pl
from jax.experimental.pallas import tpu as pltpu
from jax.sharding import PartitionSpec as P

WIN = 2048
NF = 512
NL = 1024
FLOOR = 0.1
STEP = 1024
HALF = 1024
CAP_FAR = 8
LANES = 128
CHUNKS = WIN // LANES
HC = CHUNKS // 2
QB = NF // 2
ROOT = 1.0 / math.sqrt(WIN)
F32 = jnp.float32
BF16 = jnp.bfloat16
ROWS = 16
VMEM = pl.BlockSpec(memory_space=pltpu.VMEM)
SMEM = pl.BlockSpec(memory_space=pltpu.SMEM)
PARAMS = pltpu.CompilerParams(vmem_limit_bytes=56 << 20)


def shape(dims, dtype):
    return jax.ShapeDtypeStruct(dims, dtype)


def small_tables():
    step = jnp.arange(32, dtype=jnp.int32)[:, None]
    half = jnp.arange(QB, dtype=jnp.int32)
    freq = jnp.concatenate([2 * half + 1, 2 * half + 2])[None, :]
    steps = jnp.concatenate([32 * step, step], axis=0)
    angles = (steps * freq % WIN).astype(F32) * (2.0 * math.pi / WIN)
    return jnp.cos(angles), jnp.sin(angles)


def taper_row():
    index = jnp.arange(WIN, dtype=F32)
    return (0.5 - 0.5 * jnp.cos(2.0 * math.pi * index / WIN))[None, :]


def fill_tables(cos_ref, sin_ref, odd_ref, even_ref):
    def block(a, carry):
        ca = cos_ref[pl.ds(a, 1), :]
        sa = sin_ref[pl.ds(a, 1), :]
        cb = cos_ref[32:64, :]
        sb = sin_ref[32:64, :]
        c = (ca * cb - sa * sb).astype(BF16)
        s = (-(sa * cb + ca * sb)).astype(BF16)
        rows = pl.ds(pl.multiple_of(a * 32, 32), 32)
        odd_ref[rows, :QB] = c[:, :QB]
        odd_ref[rows, QB:] = s[:, :QB]
        even_ref[rows, :QB] = c[:, QB:]
        even_ref[rows, QB:] = s[:, QB:]
        return carry

    lax.fori_loop(0, HALF // 32, block, 0)


def prepare(pick, start, count, taper_ref, turned_ref, even_ref, odd_ref):
    q = start // LANES
    s = start % LANES
    shift = (LANES - s) % LANES
    for c in range(CHUNKS):
        j = (c - q + CHUNKS) % CHUNKS
        turned_ref[:, c * LANES : (c + 1) * LANES] = taper_ref[
            :, pl.ds(pl.multiple_of(j * LANES, LANES), LANES)
        ]
    keep = lax.broadcasted_iota(jnp.int32, (ROWS, LANES), 1) < LANES - s

    def group(i, carry):
        rows = pl.ds(pl.multiple_of(i * ROWS, ROWS), ROWS)
        raw = [pick(rows, c) for c in range(CHUNKS)]
        total = raw[0]
        for c in range(1, CHUNKS):
            total = total + raw[c]
        mean = jnp.sum(total, axis=1, keepdims=True) * (1.0 / WIN)
        rolled = [pltpu.roll(r - mean, shift, 1) for r in raw]
        seg = []
        for c in range(CHUNKS):
            y = jnp.where(keep, rolled[c], rolled[(c + 1) % CHUNKS])
            seg.append((y * turned_ref[:, c * LANES : (c + 1) * LANES]).astype(BF16))
        for c in range(HC):
            j = (c - q + CHUNKS) % CHUNKS
            sign = jnp.where(j < HC, 1.0, -1.0).astype(F32)
            low = seg[c].astype(F32)
            high = seg[c + HC].astype(F32)
            lanes = pl.ds(pl.multiple_of((j % HC) * LANES, LANES), LANES)
            even_ref[rows, lanes] = (low + high).astype(BF16)
            odd_ref[rows, lanes] = ((low - high) * sign).astype(BF16)
        return carry

    lax.fori_loop(0, count // ROWS, group, 0)


def whiten_rows(spec_ref, count, live, out_ref, first_row):
    lane = lax.broadcasted_iota(jnp.int32, (ROWS, QB), 1)
    not_first = lane > 0
    not_last = lane < QB - 1

    def up(x):
        return jnp.where(not_first, pltpu.roll(x, 1, 1), 0.0)

    def down(x):
        return jnp.where(not_last, pltpu.roll(x, QB - 1, 1), 0.0)

    def group(i, carry):
        rows = pl.ds(pl.multiple_of(i * ROWS, ROWS), ROWS)
        o_re = spec_ref[rows, 0:QB] * ROOT
        o_im = spec_ref[rows, QB : 2 * QB] * ROOT
        e_re = spec_ref[rows, 2 * QB : 3 * QB] * ROOT
        e_im = spec_ref[rows, 3 * QB :] * ROOT
        odd = jnp.sqrt(o_re * o_re + o_im * o_im + 1e-06)
        even = jnp.sqrt(e_re * e_re + e_im * e_im + 1e-06)
        both = odd + even
        smooth_odd = (up(both) + both + down(odd)) / 5.0
        smooth_even = (up(even) + both + down(both)) / 5.0
        inv_odd = live / jnp.maximum(smooth_odd, FLOOR)
        inv_even = live / jnp.maximum(smooth_even, FLOOR)
        to = pl.ds(pl.multiple_of(first_row + i * ROWS, ROWS), ROWS)
        out_ref[to, 0:QB] = (o_re * inv_odd).astype(BF16)
        out_ref[to, QB : 2 * QB] = (e_re * inv_even).astype(BF16)
        out_ref[to, 2 * QB : 3 * QB] = (o_im * inv_odd).astype(BF16)
        out_ref[to, 3 * QB :] = (e_im * inv_even).astype(BF16)
        return carry

    lax.fori_loop(0, count // ROWS, group, 0)


def window(pick, start, live, count, taper_ref, turned, even, odd, t_odd, t_even, spec, out_ref, first_row):
    prepare(pick, start, count, taper_ref, turned, even, odd)
    spec[:, : 2 * QB] = jnp.dot(odd[...], t_odd[...], preferred_element_type=F32)
    spec[:, 2 * QB :] = jnp.dot(even[...], t_even[...], preferred_element_type=F32)
    whiten_rows(spec, count, live, out_ref, first_row)


def slots(c):
    return c * LANES + lax.broadcasted_iota(jnp.int32, (ROWS, LANES), 1)


def part(ref, offset, rows, c):
    return ref[rows, offset + c * LANES : offset + (c + 1) * LANES].astype(F32)


def shifted_rows(ref, first):
    def get(rows, offset, c):
        at = pl.ds(pl.multiple_of(rows.start + first, ROWS), ROWS)
        return part(ref, offset, at, c)

    return get


def choose(sel, spectra, out_refs):
    results = []
    for index, spectrum in zip(sel, spectra):
        count = index.shape[0]
        stations = sum(s.shape[0] for s in spectrum)
        hot = (lax.broadcasted_iota(jnp.int32, (count, stations), 1) == index[...]).astype(F32).astype(BF16)
        total = None
        at = 0
        for piece in spectrum:
            term = jnp.dot(hot[:, at : at + piece.shape[0]], piece[...], preferred_element_type=F32)
            total = term if total is None else total + term
            at += piece.shape[0]
        results.append(total)
    return results


def write_chosen(results, near_count, cap, refs):
    for i in range(near_count):
        for w in range(2):
            refs[i][w * cap : (w + 1) * cap, :] = results[w][i * cap : (i + 1) * cap].astype(BF16)
    base = near_count * cap
    for i in range(near_count, len(refs)):
        at = base + (i - near_count) * 2 * CAP_FAR
        refs[i][...] = (
            results[0][at : at + 2 * CAP_FAR] + results[1][at : at + 2 * CAP_FAR]
        ).astype(BF16)


def scratches(count):
    return [
        pltpu.VMEM((1, WIN), F32),
        pltpu.VMEM((count, HALF), BF16),
        pltpu.VMEM((count, HALF), BF16),
        pltpu.VMEM((count, 2 * NF), F32),
    ]


def local_kernel(near_count, cap, block, scal, main, cos_t, sin_t, taper, sel0, sel1, *rest):
    t_odd, t_even, white0, white3 = rest[:4]
    sends = rest[4:-4]
    turned, even, odd, spec = rest[-4:]
    fill_tables(cos_t, sin_t, t_odd, t_even)
    stations = main.shape[0]
    first_start = scal[0]
    last_start = scal[2] - 2 * STEP
    last_live = scal[4].astype(F32)
    for first in range(0, stations, block):
        get = shifted_rows(main, first)

        def pick0(rows, c):
            if c >= HC:
                return get(rows, HALF, c - HC)
            return jnp.where(slots(c) >= first_start, get(rows, 0, c), get(rows, 2 * HALF, c))

        def pick3(rows, c):
            if c >= HC:
                return jnp.zeros((ROWS, LANES), F32)
            return jnp.where(slots(c) >= last_start, get(rows, 2 * HALF, c), 0.0)

        rest_args = (block, taper, turned, even, odd, t_odd, t_even, spec)
        window(pick0, first_start, 1.0, *rest_args, white0, first)
        window(pick3, last_start, last_live, *rest_args, white3, first)
    results = choose((sel0, sel1), ((white0,), (white3,)), sends)
    write_chosen(results, near_count, cap, sends)


def rim_kernel(first, near_count, cap, earlier, last, scal, main, rim, tail, taper, t_odd, t_even, *rest):
    sel0, sel1 = rest[:2]
    before = rest[2 : 2 + 2 * earlier]
    rest = rest[2 + 2 * earlier :]
    white1, white2 = rest[:2]
    sends = rest[2:-4]
    turned, even, odd, spec = rest[-4:]
    count = rim.shape[0]
    start1 = scal[1]
    start2 = scal[3] - 2 * STEP
    live2 = scal[5].astype(F32)
    get = shifted_rows(main, first)

    def pick1(rows, c):
        if c < HC:
            return get(rows, 2 * HALF, c)
        return jnp.where(slots(c) >= start1, get(rows, HALF, c - HC), part(rim, 0, rows, c - HC))

    def pick2(rows, c):
        if c >= HC:
            return get(rows, 0, c - HC)
        return jnp.where(slots(c) >= start2, part(tail, 0, rows, c), get(rows, HALF, c))

    rest_args = (count, taper, turned, even, odd, t_odd, t_even, spec)
    window(pick1, lax.rem(start1, WIN), 1.0, *rest_args, white1, 0)
    window(pick2, start2, live2, *rest_args, white2, 0)
    if last:
        spectra1 = tuple(before[0::2]) + (white1,)
        spectra2 = tuple(before[1::2]) + (white2,)
        results = choose((sel0, sel1), (spectra1, spectra2), sends)
        write_chosen(results, near_count, cap, sends)


def add_pairs(near_count, cap, pieces, first_col, slot_cols, groups, incoming, cross):
    pairs = first_col.shape[0]
    width = incoming.shape[0]
    block = min(pairs, 256)
    for w in range(2):
        for i in range(near_count):
            incoming[i * cap : (i + 1) * cap, :] = pieces[i][w * cap : (w + 1) * cap, :]
        if w == 0:
            at = near_count * cap
            for i in range(near_count, len(pieces)):
                incoming[at : at + 2 * CAP_FAR, :] = pieces[i][...]
                at += 2 * CAP_FAR
            if at < width:
                incoming[at:, :] = jnp.zeros((width - at, 2 * NF), BF16)
        spectrum = groups[w]
        for p in range(0, pairs, block):
            col = first_col[p : p + block, :]
            first = None
            at = 0
            for piece in spectrum:
                n = piece.shape[0]
                hot = (lax.broadcasted_iota(jnp.int32, (block, n), 1) + at == col).astype(F32).astype(BF16)
                term = jnp.dot(hot, piece[...], preferred_element_type=F32)
                first = term if first is None else first + term
                at += n
            hot = (
                lax.broadcasted_iota(jnp.int32, (block, width), 1) == slot_cols[w][p : p + block, :]
            ).astype(F32).astype(BF16)
            second = jnp.dot(hot, incoming[...], preferred_element_type=F32)
            a_i, b_i = first[:, :NF], first[:, NF:]
            a_j, b_j = second[:, :NF], second[:, NF:]
            cross[p : p + block, :NF] += a_i * a_j + b_i * b_j
            cross[p : p + block, NF:] += b_i * a_j - a_i * b_j


def early_kernel(near_count, cap, n_pieces, first_col, slot0, slot1, white0, white3, *rest):
    pieces = rest[:n_pieces]
    cross, incoming = rest[n_pieces:]
    cross[...] = jnp.zeros_like(cross)
    add_pairs(near_count, cap, pieces, first_col, (slot0, slot1), ((white0,), (white3,)), incoming, cross)


def late_kernel(near_count, cap, n_pieces, n_white, n_dest, scale, scal, first_col, slot0, slot1, early, t_odd, t_even, *rest):
    whites = rest[: 2 * n_white]
    pieces = rest[2 * n_white : 2 * n_white + n_pieces]
    rest = rest[2 * n_white + n_pieces :]
    own = rest[0]
    outs = rest[1:n_dest]
    incoming, cross, x_odd, x_even = rest[n_dest:]
    cross[...] = early[...]
    add_pairs(
        near_count, cap, pieces, first_col, (slot0, slot1), (whites[0::2], whites[1::2]), incoming, cross
    )
    lane = lax.broadcasted_iota(jnp.int32, (1, QB), 1)
    s = jnp.where(lane % 2 == 0, scale, -scale).astype(F32)
    x_odd[:, :QB] = (cross[:, NF : NF + QB] * s).astype(BF16)
    x_odd[:, QB:] = (cross[:, :QB] * -s).astype(BF16)
    x_even[:, :QB] = (cross[:, QB:NF] * -s).astype(BF16)
    x_even[:, QB:] = (cross[:, NF + QB :] * -s).astype(BF16)
    rows = own.shape[0]
    me = scal[6]
    dims = (((1,), (1,)), ((), ()))
    for d in list(range(1, n_dest)) + [0]:
        at = pl.ds(pl.multiple_of(lax.rem(me + d, n_dest) * rows, rows), rows)
        value = lax.dot_general(t_odd[at, :], x_odd[...], dims, preferred_element_type=F32)
        value = value + lax.dot_general(t_even[at, :], x_even[...], dims, preferred_element_type=F32)
        if d == 0:
            own[...] = value
        else:
            outs[d - 1][...] = value.astype(BF16)


def cost(flops, moved):
    return pl.CostEstimate(flops=int(flops), bytes_accessed=int(moved), transcendentals=0)


def on_device(traces, offsets, pair_first, pair_slot, send_rows):
    stations, block_len = traces.shape
    n_tm = lax.axis_size("tm")
    n_sta = lax.axis_size("sta")
    windows = offsets.shape[0]
    pairs = pair_first.shape[0]
    cap = send_rows.shape[1] // n_sta
    t = lax.axis_index("tm")
    g = lax.axis_index("sta")

    n_chunks = 2
    rows = stations // n_chunks
    down = [(i + 1, i) for i in range(n_tm - 1)]
    back = [(i, i + 1) for i in range(n_tm - 1)]
    rims, tails = [], []
    for i in range(n_chunks):
        piece = traces[i * rows : (i + 1) * rows]
        rims.append(lax.ppermute(piece[:, :HALF], "tm", down))
        tails.append(lax.ppermute(piece[:, block_len - HALF :], "tm", back))
    before = lax.ppermute(offsets, "tm", back)
    has_before = (t > 0).astype(jnp.int32)
    is_last = (t == n_tm - 1).astype(jnp.int32)
    last_before = jnp.where(t > 0, before[2], 2 * STEP)
    early_scal = jnp.stack([offsets[0], offsets[1], offsets[2], offsets[2], is_last, is_last, t])
    scal = jnp.stack([offsets[0], offsets[1], offsets[2], last_before, is_last, has_before, t])

    near = [0, 1, n_sta - 1] if n_sta > 2 else list(range(n_sta))
    far = [d for d in range(n_sta) if d not in near]
    table = send_rows[0].reshape(n_sta, cap)
    near_rows = [lax.dynamic_index_in_dim(table, lax.rem(g + d, n_sta), keepdims=False) for d in near]
    far_rows = [
        lax.dynamic_index_in_dim(table, lax.rem(g + d, n_sta), keepdims=False)[:CAP_FAR] for d in far
    ]
    none = jnp.full((CAP_FAR,), -1, jnp.int32)
    sel0 = jnp.concatenate(near_rows + [x for r in far_rows for x in (r, none)])[:, None]
    sel1 = jnp.concatenate(near_rows + [x for r in far_rows for x in (none, r)])[:, None]
    n_sel = sel0.shape[0]

    distance = lax.rem(g - pair_slot // cap + n_sta, n_sta)
    inside = pair_slot % cap
    place = jnp.zeros_like(pair_slot)
    stride = jnp.zeros_like(pair_slot)
    for i, d in enumerate(near):
        place = jnp.where(distance == d, i * cap + inside, place)
    for i, d in enumerate(far):
        base = len(near) * cap + i * 2 * CAP_FAR
        place = jnp.where(distance == d, base + inside, place)
        stride = jnp.where(distance == d, CAP_FAR, stride)
    slot0 = place[:, None]
    slot1 = (place + stride)[:, None]
    first_col = pair_first[:, None]
    width = -(-n_sel // LANES) * LANES

    cos_t, sin_t = small_tables()
    taper = taper_row()
    buffers = [shape((2 * cap, 2 * NF), BF16)] * len(near) + [shape((2 * CAP_FAR, 2 * NF), BF16)] * len(far)
    dft_flops = 2 * 2 * HALF * 2 * QB * 2
    spectrum = shape((stations, 2 * NF), BF16)
    local = pl.pallas_call(
        functools.partial(local_kernel, len(near), cap, rows),
        out_shape=[shape((HALF, 2 * QB), BF16)] * 2 + [spectrum] * 2 + buffers,
        in_specs=[SMEM] + [VMEM] * 6,
        out_specs=[VMEM] * (4 + len(buffers)),
        scratch_shapes=scratches(rows),
        compiler_params=PARAMS,
        cost_estimate=cost(dft_flops * stations, 8 << 20),
        name="local_windows",
    )(early_scal, traces, cos_t, sin_t, taper, sel0, sel1)
    t_odd, t_even, white0, white3 = local[:4]

    def exchange(pieces):
        got = []
        for d, piece in zip(near + far, pieces):
            if d == 0:
                got.append(piece)
            else:
                route = [(i, (i + d) % n_sta) for i in range(n_sta)]
                got.append(lax.ppermute(piece, "sta", route))
        return got

    early_in = exchange(local[4:])
    early = pl.pallas_call(
        functools.partial(early_kernel, len(near), cap, len(buffers)),
        out_shape=shape((pairs, 2 * NF), F32),
        in_specs=[VMEM] * (5 + len(buffers)),
        out_specs=VMEM,
        scratch_shapes=[pltpu.VMEM((width, 2 * NF), BF16)],
        compiler_params=PARAMS,
        cost_estimate=cost(2 * 2 * pairs * (stations + width) * 2 * NF, 4 << 20),
        name="early_pairs",
    )(first_col, slot0, slot1, white0, white3, *early_in)

    whites = []
    late_out = None
    for i in range(n_chunks):
        last = i == n_chunks - 1
        chunk = shape((rows, 2 * NF), BF16)
        result = pl.pallas_call(
            functools.partial(rim_kernel, i * rows, len(near), cap, i, last),
            out_shape=[chunk] * 2 + (buffers if last else []),
            in_specs=[SMEM] + [VMEM] * (8 + 2 * i),
            out_specs=[VMEM] * (2 + (len(buffers) if last else 0)),
            scratch_shapes=scratches(rows),
            compiler_params=PARAMS,
            cost_estimate=cost(dft_flops * rows, 4 << 20),
            name="rim_windows_%d" % i,
        )(scal, traces, rims[i], tails[i], taper, t_odd, t_even, sel0, sel1, *whites)
        whites = whites + list(result[:2])
        late_out = result[2:]
    late_in = exchange(late_out)

    lag_rows = NL // n_tm
    scale = 1.0 / math.sqrt(NF * windows * n_tm)
    result = pl.pallas_call(
        functools.partial(late_kernel, len(near), cap, len(buffers), n_chunks, n_tm, scale),
        out_shape=[shape((lag_rows, pairs), F32)] + [shape((lag_rows, pairs), BF16)] * (n_tm - 1),
        in_specs=[SMEM] + [VMEM] * (6 + 2 * n_chunks + len(buffers)),
        out_specs=[VMEM] * n_tm,
        scratch_shapes=[
            pltpu.VMEM((width, 2 * NF), BF16),
            pltpu.VMEM((pairs, 2 * NF), F32),
            pltpu.VMEM((pairs, NF), BF16),
            pltpu.VMEM((pairs, NF), BF16),
        ],
        compiler_params=PARAMS,
        cost_estimate=cost(2 * 2 * pairs * (stations + width) * 2 * NF + 2 * NL * pairs * 2 * NF, 6 << 20),
        name="late_pairs",
    )(scal, first_col, slot0, slot1, early, t_odd, t_even, *whites, *late_in)

    total = result[0]
    for d in range(1, n_tm):
        route = [(i, (i + d) % n_tm) for i in range(n_tm)]
        total = total + lax.ppermute(result[d], "tm", route).astype(F32)
    return total


def solution(mesh):
    in_specs = (P("sta", ("day", "tm")), P(("day", "tm")), P("sta"), P("sta"), P("sta", None))
    out_specs = P(("day", "tm"), "sta")
    return jax.shard_map(
        on_device, mesh=mesh, in_specs=in_specs, out_specs=out_specs, check_vma=False
    )
```

```python
import functools
import math

import jax
import jax.numpy as jnp
import numpy as np
from jax import lax
from jax.experimental import pallas as pl
from jax.experimental.pallas import tpu as pltpu
from jax.sharding import PartitionSpec as P

WIN = 2048
NF = 512
NL = 1024
FLOOR = 0.1
STEP = 1024
HALF = 1024
CAP_FAR = 8
LANES = 128
CHUNKS = WIN // LANES
HC = CHUNKS // 2
QB = NF // 2
ROOT = 1.0 / math.sqrt(WIN)
F32 = jnp.float32
BF16 = jnp.bfloat16
ROWS = 16
UNIT = 512
UNROLL = 2
VMEM = pl.BlockSpec(memory_space=pltpu.VMEM)
SMEM = pl.BlockSpec(memory_space=pltpu.SMEM)


def small_tables():
    step = np.arange(32)[:, None]
    half = np.arange(QB)
    freq = np.concatenate([2 * half + 1, 2 * half + 2])[None, :]
    angles = np.concatenate([32 * step, step], axis=0) * freq % WIN * (2.0 * np.pi / WIN)
    return np.cos(angles).astype(np.float32), np.sin(angles).astype(np.float32)


def taper_row():
    index = np.arange(WIN)
    return (0.5 - 0.5 * np.cos(2.0 * np.pi * index / WIN)).astype(np.float32)[None, :]


def fill_tables(cos_ref, sin_ref, odd_ref, even_ref):
    def block(a, carry):
        ca = cos_ref[pl.ds(a, 1), :]
        sa = sin_ref[pl.ds(a, 1), :]
        cb = cos_ref[32:64, :]
        sb = sin_ref[32:64, :]
        c = (ca * cb - sa * sb).astype(BF16)
        s = (-(sa * cb + ca * sb)).astype(BF16)
        rows = pl.ds(pl.multiple_of(a * 32, 32), 32)
        odd_ref[rows, :QB] = c[:, :QB]
        odd_ref[rows, QB:] = s[:, :QB]
        even_ref[rows, :QB] = c[:, QB:]
        even_ref[rows, QB:] = s[:, QB:]
        return carry

    lax.fori_loop(0, HALF // 32, block, 0)


def prepare(pick, start, count, to, taper_ref, scratch):
    turned_ref, rolled_ref, sums_ref, even_ref, odd_ref = scratch[:5]
    q = start // LANES
    s = start % LANES
    shift = (LANES - s) % LANES
    spots, signs = [], []
    for c in range(CHUNKS):
        j = (c - q + CHUNKS) % CHUNKS
        turned_ref[:, c * LANES : (c + 1) * LANES] = taper_ref[
            :, pl.ds(pl.multiple_of(j * LANES, LANES), LANES)
        ]
        if c < HC:
            spots.append(j % HC)
            signs.append(jnp.where(j < HC, 1.0, -1.0).astype(F32))
    keep = lax.broadcasted_iota(jnp.int32, (ROWS, LANES), 1) < LANES - s

    def turn(i, carry):
        rows = pl.ds(pl.multiple_of(i * ROWS, ROWS), ROWS)
        rolled = [pltpu.roll(pick(rows, c).astype(F32), shift, 1) for c in range(CHUNKS)]
        turned = [jnp.where(keep, rolled[c], rolled[(c + 1) % CHUNKS]) for c in range(CHUNKS)]
        for c in range(CHUNKS):
            rolled_ref[c, rows, :] = turned[c].astype(BF16)
        while len(turned) > 1:
            turned = [turned[2 * k] + turned[2 * k + 1] for k in range(len(turned) // 2)]
        sums_ref[rows, :] = turned[0]
        return carry

    lax.fori_loop(0, count // ROWS, turn, 0, unroll=UNROLL)

    def fold(i, carry):
        rows = pl.ds(pl.multiple_of(i * ROWS, ROWS), ROWS)
        put = pl.ds(pl.multiple_of(to + i * ROWS, ROWS), ROWS)
        mean = jnp.sum(sums_ref[rows, :], axis=1, keepdims=True) * (1.0 / WIN)
        for c in range(HC):
            low = rolled_ref[c, rows, :].astype(F32)
            high = rolled_ref[c + HC, rows, :].astype(F32)
            low = ((low - mean) * turned_ref[:, c * LANES : (c + 1) * LANES]).astype(BF16)
            high = (high - mean) * turned_ref[:, (c + HC) * LANES : (c + HC + 1) * LANES]
            high = high.astype(BF16)
            even_ref[spots[c], put, :] = low + high
            odd_ref[spots[c], put, :] = (low - high) * signs[c].astype(BF16)
        return carry

    lax.fori_loop(0, count // ROWS, fold, 0, unroll=UNROLL)


def transform(t_odd, t_even, scratch):
    even_ref, odd_ref, spec = scratch[3:6]
    odd = jnp.concatenate([odd_ref[c] for c in range(HC)], axis=1)
    spec[:, : 2 * QB] = jnp.dot(odd, t_odd[...], preferred_element_type=F32)
    even = jnp.concatenate([even_ref[c] for c in range(HC)], axis=1)
    spec[:, 2 * QB :] = jnp.dot(even, t_even[...], preferred_element_type=F32)


def whiten_rows(first_row, count, live, out_ref, scratch):
    spec_ref = scratch[5]
    lane = lax.broadcasted_iota(jnp.int32, (ROWS, QB), 1)
    not_first = lane > 0
    not_last = lane < QB - 1
    numerator = live * (5.0 * ROOT)

    def up(x):
        return jnp.where(not_first, pltpu.roll(x, 1, 1), 0.0)

    def down(x):
        return jnp.where(not_last, pltpu.roll(x, QB - 1, 1), 0.0)

    def amplitude(re, im):
        power = (re * re + im * im) * (1.0 / WIN) + 1e-06
        return power * lax.rsqrt(power)

    def group(i, carry):
        rows = pl.ds(pl.multiple_of(first_row + i * ROWS, ROWS), ROWS)
        o_re = spec_ref[rows, 0:QB]
        o_im = spec_ref[rows, QB : 2 * QB]
        e_re = spec_ref[rows, 2 * QB : 3 * QB]
        e_im = spec_ref[rows, 3 * QB :]
        odd = amplitude(o_re, o_im)
        even = amplitude(e_re, e_im)
        both = odd + even
        inv_odd = numerator / jnp.maximum(up(both) + both + down(odd), 5.0 * FLOOR)
        inv_even = numerator / jnp.maximum(up(even) + both + down(both), 5.0 * FLOOR)
        to = pl.ds(pl.multiple_of(i * ROWS, ROWS), ROWS)
        out_ref[to, 0:QB] = (o_re * inv_odd).astype(BF16)
        out_ref[to, QB : 2 * QB] = (e_re * inv_even).astype(BF16)
        out_ref[to, 2 * QB : 3 * QB] = (o_im * inv_odd).astype(BF16)
        out_ref[to, 3 * QB :] = (e_im * inv_even).astype(BF16)
        return carry

    lax.fori_loop(0, count // ROWS, group, 0, unroll=2)


def slots(c):
    return c * LANES + lax.broadcasted_iota(jnp.int32, (ROWS, LANES), 1)


def part(ref, offset, rows, c):
    return ref[rows, offset + c * LANES : offset + (c + 1) * LANES].astype(F32)


def shifted_rows(ref, first):
    def get(rows, offset, c):
        at = pl.ds(pl.multiple_of(rows.start + first, ROWS), ROWS)
        return part(ref, offset, at, c)

    return get


def column(row):
    n = row.shape[1]
    return jnp.transpose(jnp.broadcast_to(row.astype(F32), (LANES, n)))


def one_hot(col, width, first=0):
    pieces = []
    for at in range(0, width, LANES):
        lane = lax.broadcasted_iota(jnp.int32, col.shape, 1) + (first + at)
        pieces.append(jnp.where(lane.astype(F32) == col, 1.0, 0.0).astype(BF16))
    hot = pieces[0] if len(pieces) == 1 else jnp.concatenate(pieces, axis=1)
    return hot[:, :width]


def lookup(col, spectra):
    total = None
    at = 0
    for piece in spectra:
        n = piece.shape[0]
        term = jnp.dot(one_hot(col, n, at), piece[...], preferred_element_type=F32)
        total = term if total is None else total + term
        at += n
    return total


def write_rows(send_rows, spectra, near, far, n_sta, cap, refs):
    g = lax.axis_index("sta")
    lane = lax.broadcasted_iota(jnp.int32, (1, n_sta * cap), 1)
    col = column(send_rows[...])
    hots = one_hot(col, sum(p.shape[0] for p in spectra[0]))
    for w in range(2):
        result = None
        at = 0
        for piece in spectra[w]:
            n = piece.shape[0]
            term = jnp.dot(hots[:, at : at + n], piece[...], preferred_element_type=F32)
            result = term if result is None else result + term
            at += n
        refs[-1][w] = result.astype(BF16)
    rows = refs[-1]
    for ref, d in zip(refs, near + far):
        first = pl.multiple_of(lax.rem(g + d, n_sta) * cap, cap)
        for w in range(2):
            if d in far:
                ref[w * ROWS : (w + 1) * ROWS, :] = rows[w, pl.ds(first, ROWS), :]
            else:
                ref[w * cap : (w + 1) * cap, :] = rows[w, pl.ds(first, cap), :]


def scratches(n_sta, cap):
    return [
        pltpu.VMEM((1, WIN), F32),
        pltpu.VMEM((CHUNKS, UNIT, LANES), BF16),
        pltpu.VMEM((UNIT, LANES), F32),
        pltpu.VMEM((HC, UNIT, LANES), BF16),
        pltpu.VMEM((HC, UNIT, LANES), BF16),
        pltpu.VMEM((UNIT, 2 * NF), F32),
        pltpu.VMEM((2, n_sta * cap, 2 * NF), BF16),
    ]


def local_kernel(groups, offsets, main, cos_t, sin_t, taper, send_rows, *rest):
    t_odd, t_even, white0, white3 = rest[:4]
    scratch = rest[-7:]
    sends = rest[4:-7] + (scratch[6],)
    fill_tables(cos_t, sin_t, t_odd, t_even)
    start0 = offsets[0]
    start3 = offsets[2] - 2 * STEP
    live3 = jnp.where(lax.axis_index("tm") == lax.axis_size("tm") - 1, 1.0, 0.0).astype(F32)
    stations = main.shape[0]
    for first in range(0, stations, UNIT):
        count = min(UNIT, stations - first)
        get = shifted_rows(main, first)

        def pick0(rows, c):
            if c >= HC:
                return get(rows, HALF, c - HC)
            return jnp.where(slots(c) >= start0, get(rows, 0, c), get(rows, 2 * HALF, c))

        def pick3(rows, c):
            if c >= HC:
                return jnp.zeros((ROWS, LANES), F32)
            return jnp.where(slots(c) >= start3, get(rows, 2 * HALF, c), 0.0)

        for pick, start, live, white in ((pick0, start0, 1.0, white0), (pick3, start3, live3, white3)):
            prepare(pick, start, count, 0, taper, scratch)
            transform(t_odd, t_even, scratch)
            whiten_rows(0, count, live, white.at[first : first + count], scratch)
    write_rows(send_rows, ((white0,), (white3,)), *groups, sends)


def rim_kernel(groups, first, earlier, last, offsets, before, main, rim, tail, taper, t_odd, t_even, send_rows, *rest):
    older = rest[: 2 * earlier]
    white1, white2 = rest[2 * earlier : 2 * earlier + 2]
    scratch = rest[-7:]
    sends = rest[2 * earlier + 2 : -7] + (scratch[6],)
    count = rim.shape[0]
    t = lax.axis_index("tm")
    start1 = offsets[1]
    start2 = jnp.where(t > 0, before[2] - 2 * STEP, 0)
    live2 = jnp.where(t > 0, 1.0, 0.0).astype(F32)
    get = shifted_rows(main, first)

    def pick1(rows, c):
        if c < HC:
            return get(rows, 2 * HALF, c)
        return jnp.where(slots(c) >= start1, get(rows, HALF, c - HC), part(rim, 0, rows, c - HC))

    def pick2(rows, c):
        if c >= HC:
            return get(rows, 0, c - HC)
        return jnp.where(slots(c) >= start2, part(tail, 0, rows, c), get(rows, HALF, c))

    prepare(pick1, lax.rem(start1, WIN), count, 0, taper, scratch)
    prepare(pick2, start2, count, count, taper, scratch)
    transform(t_odd, t_even, scratch)
    whiten_rows(0, count, 1.0, white1, scratch)
    whiten_rows(count, count, live2, white2, scratch)
    if last:
        write_rows(send_rows, (older[0::2] + (white1,), older[1::2] + (white2,)), *groups, sends)


def add_pairs(groups, pieces, pair_first, pair_slot, spectra, incoming, cross):
    near, far, n_sta, cap = groups
    pairs = pair_first.shape[1]
    width = incoming.shape[1]
    for w in range(2):
        at = 0
        for i, d in enumerate(near + far):
            n = ROWS if d in far else cap
            incoming[w, at : at + n, :] = pieces[i][w * n : (w + 1) * n, :]
            at += n
        if at < width:
            incoming[w, at:, :] = jnp.zeros((width - at, 2 * NF), BF16)
    g = lax.axis_index("sta")
    slot = pair_slot[...]
    distance = (g - slot // cap + n_sta) % n_sta
    place = jnp.zeros_like(slot)
    at = 0
    for d in near + far:
        place = jnp.where(distance == d, at + slot % cap, place)
        at += ROWS if d in far else cap
    first_col = column(pair_first[...])
    slot_col = column(place)
    block = min(pairs, 256)
    for p in range(0, pairs, block):
        hot = one_hot(slot_col[p : p + block], width)
        for w in range(2):
            first = lookup(first_col[p : p + block], spectra[w])
            second = jnp.dot(hot, incoming[w], preferred_element_type=F32)
            a_i, b_i = first[:, :NF], first[:, NF:]
            a_j, b_j = second[:, :NF], second[:, NF:]
            cross[p : p + block, :NF] += a_i * a_j + b_i * b_j
            cross[p : p + block, NF:] += b_i * a_j - a_i * b_j


def early_kernel(groups, n_pieces, pair_first, pair_slot, white0, white3, *rest):
    pieces = rest[:n_pieces]
    cross, incoming = rest[n_pieces:]
    cross[...] = jnp.zeros_like(cross)
    add_pairs(groups, pieces, pair_first, pair_slot, ((white0,), (white3,)), incoming, cross)


def late_kernel(groups, n_pieces, n_white, n_dest, scale, pair_first, pair_slot, early, t_odd, t_even, *rest):
    whites = rest[: 2 * n_white]
    pieces = rest[2 * n_white : 2 * n_white + n_pieces]
    rest = rest[2 * n_white + n_pieces :]
    own = rest[0]
    outs = rest[1:n_dest]
    incoming, cross, x_odd, x_even = rest[n_dest:]
    cross[...] = early[...]
    add_pairs(groups, pieces, pair_first, pair_slot, (whites[0::2], whites[1::2]), incoming, cross)
    lane = lax.broadcasted_iota(jnp.int32, (1, QB), 1)
    s = jnp.where(lane % 2 == 0, scale, -scale).astype(F32)
    x_odd[:, :QB] = (cross[:, NF : NF + QB] * s).astype(BF16)
    x_odd[:, QB:] = (cross[:, :QB] * -s).astype(BF16)
    x_even[:, :QB] = (cross[:, QB:NF] * -s).astype(BF16)
    x_even[:, QB:] = (cross[:, NF + QB :] * -s).astype(BF16)
    rows = own.shape[0]
    me = lax.axis_index("tm")
    dims = (((1,), (1,)), ((), ()))
    for d in list(range(1, n_dest)) + [0]:
        at = pl.ds(pl.multiple_of(lax.rem(me + d, n_dest) * rows, rows), rows)
        value = lax.dot_general(t_odd[at, :], x_odd[...], dims, preferred_element_type=F32)
        value = value + lax.dot_general(t_even[at, :], x_even[...], dims, preferred_element_type=F32)
        if d == 0:
            own[...] = value
        else:
            outs[d - 1][...] = value.astype(BF16)


def in_vmem(*arrays):
    return [pltpu.with_memory_space_constraint(a, pltpu.VMEM) for a in arrays]


def params(mib):
    return pltpu.CompilerParams(vmem_limit_bytes=mib << 20)


def cost(flops, moved):
    return pl.CostEstimate(flops=int(flops), bytes_accessed=int(moved), transcendentals=0)


def on_device(traces, offsets, pair_first, pair_slot, send_rows):
    stations, block_len = traces.shape
    n_tm = lax.axis_size("tm")
    n_sta = lax.axis_size("sta")
    windows = offsets.shape[0]
    pairs = pair_first.shape[0]
    cap = send_rows.shape[1] // n_sta

    n_chunks = 2
    rows = stations // n_chunks
    down = [(i + 1, i) for i in range(n_tm - 1)]
    back = [(i, i + 1) for i in range(n_tm - 1)]
    rims, tails = [], []
    for i in range(n_chunks):
        piece = traces[i * rows : (i + 1) * rows]
        rims.append(lax.ppermute(piece[:, :HALF], "tm", down))
        tails.append(lax.ppermute(piece[:, block_len - HALF :], "tm", back))
    before = lax.ppermute(offsets, "tm", back)

    near = [0, 1, n_sta - 1] if n_sta > 2 else list(range(n_sta))
    far = [d for d in range(n_sta) if d not in near]
    groups = (near, far, n_sta, cap)
    width = -(-(len(near) * cap + len(far) * ROWS) // LANES) * LANES
    first_row, slot_row = pair_first[None, :], pair_slot[None, :]
    cos_t, sin_t = (jnp.asarray(x) for x in small_tables())
    taper = jnp.asarray(taper_row())
    main, = in_vmem(traces)

    buffers = [pltpu.VMEM((2 * (ROWS if d in far else cap), 2 * NF), BF16) for d in near + far]
    dft_flops = 2 * 2 * HALF * 2 * QB * 2
    spectrum = pltpu.VMEM((stations, 2 * NF), BF16)
    table = pltpu.VMEM((HALF, 2 * QB), BF16)
    local = pl.pallas_call(
        functools.partial(local_kernel, groups),
        out_shape=[table] * 2 + [spectrum] * 2 + buffers,
        in_specs=[SMEM] + [VMEM] * 5,
        out_specs=[VMEM] * (4 + len(buffers)),
        scratch_shapes=scratches(n_sta, cap),
        compiler_params=params(14),
        cost_estimate=cost(dft_flops * stations, 8 << 20),
        name="local_windows",
    )(offsets, main, cos_t, sin_t, taper, send_rows)
    t_odd, t_even, white0, white3 = local[:4]

    def exchange(pieces):
        got = []
        for d, piece in zip(near + far, pieces):
            if d == 0:
                got.append(piece)
            else:
                route = [(i, (i + d) % n_sta) for i in range(n_sta)]
                got.append(lax.ppermute(piece, "sta", route))
        return got

    early_in = exchange(local[4:])
    early = pl.pallas_call(
        functools.partial(early_kernel, groups, len(buffers)),
        out_shape=pltpu.VMEM((pairs, 2 * NF), F32),
        in_specs=[VMEM] * (4 + len(buffers)),
        out_specs=VMEM,
        scratch_shapes=[pltpu.VMEM((2, width, 2 * NF), BF16)],
        compiler_params=params(12),
        cost_estimate=cost(2 * 2 * pairs * (stations + width) * 2 * NF, 4 << 20),
        name="early_pairs",
    )(first_row, slot_row, *in_vmem(white0, white3, *early_in))

    whites = []
    late_out = None
    for i in range(n_chunks):
        last = i == n_chunks - 1
        chunk = pltpu.VMEM((rows, 2 * NF), BF16)
        result = pl.pallas_call(
            functools.partial(rim_kernel, groups, i * rows, i, last),
            out_shape=[chunk] * 2 + (buffers if last else []),
            in_specs=[SMEM] * 2 + [VMEM] * (7 + 2 * i),
            out_specs=[VMEM] * (2 + (len(buffers) if last else 0)),
            scratch_shapes=scratches(n_sta, cap),
            compiler_params=params(14),
            cost_estimate=cost(dft_flops * rows, 4 << 20),
            name="rim_windows_%d" % i,
        )(offsets, before, *in_vmem(main, rims[i], tails[i]), taper, *in_vmem(t_odd, t_even), send_rows, *in_vmem(*whites))
        whites = whites + list(result[:2])
        late_out = result[2:]
    late_in = exchange(late_out)

    lag_rows = NL // n_tm
    scale = 1.0 / math.sqrt(NF * windows * n_tm)
    result = pl.pallas_call(
        functools.partial(late_kernel, groups, len(buffers), n_chunks, n_tm, scale),
        out_shape=[pltpu.VMEM((lag_rows, pairs), F32)] + [pltpu.VMEM((lag_rows, pairs), BF16)] * (n_tm - 1),
        in_specs=[VMEM] * (5 + 2 * n_chunks + len(buffers)),
        out_specs=[VMEM] * n_tm,
        scratch_shapes=[
            pltpu.VMEM((2, width, 2 * NF), BF16),
            pltpu.VMEM((pairs, 2 * NF), F32),
            pltpu.VMEM((pairs, NF), BF16),
            pltpu.VMEM((pairs, NF), BF16),
        ],
        compiler_params=params(14),
        cost_estimate=cost(2 * 2 * pairs * (stations + width) * 2 * NF + 2 * NL * pairs * 2 * NF, 6 << 20),
        name="late_pairs",
    )(first_row, slot_row, *in_vmem(early, t_odd, t_even, *whites, *late_in))

    total = result[0]
    for d in range(1, n_tm):
        route = [(i, (i + d) % n_tm) for i in range(n_tm)]
        total = total + lax.ppermute(result[d], "tm", route).astype(F32)
    return total


def solution(mesh):
    in_specs = (P("sta", ("day", "tm")), P(("day", "tm")), P("sta"), P("sta"), P("sta", None))
    out_specs = P(("day", "tm"), "sta")
    return jax.shard_map(
        on_device, mesh=mesh, in_specs=in_specs, out_specs=out_specs, check_vma=False
    )
```

```python
import functools
import math

import jax
import jax.numpy as jnp
import numpy as np
from jax import lax
from jax.experimental import pallas as pl
from jax.experimental.pallas import tpu as pltpu
from jax.sharding import PartitionSpec as P

WIN = 2048
NF = 512
NL = 1024
FLOOR = 0.1
STEP = 1024
HALF = 1024
CAP_FAR = 8
LANES = 128
CHUNKS = WIN // LANES
HC = CHUNKS // 2
QB = NF // 2
ROOT = 1.0 / math.sqrt(WIN)
F32 = jnp.float32
BF16 = jnp.bfloat16
ROWS = 16
UNIT = 512
TURN_UNROLL = 4
FOLD_UNROLL = 4
WHITEN_UNROLL = 8
VMEM = pl.BlockSpec(memory_space=pltpu.VMEM)
SMEM = pl.BlockSpec(memory_space=pltpu.SMEM)


def small_tables():
    step = np.arange(32)[:, None]
    half = np.arange(QB)
    freq = np.concatenate([2 * half + 1, 2 * half + 2])[None, :]
    angles = np.concatenate([32 * step, step], axis=0) * freq % WIN * (2.0 * np.pi / WIN)
    return np.cos(angles).astype(np.float32), np.sin(angles).astype(np.float32)


def taper_row():
    index = np.arange(WIN)
    return (0.5 - 0.5 * np.cos(2.0 * np.pi * index / WIN)).astype(np.float32)[None, :]


def fill_tables(cos_ref, sin_ref, odd_ref, even_ref):
    def block(a, carry):
        ca = cos_ref[pl.ds(a, 1), :]
        sa = sin_ref[pl.ds(a, 1), :]
        cb = cos_ref[32:64, :]
        sb = sin_ref[32:64, :]
        c = (ca * cb - sa * sb).astype(BF16)
        s = (-(sa * cb + ca * sb)).astype(BF16)
        rows = pl.ds(pl.multiple_of(a * 32, 32), 32)
        odd_ref[rows, :QB] = c[:, :QB]
        odd_ref[rows, QB:] = s[:, :QB]
        even_ref[rows, :QB] = c[:, QB:]
        even_ref[rows, QB:] = s[:, QB:]
        return carry

    lax.fori_loop(0, HALF // 32, block, 0)


def prepare(pick, start, count, to, taper_ref, scratch):
    turned_ref, rolled_ref, sums_ref, even_ref, odd_ref = scratch[:5]
    q = start // LANES
    s = start % LANES
    shift = (LANES - s) % LANES
    spots, signs = [], []
    for c in range(CHUNKS):
        j = (c - q + CHUNKS) % CHUNKS
        turned_ref[:, c * LANES : (c + 1) * LANES] = taper_ref[
            :, pl.ds(pl.multiple_of(j * LANES, LANES), LANES)
        ]
        if c < HC:
            spots.append(j % HC)
            signs.append(jnp.where(j < HC, 1.0, -1.0).astype(F32))
    keep = lax.broadcasted_iota(jnp.int32, (ROWS, LANES), 1) < LANES - s

    def turn(i, carry):
        rows = pl.ds(pl.multiple_of(i * ROWS, ROWS), ROWS)
        rolled = [pltpu.roll(pick(rows, c).astype(F32), shift, 1) for c in range(CHUNKS)]
        turned = [jnp.where(keep, rolled[c], rolled[(c + 1) % CHUNKS]) for c in range(CHUNKS)]
        for c in range(CHUNKS):
            rolled_ref[c, rows, :] = turned[c]
        while len(turned) > 1:
            turned = [turned[2 * k] + turned[2 * k + 1] for k in range(len(turned) // 2)]
        sums_ref[rows, :] = turned[0]
        return carry

    lax.fori_loop(0, count // ROWS, turn, 0, unroll=TURN_UNROLL)

    def average(i, carry):
        rows = pl.ds(pl.multiple_of(i * 8 * ROWS, ROWS), 8 * ROWS)
        mean = jnp.sum(sums_ref[rows, :], axis=1, keepdims=True) * (1.0 / WIN)
        sums_ref[rows, :] = jnp.broadcast_to(mean, (8 * ROWS, LANES))
        return carry

    lax.fori_loop(0, count // (8 * ROWS), average, 0)

    def fold(i, carry):
        rows = pl.ds(pl.multiple_of(i * ROWS, ROWS), ROWS)
        put = pl.ds(pl.multiple_of(to + i * ROWS, ROWS), ROWS)
        mean = sums_ref[rows, :]
        for c in range(HC):
            low = rolled_ref[c, rows, :]
            high = rolled_ref[c + HC, rows, :]
            low = ((low - mean) * turned_ref[:, c * LANES : (c + 1) * LANES]).astype(BF16)
            high = (high - mean) * turned_ref[:, (c + HC) * LANES : (c + HC + 1) * LANES]
            high = high.astype(BF16)
            even_ref[spots[c], put, :] = low + high
            odd_ref[spots[c], put, :] = (low - high) * signs[c].astype(BF16)
        return carry

    lax.fori_loop(0, count // ROWS, fold, 0, unroll=FOLD_UNROLL)


def transform(t_odd, t_even, scratch):
    even_ref, odd_ref, spec = scratch[3:6]
    odd = jnp.concatenate([odd_ref[c] for c in range(HC)], axis=1)
    spec[:, : 2 * QB] = jnp.dot(odd, t_odd[...], preferred_element_type=F32)
    even = jnp.concatenate([even_ref[c] for c in range(HC)], axis=1)
    spec[:, 2 * QB :] = jnp.dot(even, t_even[...], preferred_element_type=F32)


def whiten_rows(first_row, count, live, out_ref, scratch):
    spec_ref = scratch[5]
    lane = lax.broadcasted_iota(jnp.int32, (ROWS, QB), 1)
    not_first = lane > 0
    not_last = lane < QB - 1
    numerator = live * (5.0 * ROOT)

    def up(x):
        return jnp.where(not_first, pltpu.roll(x, 1, 1), 0.0)

    def down(x):
        return jnp.where(not_last, pltpu.roll(x, QB - 1, 1), 0.0)

    def amplitude(re, im):
        power = (re * re + im * im) * (1.0 / WIN) + 1e-06
        return power * lax.rsqrt(power)

    def group(i, carry):
        rows = pl.ds(pl.multiple_of(first_row + i * ROWS, ROWS), ROWS)
        o_re = spec_ref[rows, 0:QB]
        o_im = spec_ref[rows, QB : 2 * QB]
        e_re = spec_ref[rows, 2 * QB : 3 * QB]
        e_im = spec_ref[rows, 3 * QB :]
        odd = amplitude(o_re, o_im)
        even = amplitude(e_re, e_im)
        both = odd + even
        inv_odd = numerator / jnp.maximum(up(both) + both + down(odd), 5.0 * FLOOR)
        inv_even = numerator / jnp.maximum(up(even) + both + down(both), 5.0 * FLOOR)
        to = pl.ds(pl.multiple_of(i * ROWS, ROWS), ROWS)
        out_ref[to, 0:QB] = (o_re * inv_odd).astype(BF16)
        out_ref[to, QB : 2 * QB] = (e_re * inv_even).astype(BF16)
        out_ref[to, 2 * QB : 3 * QB] = (o_im * inv_odd).astype(BF16)
        out_ref[to, 3 * QB :] = (e_im * inv_even).astype(BF16)
        return carry

    lax.fori_loop(0, count // ROWS, group, 0, unroll=WHITEN_UNROLL)


def slots(c):
    return c * LANES + lax.broadcasted_iota(jnp.int32, (ROWS, LANES), 1)


def part(ref, offset, rows, c):
    return ref[rows, offset + c * LANES : offset + (c + 1) * LANES].astype(F32)


def shifted_rows(ref, first):
    def get(rows, offset, c):
        at = pl.ds(pl.multiple_of(rows.start + first, ROWS), ROWS)
        return part(ref, offset, at, c)

    return get


def column(row):
    n = row.shape[1]
    return jnp.transpose(jnp.broadcast_to(row.astype(F32), (LANES, n)))


def one_hot(col, width, first=0):
    pieces = []
    for at in range(0, width, LANES):
        lane = lax.broadcasted_iota(jnp.int32, col.shape, 1) + (first + at)
        pieces.append(jnp.where(lane.astype(F32) == col, 1.0, 0.0).astype(BF16))
    hot = pieces[0] if len(pieces) == 1 else jnp.concatenate(pieces, axis=1)
    return hot[:, :width]


def lookup(col, spectra):
    total = None
    at = 0
    for piece in spectra:
        n = piece.shape[0]
        term = jnp.dot(one_hot(col, n, at), piece[...], preferred_element_type=F32)
        total = term if total is None else total + term
        at += n
    return total


def write_rows(send_rows, spectra, near, far, n_sta, cap, refs):
    g = lax.axis_index("sta")
    lane = lax.broadcasted_iota(jnp.int32, (1, n_sta * cap), 1)
    col = column(send_rows[...])
    hots = one_hot(col, sum(p.shape[0] for p in spectra[0]))
    for w in range(2):
        result = None
        at = 0
        for piece in spectra[w]:
            n = piece.shape[0]
            term = jnp.dot(hots[:, at : at + n], piece[...], preferred_element_type=F32)
            result = term if result is None else result + term
            at += n
        refs[-1][w] = result.astype(BF16)
    rows = refs[-1]
    for ref, d in zip(refs, near + far):
        first = pl.multiple_of(lax.rem(g + d, n_sta) * cap, cap)
        for w in range(2):
            if d in far:
                ref[w * ROWS : (w + 1) * ROWS, :] = rows[w, pl.ds(first, ROWS), :]
            else:
                ref[w * cap : (w + 1) * cap, :] = rows[w, pl.ds(first, cap), :]


def scratches(n_sta, cap):
    return [
        pltpu.VMEM((1, WIN), F32),
        pltpu.VMEM((CHUNKS, UNIT, LANES), F32),
        pltpu.VMEM((UNIT, LANES), F32),
        pltpu.VMEM((HC, UNIT, LANES), BF16),
        pltpu.VMEM((HC, UNIT, LANES), BF16),
        pltpu.VMEM((UNIT, 2 * NF), F32),
        pltpu.VMEM((2, n_sta * cap, 2 * NF), BF16),
    ]


def local_kernel(groups, offsets, main, cos_t, sin_t, taper, send_rows, *rest):
    t_odd, t_even, white0, white3 = rest[:4]
    scratch = rest[-7:]
    sends = rest[4:-7] + (scratch[6],)
    fill_tables(cos_t, sin_t, t_odd, t_even)
    start0 = offsets[0]
    start3 = offsets[2] - 2 * STEP
    live3 = jnp.where(lax.axis_index("tm") == lax.axis_size("tm") - 1, 1.0, 0.0).astype(F32)
    stations = main.shape[0]
    for first in range(0, stations, UNIT):
        count = min(UNIT, stations - first)
        get = shifted_rows(main, first)

        def pick0(rows, c):
            if c >= HC:
                return get(rows, HALF, c - HC)
            return jnp.where(slots(c) >= start0, get(rows, 0, c), get(rows, 2 * HALF, c))

        def pick3(rows, c):
            if c >= HC:
                return jnp.zeros((ROWS, LANES), F32)
            return jnp.where(slots(c) >= start3, get(rows, 2 * HALF, c), 0.0)

        for pick, start, live, white in ((pick0, start0, 1.0, white0), (pick3, start3, live3, white3)):
            prepare(pick, start, count, 0, taper, scratch)
            transform(t_odd, t_even, scratch)
            whiten_rows(0, count, live, white.at[first : first + count], scratch)
    write_rows(send_rows, ((white0,), (white3,)), *groups, sends)


def swap_routes(n):
    routes = []
    for first in (0, 1):
        partner = list(range(n))
        for i in range(first, n - 1, 2):
            partner[i], partner[i + 1] = i + 1, i
        routes.append(list(enumerate(partner)))
    return routes


def pack_kernel(rows, offsets, main, *outs):
    t = lax.axis_index("tm")
    n = lax.axis_size("tm")
    start = offsets[2] - 2 * STEP
    high, low = start // 8, start % 8
    lane = lax.broadcasted_iota(jnp.int32, (ROWS, HALF), 1)
    for i, out in enumerate(outs):
        chunk, swap = i // 2, i % 2
        at = jnp.where(t % 2 == swap, 2 * HALF, 0)
        lanes = pl.ds(pl.multiple_of(at, LANES), HALF)
        alone = n % 2 != swap
        keep = jnp.where(t == n - 1, 0.0, 1.0).astype(BF16) if alone else None
        for r in range(0, rows, 64):
            value = main[chunk * rows + r : chunk * rows + r + 64, lanes]
            out[r : r + 64, :] = value if keep is None else value * keep
        if chunk == 0:
            out[rows:, :] = jnp.where(lane < NF, high, low).astype(F32).astype(BF16)


def sent_start(ref, rows):
    high = jnp.max(ref[rows:, 0:LANES].astype(F32))
    low = jnp.max(ref[rows:, HALF - LANES :].astype(F32))
    return (high * 8.0 + low).astype(jnp.int32)


def rim_kernel(groups, first, earlier, last, offsets, main, *rest):
    recv = rest[:2]
    heads = rest[2:4] if earlier else recv
    rest = rest[2 + 2 * earlier :]
    taper, t_odd, t_even, send_rows = rest[:4]
    rest = rest[4:]
    older = rest[: 2 * earlier]
    whites = rest[2 * earlier : 2 * earlier + 2]
    scratch = rest[-7:]
    sends = rest[2 * earlier + 2 : -7] + (scratch[6],)
    count = whites[0].shape[0]
    t = lax.axis_index("tm")
    lane = lax.broadcasted_iota(jnp.int32, (ROWS, LANES), 1)
    for swap in range(2):
        ahead = t % 2 == swap
        start = jnp.where(ahead, offsets[1] - STEP, sent_start(heads[swap], count))
        sign = jnp.where(ahead, 1, -1)
        least = jnp.where(ahead, 0, 1)
        whole = jnp.where(ahead, 2 * HALF, 0)
        base = (lane - start) * sign

        def pick(rows, c):
            at = pl.ds(pl.multiple_of(rows.start + first, ROWS), ROWS)
            if c >= HC:
                return main[at, pl.ds(pl.multiple_of(whole + (c - HC) * LANES, LANES), LANES)].astype(F32)
            own = part(main, HALF, at, c)
            return jnp.where(base >= least - sign * (c * LANES), own, part(recv[swap], 0, rows, c))

        prepare(pick, start, count, swap * count, taper, scratch)
    transform(t_odd, t_even, scratch)
    live = jnp.where(t > 0, 1.0, 0.0).astype(F32)
    whiten_rows(0, count, 1.0, whites[0], scratch)
    whiten_rows(count, count, live, whites[1], scratch)
    if last:
        write_rows(send_rows, (older[0::2] + whites[:1], older[1::2] + whites[1:]), *groups, sends)


def add_pairs(groups, pieces, pair_first, pair_slot, spectra, incoming, cross):
    near, far, n_sta, cap = groups
    pairs = pair_first.shape[1]
    width = incoming.shape[1]
    for w in range(2):
        at = 0
        for i, d in enumerate(near + far):
            n = ROWS if d in far else cap
            incoming[w, at : at + n, :] = pieces[i][w * n : (w + 1) * n, :]
            at += n
        if at < width:
            incoming[w, at:, :] = jnp.zeros((width - at, 2 * NF), BF16)
    g = lax.axis_index("sta")
    slot = pair_slot[...]
    distance = (g - slot // cap + n_sta) % n_sta
    place = jnp.zeros_like(slot)
    at = 0
    for d in near + far:
        place = jnp.where(distance == d, at + slot % cap, place)
        at += ROWS if d in far else cap
    first_col = column(pair_first[...])
    slot_col = column(place)
    block = min(pairs, 256)
    for p in range(0, pairs, block):
        hot = one_hot(slot_col[p : p + block], width)
        for w in range(2):
            first = lookup(first_col[p : p + block], spectra[w])
            second = jnp.dot(hot, incoming[w], preferred_element_type=F32)
            a_i, b_i = first[:, :NF], first[:, NF:]
            a_j, b_j = second[:, :NF], second[:, NF:]
            cross[p : p + block, :NF] += a_i * a_j + b_i * b_j
            cross[p : p + block, NF:] += b_i * a_j - a_i * b_j


def early_kernel(groups, n_pieces, pair_first, pair_slot, white0, white3, *rest):
    pieces = rest[:n_pieces]
    cross, incoming = rest[n_pieces:]
    cross[...] = jnp.zeros_like(cross)
    add_pairs(groups, pieces, pair_first, pair_slot, ((white0,), (white3,)), incoming, cross)


def late_kernel(groups, n_pieces, n_white, n_dest, scale, pair_first, pair_slot, early, t_odd, t_even, *rest):
    whites = rest[: 2 * n_white]
    pieces = rest[2 * n_white : 2 * n_white + n_pieces]
    rest = rest[2 * n_white + n_pieces :]
    own = rest[0]
    outs = rest[1:n_dest]
    incoming, cross, x_odd, x_even = rest[n_dest:]
    cross[...] = early[...]
    add_pairs(groups, pieces, pair_first, pair_slot, (whites[0::2], whites[1::2]), incoming, cross)
    lane = lax.broadcasted_iota(jnp.int32, (1, QB), 1)
    s = jnp.where(lane % 2 == 0, scale, -scale).astype(F32)
    x_odd[:, :QB] = (cross[:, NF : NF + QB] * s).astype(BF16)
    x_odd[:, QB:] = (cross[:, :QB] * -s).astype(BF16)
    x_even[:, :QB] = (cross[:, QB:NF] * -s).astype(BF16)
    x_even[:, QB:] = (cross[:, NF + QB :] * -s).astype(BF16)
    rows = own.shape[0]
    me = lax.axis_index("tm")
    dims = (((1,), (1,)), ((), ()))
    for d in list(range(1, n_dest)) + [0]:
        at = pl.ds(pl.multiple_of(lax.rem(me + d, n_dest) * rows, rows), rows)
        value = lax.dot_general(t_odd[at, :], x_odd[...], dims, preferred_element_type=F32)
        value = value + lax.dot_general(t_even[at, :], x_even[...], dims, preferred_element_type=F32)
        if d == 0:
            own[...] = value
        else:
            outs[d - 1][...] = value.astype(BF16)


def in_vmem(*arrays):
    return [pltpu.with_memory_space_constraint(a, pltpu.VMEM) for a in arrays]


def params(mib):
    return pltpu.CompilerParams(vmem_limit_bytes=mib << 20)


def cost(flops, moved):
    return pl.CostEstimate(flops=int(flops), bytes_accessed=int(moved), transcendentals=0)


def on_device(traces, offsets, pair_first, pair_slot, send_rows):
    stations, block_len = traces.shape
    n_tm = lax.axis_size("tm")
    n_sta = lax.axis_size("sta")
    windows = offsets.shape[0]
    pairs = pair_first.shape[0]
    cap = send_rows.shape[1] // n_sta

    n_chunks = 2
    rows = stations // n_chunks
    main, = in_vmem(traces)
    routes = swap_routes(n_tm)
    packed = pl.pallas_call(
        functools.partial(pack_kernel, rows),
        out_shape=[
            pltpu.VMEM((rows + (ROWS if i < 2 else 0), HALF), BF16) for i in range(2 * n_chunks)
        ],
        in_specs=[SMEM, VMEM],
        out_specs=[VMEM] * (2 * n_chunks),
        compiler_params=params(1),
        cost_estimate=cost(0, 4 << 20),
        name="pack_edges",
    )(offsets, main)
    edges = [lax.ppermute(x, "tm", routes[i % 2]) for i, x in enumerate(packed)]

    near = [0, 1, n_sta - 1] if n_sta > 2 else list(range(n_sta))
    far = [d for d in range(n_sta) if d not in near]
    groups = (near, far, n_sta, cap)
    width = -(-(len(near) * cap + len(far) * ROWS) // LANES) * LANES
    first_row, slot_row = pair_first[None, :], pair_slot[None, :]
    cos_t, sin_t = (jnp.asarray(x) for x in small_tables())
    taper = jnp.asarray(taper_row())

    buffers = [pltpu.VMEM((2 * (ROWS if d in far else cap), 2 * NF), BF16) for d in near + far]
    dft_flops = 2 * 2 * HALF * 2 * QB * 2
    spectrum = pltpu.VMEM((stations, 2 * NF), BF16)
    table = pltpu.VMEM((HALF, 2 * QB), BF16)
    local = pl.pallas_call(
        functools.partial(local_kernel, groups),
        out_shape=[table] * 2 + [spectrum] * 2 + buffers,
        in_specs=[SMEM] + [VMEM] * 5,
        out_specs=[VMEM] * (4 + len(buffers)),
        scratch_shapes=scratches(n_sta, cap),
        compiler_params=params(18),
        cost_estimate=cost(dft_flops * stations, 8 << 20),
        name="local_windows",
    )(offsets, main, cos_t, sin_t, taper, send_rows)
    t_odd, t_even, white0, white3 = local[:4]

    def exchange(pieces):
        got = []
        for d, piece in zip(near + far, pieces):
            if d == 0:
                got.append(piece)
            else:
                route = [(i, (i + d) % n_sta) for i in range(n_sta)]
                got.append(lax.ppermute(piece, "sta", route))
        return got

    early_in = exchange(local[4:])
    early = pl.pallas_call(
        functools.partial(early_kernel, groups, len(buffers)),
        out_shape=pltpu.VMEM((pairs, 2 * NF), F32),
        in_specs=[VMEM] * (4 + len(buffers)),
        out_specs=VMEM,
        scratch_shapes=[pltpu.VMEM((2, width, 2 * NF), BF16)],
        compiler_params=params(12),
        cost_estimate=cost(2 * 2 * pairs * (stations + width) * 2 * NF, 4 << 20),
        name="early_pairs",
    )(first_row, slot_row, *in_vmem(white0, white3, *early_in))

    whites = []
    late_out = None
    for i in range(n_chunks):
        last = i == n_chunks - 1
        chunk = pltpu.VMEM((rows, 2 * NF), BF16)
        result = pl.pallas_call(
            functools.partial(rim_kernel, groups, i * rows, i, last),
            out_shape=[chunk] * 2 + (buffers if last else []),
            in_specs=[SMEM] + [VMEM] * (7 + 4 * i),
            out_specs=[VMEM] * (2 + (len(buffers) if last else 0)),
            scratch_shapes=scratches(n_sta, cap),
            compiler_params=params(18),
            cost_estimate=cost(dft_flops * rows, 4 << 20),
            name="rim_windows_%d" % i,
        )(
            offsets,
            *in_vmem(main, *edges[2 * i : 2 * i + 2], *(edges[:2] * i)),
            taper,
            *in_vmem(t_odd, t_even),
            send_rows,
            *in_vmem(*whites),
        )
        whites = whites + list(result[:2])
        late_out = result[2:]
    late_in = exchange(late_out)

    lag_rows = NL // n_tm
    scale = 1.0 / math.sqrt(NF * windows * n_tm)
    result = pl.pallas_call(
        functools.partial(late_kernel, groups, len(buffers), n_chunks, n_tm, scale),
        out_shape=[pltpu.VMEM((lag_rows, pairs), F32)] + [pltpu.VMEM((lag_rows, pairs), BF16)] * (n_tm - 1),
        in_specs=[VMEM] * (5 + 2 * n_chunks + len(buffers)),
        out_specs=[VMEM] * n_tm,
        scratch_shapes=[
            pltpu.VMEM((2, width, 2 * NF), BF16),
            pltpu.VMEM((pairs, 2 * NF), F32),
            pltpu.VMEM((pairs, NF), BF16),
            pltpu.VMEM((pairs, NF), BF16),
        ],
        compiler_params=params(18),
        cost_estimate=cost(2 * 2 * pairs * (stations + width) * 2 * NF + 2 * NL * pairs * 2 * NF, 6 << 20),
        name="late_pairs",
    )(first_row, slot_row, *in_vmem(early, t_odd, t_even, *whites, *late_in))

    total = result[0]
    for d in range(1, n_tm):
        route = [(i, (i + d) % n_tm) for i in range(n_tm)]
        total = total + lax.ppermute(result[d], "tm", route).astype(F32)
    return total


def solution(mesh):
    in_specs = (P("sta", ("day", "tm")), P(("day", "tm")), P("sta"), P("sta"), P("sta", None))
    out_specs = P(("day", "tm"), "sta")
    return jax.shard_map(
        on_device, mesh=mesh, in_specs=in_specs, out_specs=out_specs, check_vma=False
    )
```

```python
import functools
import math

import jax
import jax.numpy as jnp
import numpy as np
from jax import lax
from jax.experimental import pallas as pl
from jax.experimental.pallas import tpu as pltpu
from jax.sharding import PartitionSpec as P

WIN = 2048
NF = 512
NL = 1024
FLOOR = 0.1
STEP = 1024
HALF = 1024
CAP_FAR = 8
LANES = 128
CHUNKS = WIN // LANES
HC = CHUNKS // 2
QB = NF // 2
ROOT = 1.0 / math.sqrt(WIN)
F32 = jnp.float32
BF16 = jnp.bfloat16
ROWS = 16
N_SMALL = 4
UNIT = 512
TURN_UNROLL = 4
FOLD_UNROLL = 4
WHITEN_UNROLL = 8
VMEM = pl.BlockSpec(memory_space=pltpu.VMEM)
SMEM = pl.BlockSpec(memory_space=pltpu.SMEM)
ANY = pl.BlockSpec(memory_space=pltpu.HBM)


def small_tables():
    step = np.arange(32)[:, None]
    half = np.arange(QB)
    freq = np.concatenate([2 * half + 1, 2 * half + 2])[None, :]
    angles = np.concatenate([32 * step, step], axis=0) * freq % WIN * (2.0 * np.pi / WIN)
    return np.cos(angles).astype(np.float32), np.sin(angles).astype(np.float32)


def taper_row():
    index = np.arange(WIN)
    return (0.5 - 0.5 * np.cos(2.0 * np.pi * index / WIN)).astype(np.float32)[None, :]


def fill_tables(cos_ref, sin_ref, odd_ref, even_ref):
    def block(a, carry):
        ca = cos_ref[pl.ds(a, 1), :]
        sa = sin_ref[pl.ds(a, 1), :]
        cb = cos_ref[32:64, :]
        sb = sin_ref[32:64, :]
        c = (ca * cb - sa * sb).astype(BF16)
        s = (-(sa * cb + ca * sb)).astype(BF16)
        rows = pl.ds(pl.multiple_of(a * 32, 32), 32)
        odd_ref[rows, :QB] = c[:, :QB]
        odd_ref[rows, QB:] = s[:, :QB]
        even_ref[rows, :QB] = c[:, QB:]
        even_ref[rows, QB:] = s[:, QB:]
        return carry

    lax.fori_loop(0, HALF // 32, block, 0)


def prepare(pick, start, count, to, taper_ref, scratch):
    turned_ref, rolled_ref, sums_ref, even_ref, odd_ref = scratch[:5]
    q = start // LANES
    s = start % LANES
    shift = (LANES - s) % LANES
    spots, signs = [], []
    for c in range(CHUNKS):
        j = (c - q + CHUNKS) % CHUNKS
        turned_ref[:, c * LANES : (c + 1) * LANES] = taper_ref[
            :, pl.ds(pl.multiple_of(j * LANES, LANES), LANES)
        ]
        if c < HC:
            spots.append(j % HC)
            signs.append(jnp.where(j < HC, 1.0, -1.0).astype(F32))
    keep = lax.broadcasted_iota(jnp.int32, (ROWS, LANES), 1) < LANES - s

    def turn(i, carry):
        rows = pl.ds(pl.multiple_of(i * ROWS, ROWS), ROWS)
        rolled = [pltpu.roll(pick(rows, c).astype(F32), shift, 1) for c in range(CHUNKS)]
        turned = [jnp.where(keep, rolled[c], rolled[(c + 1) % CHUNKS]) for c in range(CHUNKS)]
        for c in range(CHUNKS):
            rolled_ref[c, rows, :] = turned[c]
        while len(turned) > 1:
            turned = [turned[2 * k] + turned[2 * k + 1] for k in range(len(turned) // 2)]
        sums_ref[rows, :] = turned[0]
        return carry

    lax.fori_loop(0, count // ROWS, turn, 0, unroll=TURN_UNROLL)

    def average(i, carry):
        rows = pl.ds(pl.multiple_of(i * 8 * ROWS, ROWS), 8 * ROWS)
        mean = jnp.sum(sums_ref[rows, :], axis=1, keepdims=True) * (1.0 / WIN)
        sums_ref[rows, :] = jnp.broadcast_to(mean, (8 * ROWS, LANES))
        return carry

    lax.fori_loop(0, count // (8 * ROWS), average, 0)

    def fold(i, carry):
        rows = pl.ds(pl.multiple_of(i * ROWS, ROWS), ROWS)
        put = pl.ds(pl.multiple_of(to + i * ROWS, ROWS), ROWS)
        mean = sums_ref[rows, :]
        for c in range(HC):
            low = rolled_ref[c, rows, :]
            high = rolled_ref[c + HC, rows, :]
            low = ((low - mean) * turned_ref[:, c * LANES : (c + 1) * LANES]).astype(BF16)
            high = (high - mean) * turned_ref[:, (c + HC) * LANES : (c + HC + 1) * LANES]
            high = high.astype(BF16)
            even_ref[spots[c], put, :] = low + high
            odd_ref[spots[c], put, :] = (low - high) * signs[c].astype(BF16)
        return carry

    lax.fori_loop(0, count // ROWS, fold, 0, unroll=FOLD_UNROLL)


def transform(t_odd, t_even, scratch):
    even_ref, odd_ref, spec = scratch[3:6]
    odd = jnp.concatenate([odd_ref[c] for c in range(HC)], axis=1)
    spec[:, : 2 * QB] = jnp.dot(odd, t_odd[...], preferred_element_type=F32)
    even = jnp.concatenate([even_ref[c] for c in range(HC)], axis=1)
    spec[:, 2 * QB :] = jnp.dot(even, t_even[...], preferred_element_type=F32)


def whiten_rows(first_row, count, live, out_ref, scratch):
    spec_ref = scratch[5]
    lane = lax.broadcasted_iota(jnp.int32, (ROWS, QB), 1)
    not_first = lane > 0
    not_last = lane < QB - 1
    numerator = live * (5.0 * ROOT)

    def up(x):
        return jnp.where(not_first, pltpu.roll(x, 1, 1), 0.0)

    def down(x):
        return jnp.where(not_last, pltpu.roll(x, QB - 1, 1), 0.0)

    def amplitude(re, im):
        power = (re * re + im * im) * (1.0 / WIN) + 1e-06
        return power * lax.rsqrt(power)

    def group(i, carry):
        rows = pl.ds(pl.multiple_of(first_row + i * ROWS, ROWS), ROWS)
        o_re = spec_ref[rows, 0:QB]
        o_im = spec_ref[rows, QB : 2 * QB]
        e_re = spec_ref[rows, 2 * QB : 3 * QB]
        e_im = spec_ref[rows, 3 * QB :]
        odd = amplitude(o_re, o_im)
        even = amplitude(e_re, e_im)
        both = odd + even
        inv_odd = numerator / jnp.maximum(up(both) + both + down(odd), 5.0 * FLOOR)
        inv_even = numerator / jnp.maximum(up(even) + both + down(both), 5.0 * FLOOR)
        to = pl.ds(pl.multiple_of(i * ROWS, ROWS), ROWS)
        out_ref[to, 0:QB] = (o_re * inv_odd).astype(BF16)
        out_ref[to, QB : 2 * QB] = (e_re * inv_even).astype(BF16)
        out_ref[to, 2 * QB : 3 * QB] = (o_im * inv_odd).astype(BF16)
        out_ref[to, 3 * QB :] = (e_im * inv_even).astype(BF16)
        return carry

    lax.fori_loop(0, count // ROWS, group, 0, unroll=WHITEN_UNROLL)


def slots(c):
    return c * LANES + lax.broadcasted_iota(jnp.int32, (ROWS, LANES), 1)


def part(ref, offset, rows, c):
    return ref[rows, offset + c * LANES : offset + (c + 1) * LANES].astype(F32)


def shifted_rows(ref, first):
    def get(rows, offset, c):
        at = pl.ds(pl.multiple_of(rows.start + first, ROWS), ROWS)
        return part(ref, offset, at, c)

    return get


def column(row):
    n = row.shape[1]
    return jnp.transpose(jnp.broadcast_to(row.astype(F32), (LANES, n)))


def one_hot(col, width, first=0):
    pieces = []
    for at in range(0, width, LANES):
        lane = lax.broadcasted_iota(jnp.int32, col.shape, 1) + (first + at)
        pieces.append(jnp.where(lane.astype(F32) == col, 1.0, 0.0).astype(BF16))
    hot = pieces[0] if len(pieces) == 1 else jnp.concatenate(pieces, axis=1)
    return hot[:, :width]


def write_rows(send_rows, spectra, near, far, n_sta, cap, refs):
    g = lax.axis_index("sta")
    lane = lax.broadcasted_iota(jnp.int32, (1, n_sta * cap), 1)
    col = column(send_rows[...])
    hots = one_hot(col, sum(p.shape[0] for p in spectra[0]))
    for w in range(2):
        result = None
        at = 0
        for piece in spectra[w]:
            n = piece.shape[0]
            term = jnp.dot(hots[:, at : at + n], piece[...], preferred_element_type=F32)
            result = term if result is None else result + term
            at += n
        refs[-1][w] = result.astype(BF16)
    rows = refs[-1]
    for ref, d in zip(refs, near + far):
        first = pl.multiple_of(lax.rem(g + d, n_sta) * cap, cap)
        for w in range(2):
            if d in far:
                ref[w * CAP_FAR : (w + 1) * CAP_FAR, :] = rows[w, pl.ds(first, CAP_FAR), :]
            else:
                ref[w * cap : (w + 1) * cap, :] = rows[w, pl.ds(first, cap), :]


def scratches(n_sta, cap):
    return [
        pltpu.VMEM((1, WIN), F32),
        pltpu.VMEM((CHUNKS, UNIT, LANES), F32),
        pltpu.VMEM((UNIT, LANES), F32),
        pltpu.VMEM((HC, UNIT, LANES), BF16),
        pltpu.VMEM((HC, UNIT, LANES), BF16),
        pltpu.VMEM((UNIT, 2 * NF), F32),
        pltpu.VMEM((2, n_sta * cap, 2 * NF), BF16),
    ]


def local_kernel(groups, offsets, main, cos_t, sin_t, taper, send_rows, *rest):
    t_odd, t_even, white0, white3 = rest[:4]
    scratch = rest[-7:]
    sends = rest[4:-7] + (scratch[6],)
    fill_tables(cos_t, sin_t, t_odd, t_even)
    start0 = offsets[0]
    start3 = offsets[2] - 2 * STEP
    live3 = jnp.where(lax.axis_index("tm") == lax.axis_size("tm") - 1, 1.0, 0.0).astype(F32)
    stations = main.shape[0]
    for first in range(0, stations, UNIT):
        count = min(UNIT, stations - first)
        get = shifted_rows(main, first)

        def pick0(rows, c):
            if c >= HC:
                return get(rows, HALF, c - HC)
            return jnp.where(slots(c) >= start0, get(rows, 0, c), get(rows, 2 * HALF, c))

        def pick3(rows, c):
            if c >= HC:
                return jnp.zeros((ROWS, LANES), F32)
            return jnp.where(slots(c) >= start3, get(rows, 2 * HALF, c), 0.0)

        for pick, start, live, white in ((pick0, start0, 1.0, white0), (pick3, start3, live3, white3)):
            prepare(pick, start, count, 0, taper, scratch)
            transform(t_odd, t_even, scratch)
            whiten_rows(0, count, live, white.at[first : first + count], scratch)
    write_rows(send_rows, ((white0,), (white3,)), *groups, sends)


def swap_routes(n):
    routes = []
    for first in (0, 1):
        partner = list(range(n))
        for i in range(first, n - 1, 2):
            partner[i], partner[i + 1] = i + 1, i
        routes.append(list(enumerate(partner)))
    return routes


def pack_kernel(rows, n_out, offsets, main, *rest):
    small = rest[: N_SMALL]
    outs = rest[N_SMALL : N_SMALL + n_out]
    offsets_out = rest[N_SMALL + n_out]
    small_out = rest[N_SMALL + n_out + 1 : -1]
    sems = rest[-1]
    t = lax.axis_index("tm")
    n = lax.axis_size("tm")

    def edge(i):
        chunk, swap = i // 2, i % 2
        at = jnp.where(t % 2 == swap, 2 * HALF, 0)
        lanes = pl.ds(pl.multiple_of(at, LANES), HALF)
        source = main.at[pl.ds(chunk * rows, rows), lanes]
        return pltpu.make_async_copy(source, outs[i].at[pl.ds(0, rows)], sems.at[i])

    first = pltpu.make_async_copy(offsets, offsets_out, sems.at[n_out])
    first.start()
    copies = []
    for i in range(n_out):
        if n % 2 == i % 2:
            copies.append(edge(i))
            copies[-1].start()
        else:
            @pl.when(t == n - 1)
            def _():
                outs[i][0:rows, :] = jnp.zeros((rows, HALF), BF16)

            @pl.when(t < n - 1)
            def _():
                edge(i).start()
    for k in range(N_SMALL):
        copies.append(pltpu.make_async_copy(small[k], small_out[k], sems.at[n_out + 1 + k]))
        copies[-1].start()
    first.wait()
    start = offsets_out[2] - 2 * STEP
    high, low = start // 8, start % 8
    lane = lax.broadcasted_iota(jnp.int32, (ROWS, HALF), 1)
    for i in range(2):
        outs[i][rows:, :] = jnp.where(lane < NF, high, low).astype(F32).astype(BF16)
    for copy in copies:
        copy.wait()
    for i in range(n_out):
        if n % 2 != i % 2:
            @pl.when(t < n - 1)
            def _():
                edge(i).wait()


def sent_start(ref, rows):
    high = jnp.max(ref[rows:, 0:LANES].astype(F32))
    low = jnp.max(ref[rows:, HALF - LANES :].astype(F32))
    return (high * 8.0 + low).astype(jnp.int32)


def rim_kernel(groups, first, earlier, last, offsets, main, *rest):
    recv = rest[:2]
    heads = rest[2:4] if earlier else recv
    rest = rest[2 + 2 * earlier :]
    taper, t_odd, t_even, send_rows = rest[:4]
    rest = rest[4:]
    older = rest[: 2 * earlier]
    whites = rest[2 * earlier : 2 * earlier + 2]
    scratch = rest[-7:]
    sends = rest[2 * earlier + 2 : -7] + (scratch[6],)
    count = whites[0].shape[0]
    t = lax.axis_index("tm")
    lane = lax.broadcasted_iota(jnp.int32, (ROWS, LANES), 1)
    for swap in range(2):
        ahead = t % 2 == swap
        start = jnp.where(ahead, offsets[1] - STEP, sent_start(heads[swap], count))
        sign = jnp.where(ahead, 1, -1)
        least = jnp.where(ahead, 0, 1)
        whole = jnp.where(ahead, 2 * HALF, 0)
        base = (lane - start) * sign

        def pick(rows, c):
            at = pl.ds(pl.multiple_of(rows.start + first, ROWS), ROWS)
            if c >= HC:
                return main[at, pl.ds(pl.multiple_of(whole + (c - HC) * LANES, LANES), LANES)].astype(F32)
            own = part(main, HALF, at, c)
            return jnp.where(base >= least - sign * (c * LANES), own, part(recv[swap], 0, rows, c))

        prepare(pick, start, count, swap * count, taper, scratch)
    transform(t_odd, t_even, scratch)
    live = jnp.where(t > 0, 1.0, 0.0).astype(F32)
    whiten_rows(0, count, 1.0, whites[0], scratch)
    whiten_rows(count, count, live, whites[1], scratch)
    if last:
        write_rows(send_rows, (older[0::2] + whites[:1], older[1::2] + whites[1:]), *groups, sends)


def slot_table(groups, pair_slot, width):
    near, far, n_sta, cap = groups
    g = lax.axis_index("sta")
    slot = pair_slot[...]
    distance = (g - slot // cap + n_sta) % n_sta
    place = jnp.zeros_like(slot)
    at = 0
    for d in near + far:
        place = jnp.where(distance == d, at + slot % cap, place)
        at += CAP_FAR if d in far else cap
    return one_hot(column(place), width)


def second_rows(groups, pieces, hot, incoming, out):
    near, far, n_sta, cap = groups
    width = incoming.shape[1]
    for w in range(2):
        at = 0
        for i, d in enumerate(near + far):
            n = CAP_FAR if d in far else cap
            incoming[w, at : at + n, :] = pieces[i][w * n : (w + 1) * n, :]
            at += n
        if at < width:
            incoming[w, at:, :] = jnp.zeros((width - at, 2 * NF), BF16)
    for w in range(2):
        for c in range(0, 2 * NF, NF):
            out[w, :, c : c + NF] = jnp.dot(hot[...], incoming[w, :, c : c + NF], preferred_element_type=F32)


def first_rows(hots, spectra, scale, out):
    lane = lax.broadcasted_iota(jnp.int32, (1, QB), 1)
    s = jnp.where(lane % 2 == 0, scale, -scale).astype(F32)
    for c in range(0, 2 * NF, QB):
        total = None
        for hot, piece in zip(hots, spectra):
            term = jnp.dot(hot, piece[:, c : c + QB], preferred_element_type=F32)
            total = term if total is None else total + term
        out[:, c : c + QB] = total * (s if c % NF == 0 else -s)


def station_tables(col, spectra):
    hots, at = [], 0
    for piece in spectra:
        hots.append(one_hot(col, piece.shape[0], at))
        at += piece.shape[0]
    return hots


def add_products(first, second, rows, c, start):
    re_lanes = slice(c, c + LANES)
    im_lanes = slice(NF + c, NF + c + LANES)
    one, two = start
    for w in range(2):
        a_i, b_i = first[w, rows, re_lanes], first[w, rows, im_lanes]
        a_j, b_j = second[w, rows, re_lanes], second[w, rows, im_lanes]
        re = a_i * a_j + b_i * b_j
        im = b_i * a_j - a_i * b_j
        if c < QB:
            one, two = one + im, two - re
        else:
            one, two = one + re, two + im
    return one, two


def early_kernel(groups, n_pieces, n_white, scale, pair_first, pair_slot, white0, white3, *rest):
    whites = rest[: 2 * n_white]
    rest = rest[2 * n_white :]
    pieces = rest[:n_pieces]
    cross, later, hot = rest[n_pieces : n_pieces + 3]
    incoming, first, second = rest[n_pieces + 3 :]
    pairs = pair_first.shape[1]
    col = column(pair_first[...])
    hots = station_tables(col, (white0,))
    first_rows(hots, (white0,), scale, first.at[0])
    first_rows(hots, (white3,), scale, first.at[1])
    hot[...] = slot_table(groups, pair_slot, hot.shape[1])
    second_rows(groups, pieces, hot, incoming, second)

    def group(i, carry):
        rows = pl.ds(pl.multiple_of(i * ROWS, ROWS), ROWS)
        for c in range(0, NF, LANES):
            one, two = add_products(first, second, rows, c, (0.0, 0.0))
            cross[rows, c : c + LANES] = one
            cross[rows, NF + c : NF + c + LANES] = two
        return carry

    lax.fori_loop(0, pairs // ROWS, group, 0, unroll=2)
    hots = station_tables(col, whites[0::2])
    first_rows(hots, whites[0::2], scale, later.at[0])
    first_rows(hots, whites[1::2], scale, later.at[1])


def late_kernel(groups, n_pieces, n_dest, early, first, hot, t_odd, t_even, *rest):
    pieces = rest[:n_pieces]
    own = rest[n_pieces]
    outs = rest[n_pieces + 1 : n_pieces + n_dest]
    incoming, second, x_odd, x_even = rest[n_pieces + n_dest :]
    pairs = early.shape[0]
    second_rows(groups, pieces, hot, incoming, second)

    def group(i, carry):
        rows = pl.ds(pl.multiple_of(i * ROWS, ROWS), ROWS)
        for c in range(0, NF, LANES):
            start = (early[rows, c : c + LANES], early[rows, NF + c : NF + c + LANES])
            one, two = add_products(first, second, rows, c, start)
            out = x_odd if c < QB else x_even
            at = c % QB
            out[rows, at : at + LANES] = one.astype(BF16)
            out[rows, QB + at : QB + at + LANES] = two.astype(BF16)
        return carry

    lax.fori_loop(0, pairs // ROWS, group, 0, unroll=2)
    rows = own.shape[0]
    me = lax.axis_index("tm")
    dims = (((1,), (1,)), ((), ()))
    order = list(range(n_dest))
    spots = [pl.ds(pl.multiple_of(lax.rem(me + d, n_dest) * rows, rows), rows) for d in order]
    odd = jnp.concatenate([t_odd[at, :] for at in spots], axis=0)
    even = jnp.concatenate([t_even[at, :] for at in spots], axis=0)
    value = lax.dot_general(odd, x_odd[...], dims, preferred_element_type=F32)
    value = value + lax.dot_general(even, x_even[...], dims, preferred_element_type=F32)
    for d in order:
        piece = value[d * rows : (d + 1) * rows, :]
        if d == 0:
            own[...] = piece
        else:
            outs[d - 1][...] = piece.astype(BF16)


def in_vmem(*arrays):
    return [pltpu.with_memory_space_constraint(a, pltpu.VMEM) for a in arrays]


def in_smem(*arrays):
    return [pltpu.with_memory_space_constraint(a, pltpu.SMEM) for a in arrays]


def in_hbm(*arrays):
    return [pltpu.with_memory_space_constraint(a, pltpu.HBM) for a in arrays]


def params(mib):
    return pltpu.CompilerParams(vmem_limit_bytes=mib << 20)


def cost(flops, moved):
    return pl.CostEstimate(flops=int(flops), bytes_accessed=int(moved), transcendentals=0)


def on_device(traces, offsets, pair_first, pair_slot, send_rows):
    stations, block_len = traces.shape
    n_tm = lax.axis_size("tm")
    n_sta = lax.axis_size("sta")
    windows = offsets.shape[0]
    pairs = pair_first.shape[0]
    cap = send_rows.shape[1] // n_sta

    n_chunks = 2
    rows = stations // n_chunks
    main, = in_vmem(traces)
    routes = swap_routes(n_tm)
    small = [jnp.asarray(x) for x in small_tables()] + [jnp.asarray(taper_row()), send_rows]
    packed = pl.pallas_call(
        functools.partial(pack_kernel, rows, 2 * n_chunks),
        out_shape=[
            pltpu.VMEM((rows + (ROWS if i < 2 else 0), HALF), BF16) for i in range(2 * n_chunks)
        ]
        + [pltpu.SMEM(offsets.shape, jnp.int32)]
        + [pltpu.VMEM(x.shape, x.dtype) for x in small],
        in_specs=[ANY] * (2 + N_SMALL),
        out_specs=[VMEM] * (2 * n_chunks) + [SMEM] + [VMEM] * N_SMALL,
        scratch_shapes=[pltpu.SemaphoreType.DMA((2 * n_chunks + 1 + N_SMALL,))],
        compiler_params=params(1),
        cost_estimate=cost(0, 4 << 20),
        name="pack_edges",
    )(*in_hbm(offsets, traces, *small))
    starts = packed[2 * n_chunks]
    cos_t, sin_t, taper, send_rows = packed[2 * n_chunks + 1 :]
    packed = packed[: 2 * n_chunks]
    edges = [lax.ppermute(x, "tm", routes[i % 2]) for i, x in enumerate(packed)]

    near = [0, 1, n_sta - 1] if n_sta > 2 else list(range(n_sta))
    far = [d for d in range(n_sta) if d not in near]
    groups = (near, far, n_sta, cap)
    width = -(-(len(near) * cap + len(far) * CAP_FAR) // LANES) * LANES
    first_row, slot_row = pair_first[None, :], pair_slot[None, :]

    buffers = [pltpu.VMEM((2 * (CAP_FAR if d in far else cap), 2 * NF), BF16) for d in near + far]
    dft_flops = 2 * 2 * HALF * 2 * QB * 2
    spectrum = pltpu.VMEM((stations, 2 * NF), BF16)
    table = pltpu.VMEM((HALF, 2 * QB), BF16)
    local = pl.pallas_call(
        functools.partial(local_kernel, groups),
        out_shape=[table] * 2 + [spectrum] * 2 + buffers,
        in_specs=[SMEM] + [VMEM] * 5,
        out_specs=[VMEM] * (4 + len(buffers)),
        scratch_shapes=scratches(n_sta, cap),
        compiler_params=params(18),
        cost_estimate=cost(dft_flops * stations, 8 << 20),
        name="local_windows",
    )(*in_smem(starts), *in_vmem(main, cos_t, sin_t, taper, send_rows))
    t_odd, t_even, white0, white3 = local[:4]

    def exchange(pieces):
        got = []
        for d, piece in zip(near + far, pieces):
            if d == 0:
                got.append(piece)
            else:
                route = [(i, (i + d) % n_sta) for i in range(n_sta)]
                got.append(lax.ppermute(piece, "sta", route))
        return got

    early_in = exchange(local[4:])
    whites = []
    late_out = None
    for i in range(n_chunks):
        last = i == n_chunks - 1
        chunk = pltpu.VMEM((rows, 2 * NF), BF16)
        result = pl.pallas_call(
            functools.partial(rim_kernel, groups, i * rows, i, last),
            out_shape=[chunk] * 2 + (buffers if last else []),
            in_specs=[SMEM] + [VMEM] * (7 + 4 * i),
            out_specs=[VMEM] * (2 + (len(buffers) if last else 0)),
            scratch_shapes=scratches(n_sta, cap),
            compiler_params=params(18),
            cost_estimate=cost(dft_flops * rows, 4 << 20),
            name="rim_windows_%d" % i,
        )(
            *in_smem(starts),
            *in_vmem(main, *edges[2 * i : 2 * i + 2], *(edges[:2] * i)),
            *in_vmem(taper, t_odd, t_even, send_rows, *whites),
        )
        whites = whites + list(result[:2])
        late_out = result[2:]
    late_in = exchange(late_out)
    scale = 1.0 / math.sqrt(NF * windows * n_tm)
    early, first, hot = pl.pallas_call(
        functools.partial(early_kernel, groups, len(buffers), n_chunks, scale),
        out_shape=[
            pltpu.VMEM((pairs, 2 * NF), F32),
            pltpu.VMEM((2, pairs, 2 * NF), F32),
            pltpu.VMEM((pairs, width), BF16),
        ],
        in_specs=[VMEM] * (4 + 2 * n_chunks + len(buffers)),
        out_specs=[VMEM] * 3,
        scratch_shapes=[
            pltpu.VMEM((2, width, 2 * NF), BF16),
            pltpu.VMEM((2, pairs, 2 * NF), F32),
            pltpu.VMEM((2, pairs, 2 * NF), F32),
        ],
        compiler_params=params(16),
        cost_estimate=cost(2 * 2 * pairs * (2 * stations + width) * 2 * NF, 4 << 20),
        name="early_pairs",
    )(first_row, slot_row, *in_vmem(white0, white3, *whites, *early_in))

    lag_rows = NL // n_tm
    result = pl.pallas_call(
        functools.partial(late_kernel, groups, len(buffers), n_tm),
        out_shape=[pltpu.VMEM((lag_rows, pairs), F32)] + [pltpu.VMEM((lag_rows, pairs), BF16)] * (n_tm - 1),
        in_specs=[VMEM] * (5 + len(buffers)),
        out_specs=[VMEM] * n_tm,
        scratch_shapes=[
            pltpu.VMEM((2, width, 2 * NF), BF16),
            pltpu.VMEM((2, pairs, 2 * NF), F32),
            pltpu.VMEM((pairs, NF), BF16),
            pltpu.VMEM((pairs, NF), BF16),
        ],
        compiler_params=params(18),
        cost_estimate=cost(2 * 2 * pairs * width * 2 * NF + 2 * NL * pairs * 2 * NF, 6 << 20),
        name="late_pairs",
    )(*in_vmem(early, first, hot, t_odd, t_even, *late_in))

    total = result[0]
    for d in range(1, n_tm):
        route = [(i, (i + d) % n_tm) for i in range(n_tm)]
        total = total + lax.ppermute(result[d], "tm", route).astype(F32)
    return total


def solution(mesh):
    in_specs = (P("sta", ("day", "tm")), P(("day", "tm")), P("sta"), P("sta"), P("sta", None))
    out_specs = P(("day", "tm"), "sta")
    return jax.shard_map(
        on_device, mesh=mesh, in_specs=in_specs, out_specs=out_specs, check_vma=False
    )
```

```python
import functools
import math

import jax
import jax.numpy as jnp
import numpy as np
from jax import lax
from jax.experimental import pallas as pl
from jax.experimental.pallas import tpu as pltpu
from jax.sharding import PartitionSpec as P

WIN = 2048
NF = 512
NL = 1024
FLOOR = 0.1
STEP = 1024
HALF = 1024
CAP_FAR = 8
LANES = 128
CHUNKS = WIN // LANES
HC = CHUNKS // 2
QB = NF // 2
ROOT = 1.0 / math.sqrt(WIN)
F32 = jnp.float32
BF16 = jnp.bfloat16
ROWS = 16
N_SMALL = 4
UNIT = 512
VMEM = pl.BlockSpec(memory_space=pltpu.VMEM)
SMEM = pl.BlockSpec(memory_space=pltpu.SMEM)
ANY = pl.BlockSpec(memory_space=pltpu.HBM)


def loop(count, most, body):
    trips = count // ROWS
    unroll = max(u for u in range(1, most + 1) if trips % u == 0)
    lax.fori_loop(0, trips, body, 0, unroll=unroll)


def small_tables():
    step = np.arange(32)[:, None]
    half = np.arange(QB)
    freq = np.concatenate([2 * half + 1, 2 * half + 2])[None, :]
    angles = np.concatenate([32 * step, step], axis=0) * freq % WIN * (2.0 * np.pi / WIN)
    return np.cos(angles).astype(np.float32), np.sin(angles).astype(np.float32)


def taper_row():
    index = np.arange(WIN)
    return (0.5 - 0.5 * np.cos(2.0 * np.pi * index / WIN)).astype(np.float32)[None, :]


def fill_tables(cos_ref, sin_ref, odd_ref, even_ref):
    def block(a, carry):
        ca = cos_ref[pl.ds(a, 1), :]
        sa = sin_ref[pl.ds(a, 1), :]
        cb = cos_ref[32:64, :]
        sb = sin_ref[32:64, :]
        c = (ca * cb - sa * sb).astype(BF16)
        s = (-(sa * cb + ca * sb)).astype(BF16)
        rows = pl.ds(pl.multiple_of(a * 32, 32), 32)
        odd_ref[rows, :QB] = c[:, :QB]
        odd_ref[rows, QB:] = s[:, :QB]
        even_ref[rows, :QB] = c[:, QB:]
        even_ref[rows, QB:] = s[:, QB:]
        return carry

    lax.fori_loop(0, HALF // 32, block, 0)


def prepare(pick, start, count, to, taper_ref, scratch):
    turned_ref, rolled_ref, sums_ref, even_ref, odd_ref = scratch[:5]
    q = start // LANES
    s = start % LANES
    shift = (LANES - s) % LANES
    spots, signs = [], []
    for c in range(CHUNKS):
        j = (c - q + CHUNKS) % CHUNKS
        turned_ref[:, c * LANES : (c + 1) * LANES] = taper_ref[
            :, pl.ds(pl.multiple_of(j * LANES, LANES), LANES)
        ]
        if c < HC:
            spots.append(j % HC)
            signs.append(jnp.where(j < HC, 1.0, -1.0).astype(F32))
    keep = lax.broadcasted_iota(jnp.int32, (ROWS, LANES), 1) < LANES - s

    def turn(i, carry):
        rows = pl.ds(pl.multiple_of(i * ROWS, ROWS), ROWS)
        rolled = [pltpu.roll(pick(rows, c).astype(F32), shift, 1) for c in range(CHUNKS)]
        turned = [jnp.where(keep, rolled[c], rolled[(c + 1) % CHUNKS]) for c in range(CHUNKS)]
        for c in range(CHUNKS):
            rolled_ref[c, rows, :] = turned[c]
        while len(turned) > 1:
            turned = [turned[2 * k] + turned[2 * k + 1] for k in range(len(turned) // 2)]
        sums_ref[rows, :] = turned[0]
        return carry

    loop(count, 4, turn)

    def average(i, carry):
        rows = pl.ds(pl.multiple_of(i * ROWS, ROWS), ROWS)
        mean = jnp.sum(sums_ref[rows, :], axis=1, keepdims=True) * (1.0 / WIN)
        sums_ref[rows, :] = jnp.broadcast_to(mean, (ROWS, LANES))
        return carry

    loop(count, 10, average)

    def fold(i, carry):
        rows = pl.ds(pl.multiple_of(i * ROWS, ROWS), ROWS)
        put = pl.ds(pl.multiple_of(to + i * ROWS, ROWS), ROWS)
        mean = sums_ref[rows, :]
        for c in range(HC):
            low = rolled_ref[c, rows, :]
            high = rolled_ref[c + HC, rows, :]
            low = ((low - mean) * turned_ref[:, c * LANES : (c + 1) * LANES]).astype(BF16)
            high = (high - mean) * turned_ref[:, (c + HC) * LANES : (c + HC + 1) * LANES]
            high = high.astype(BF16)
            even_ref[spots[c], put, :] = low + high
            odd_ref[spots[c], put, :] = (low - high) * signs[c].astype(BF16)
        return carry

    loop(count, 4, fold)


def transform(count, t_odd, t_even, scratch):
    even_ref, odd_ref, spec = scratch[3:6]
    odd = jnp.concatenate([odd_ref[c, :count] for c in range(HC)], axis=1)
    spec[:count, : 2 * QB] = jnp.dot(odd, t_odd[...], preferred_element_type=F32)
    even = jnp.concatenate([even_ref[c, :count] for c in range(HC)], axis=1)
    spec[:count, 2 * QB :] = jnp.dot(even, t_even[...], preferred_element_type=F32)


def whiten_rows(first_row, count, live, out_ref, scratch):
    spec_ref = scratch[5]
    lane = lax.broadcasted_iota(jnp.int32, (ROWS, QB), 1)
    not_first = lane > 0
    not_last = lane < QB - 1
    numerator = live * (5.0 * ROOT)

    def up(x):
        return jnp.where(not_first, pltpu.roll(x, 1, 1), 0.0)

    def down(x):
        return jnp.where(not_last, pltpu.roll(x, QB - 1, 1), 0.0)

    def amplitude(re, im):
        power = (re * re + im * im) * (1.0 / WIN) + 1e-06
        return power * lax.rsqrt(power)

    def group(i, carry):
        rows = pl.ds(pl.multiple_of(first_row + i * ROWS, ROWS), ROWS)
        o_re = spec_ref[rows, 0:QB]
        o_im = spec_ref[rows, QB : 2 * QB]
        e_re = spec_ref[rows, 2 * QB : 3 * QB]
        e_im = spec_ref[rows, 3 * QB :]
        odd = amplitude(o_re, o_im)
        even = amplitude(e_re, e_im)
        both = odd + even
        inv_odd = numerator / jnp.maximum(up(both) + both + down(odd), 5.0 * FLOOR)
        inv_even = numerator / jnp.maximum(up(even) + both + down(both), 5.0 * FLOOR)
        to = pl.ds(pl.multiple_of(i * ROWS, ROWS), ROWS)
        out_ref[to, 0:QB] = (o_re * inv_odd).astype(BF16)
        out_ref[to, QB : 2 * QB] = (e_re * inv_even).astype(BF16)
        out_ref[to, 2 * QB : 3 * QB] = (o_im * inv_odd).astype(BF16)
        out_ref[to, 3 * QB :] = (e_im * inv_even).astype(BF16)
        return carry

    loop(count, 8, group)


def slots(c):
    return c * LANES + lax.broadcasted_iota(jnp.int32, (ROWS, LANES), 1)


def part(ref, offset, rows, c):
    return ref[rows, offset + c * LANES : offset + (c + 1) * LANES].astype(F32)


def shifted_rows(ref, first):
    def get(rows, offset, c):
        at = pl.ds(pl.multiple_of(rows.start + first, ROWS), ROWS)
        return part(ref, offset, at, c)

    return get


def column(row):
    n = row.shape[1]
    return jnp.transpose(jnp.broadcast_to(row.astype(F32), (LANES, n)))


def one_hot(col, width, first=0):
    pieces = []
    for at in range(0, width, LANES):
        lane = lax.broadcasted_iota(jnp.int32, col.shape, 1) + (first + at)
        pieces.append(jnp.where(lane.astype(F32) == col, 1.0, 0.0).astype(BF16))
    hot = pieces[0] if len(pieces) == 1 else jnp.concatenate(pieces, axis=1)
    return hot[:, :width]


def write_rows(send_rows, spectra, near, far, n_sta, cap, refs):
    g = lax.axis_index("sta")
    lane = lax.broadcasted_iota(jnp.int32, (1, n_sta * cap), 1)
    col = column(send_rows[...])
    hots = one_hot(col, sum(p.shape[0] for p in spectra[0]))
    for w in range(2):
        result = None
        at = 0
        for piece in spectra[w]:
            n = piece.shape[0]
            term = jnp.dot(hots[:, at : at + n], piece[...], preferred_element_type=F32)
            result = term if result is None else result + term
            at += n
        refs[-1][w] = result.astype(BF16)
    rows = refs[-1]
    for ref, d in zip(refs, near + far):
        first = pl.multiple_of(lax.rem(g + d, n_sta) * cap, cap)
        for w in range(2):
            if d in far:
                ref[w * CAP_FAR : (w + 1) * CAP_FAR, :] = rows[w, pl.ds(first, CAP_FAR), :]
            else:
                ref[w * cap : (w + 1) * cap, :] = rows[w, pl.ds(first, cap), :]


def scratches(n_sta, cap, rows):
    return [
        pltpu.VMEM((1, WIN), F32),
        pltpu.VMEM((CHUNKS, rows, LANES), F32),
        pltpu.VMEM((rows, LANES), F32),
        pltpu.VMEM((HC, rows, LANES), BF16),
        pltpu.VMEM((HC, rows, LANES), BF16),
        pltpu.VMEM((rows, 2 * NF), F32),
        pltpu.VMEM((2, n_sta * cap, 2 * NF), BF16),
    ]


def local_kernel(groups, offsets, main, cos_t, sin_t, taper, send_rows, *rest):
    t_odd, t_even, white0, white3 = rest[:4]
    scratch = rest[-7:]
    sends = rest[4:-7] + (scratch[6],)
    fill_tables(cos_t, sin_t, t_odd, t_even)
    start0 = offsets[0]
    start3 = offsets[2] - 2 * STEP
    live3 = jnp.where(lax.axis_index("tm") == lax.axis_size("tm") - 1, 1.0, 0.0).astype(F32)
    stations = main.shape[0]
    for first in range(0, stations, UNIT):
        count = min(UNIT, stations - first)
        get = shifted_rows(main, first)

        def pick0(rows, c):
            if c >= HC:
                return get(rows, HALF, c - HC)
            return jnp.where(slots(c) >= start0, get(rows, 0, c), get(rows, 2 * HALF, c))

        def pick3(rows, c):
            if c >= HC:
                return jnp.zeros((ROWS, LANES), F32)
            return jnp.where(slots(c) >= start3, get(rows, 2 * HALF, c), 0.0)

        for pick, start, live, white in ((pick0, start0, 1.0, white0), (pick3, start3, live3, white3)):
            prepare(pick, start, count, 0, taper, scratch)
            transform(count, t_odd, t_even, scratch)
            whiten_rows(0, count, live, white.at[first : first + count], scratch)
    write_rows(send_rows, ((white0,), (white3,)), *groups, sends)


def swap_routes(n):
    routes = []
    for first in (0, 1):
        partner = list(range(n))
        for i in range(first, n - 1, 2):
            partner[i], partner[i + 1] = i + 1, i
        routes.append(list(enumerate(partner)))
    return routes


def pack_kernel(sizes, offsets, main, *rest):
    n_out = 2 * len(sizes)
    small = rest[:N_SMALL]
    outs = rest[N_SMALL : N_SMALL + n_out]
    offsets_out = rest[N_SMALL + n_out]
    small_out = rest[N_SMALL + n_out + 1 : -1]
    sems = rest[-1]
    t = lax.axis_index("tm")
    n = lax.axis_size("tm")

    def edge(i):
        chunk, swap = i // 2, i % 2
        at = jnp.where(t % 2 == swap, 2 * HALF, 0)
        lanes = pl.ds(pl.multiple_of(at, LANES), HALF)
        source = main.at[pl.ds(sum(sizes[:chunk]), sizes[chunk]), lanes]
        return pltpu.make_async_copy(source, outs[i].at[pl.ds(0, sizes[chunk])], sems.at[i])

    first = pltpu.make_async_copy(offsets, offsets_out, sems.at[n_out])
    first.start()
    copies = []
    for i in range(n_out):
        if n % 2 == i % 2:
            copies.append(edge(i))
            copies[-1].start()
        else:
            @pl.when(t == n - 1)
            def _():
                outs[i][0 : sizes[i // 2], :] = jnp.zeros((sizes[i // 2], HALF), BF16)

            @pl.when(t < n - 1)
            def _():
                edge(i).start()
    for k in range(N_SMALL):
        copies.append(pltpu.make_async_copy(small[k], small_out[k], sems.at[n_out + 1 + k]))
        copies[-1].start()
    first.wait()
    start = offsets_out[2] - 2 * STEP
    high, low = start // 8, start % 8
    lane = lax.broadcasted_iota(jnp.int32, (ROWS, HALF), 1)
    for i in range(2):
        outs[i][sizes[0] :, :] = jnp.where(lane < NF, high, low).astype(F32).astype(BF16)
    for copy in copies:
        copy.wait()
    for i in range(n_out):
        if n % 2 != i % 2:
            @pl.when(t < n - 1)
            def _():
                edge(i).wait()


def sent_start(ref):
    rows = ref.shape[0] - ROWS
    high = jnp.max(ref[rows:, 0:LANES].astype(F32))
    low = jnp.max(ref[rows:, HALF - LANES :].astype(F32))
    return (high * 8.0 + low).astype(jnp.int32)


def rim_kernel(groups, first, earlier, last, offsets, main, *rest):
    recv = rest[:2]
    heads = rest[2:4] if earlier else recv
    rest = rest[2 + 2 * earlier :]
    taper, t_odd, t_even, send_rows = rest[:4]
    rest = rest[4:]
    older = rest[: 2 * earlier]
    rest = rest[1:] if last else rest
    whites = rest[2 * earlier : 2 * earlier + 2]
    scratch = rest[-7:]
    sends = rest[2 * earlier + 2 : -7] + (scratch[6],)
    count = whites[0].shape[0]
    t = lax.axis_index("tm")
    lane = lax.broadcasted_iota(jnp.int32, (ROWS, LANES), 1)
    for swap in range(2):
        ahead = t % 2 == swap
        start = jnp.where(ahead, offsets[1] - STEP, sent_start(heads[swap]))
        sign = jnp.where(ahead, 1, -1)
        least = jnp.where(ahead, 0, 1)
        whole = jnp.where(ahead, 2 * HALF, 0)
        base = (lane - start) * sign

        def pick(rows, c):
            at = pl.ds(pl.multiple_of(rows.start + first, ROWS), ROWS)
            if c >= HC:
                return main[at, pl.ds(pl.multiple_of(whole + (c - HC) * LANES, LANES), LANES)].astype(F32)
            own = part(main, HALF, at, c)
            return jnp.where(base >= least - sign * (c * LANES), own, part(recv[swap], 0, rows, c))

        prepare(pick, start, count, swap * count, taper, scratch)
    transform(2 * count, t_odd, t_even, scratch)
    live = jnp.where(t > 0, 1.0, 0.0).astype(F32)
    whiten_rows(0, count, 1.0, whites[0], scratch)
    whiten_rows(count, count, live, whites[1], scratch)
    if last:
        write_rows(send_rows, (older[0::2] + whites[:1], older[1::2] + whites[1:]), *groups, sends)


def slot_table(groups, pair_slot, width):
    near, far, n_sta, cap = groups
    g = lax.axis_index("sta")
    slot = pair_slot[...]
    distance = (g - slot // cap + n_sta) % n_sta
    place = jnp.zeros_like(slot)
    at = 0
    for d in near + far:
        place = jnp.where(distance == d, at + slot % cap, place)
        at += CAP_FAR if d in far else cap
    return one_hot(column(place), width)


def second_rows(groups, pieces, hot, first_pair, incoming, out):
    near, far, n_sta, cap = groups
    width = incoming.shape[1]
    for w in range(2):
        at = 0
        for i, d in enumerate(near + far):
            n = CAP_FAR if d in far else cap
            incoming[w, at : at + n, :] = pieces[i][w * n : (w + 1) * n, :]
            at += n
        if at < width:
            incoming[w, at:, :] = jnp.zeros((width - at, 2 * NF), BF16)
    for w in range(2):
        for c in range(0, 2 * NF, NF):
            rows = hot[first_pair : first_pair + out.shape[1], :]
            out[w, :, c : c + NF] = jnp.dot(rows, incoming[w, :, c : c + NF], preferred_element_type=F32)


def first_rows(hots, spectra, scale, out):
    lane = lax.broadcasted_iota(jnp.int32, (1, QB), 1)
    s = jnp.where(lane % 2 == 0, scale, -scale).astype(F32)
    for c in range(0, 2 * NF, QB):
        total = None
        for hot, piece in zip(hots, spectra):
            term = jnp.dot(hot, piece[:, c : c + QB], preferred_element_type=F32)
            total = term if total is None else total + term
        out[:, c : c + QB] = total * (s if c % NF == 0 else -s)


def station_tables(col, spectra):
    hots, at = [], 0
    for piece in spectra:
        hots.append(one_hot(col, piece.shape[0], at))
        at += piece.shape[0]
    return hots


def add_products(first, second, first_at, second_at, c, start):
    re_lanes = slice(c, c + LANES)
    im_lanes = slice(NF + c, NF + c + LANES)
    one, two = start
    for w in range(2):
        a_i, b_i = first[w, first_at, re_lanes], first[w, first_at, im_lanes]
        a_j, b_j = second[w, second_at, re_lanes], second[w, second_at, im_lanes]
        re = a_i * a_j + b_i * b_j
        im = b_i * a_j - a_i * b_j
        if c < QB:
            one, two = one + im, two - re
        else:
            one, two = one + re, two + im
    return one, two


def early_kernel(groups, n_pieces, scale, pair_first, pair_slot, white0, white3, *rest):
    pieces = rest[:n_pieces]
    cross, hot = rest[n_pieces : n_pieces + 2]
    incoming, first, second = rest[n_pieces + 2 :]
    pairs = pair_first.shape[1]
    hots = station_tables(column(pair_first[...]), (white0,))
    first_rows(hots, (white0,), scale, first.at[0])
    first_rows(hots, (white3,), scale, first.at[1])
    hot[...] = slot_table(groups, pair_slot, hot.shape[1])
    second_rows(groups, pieces, hot, 0, incoming, second)

    def group(i, carry):
        rows = pl.ds(pl.multiple_of(i * ROWS, ROWS), ROWS)
        for c in range(0, NF, LANES):
            one, two = add_products(first, second, rows, rows, c, (0.0, 0.0))
            cross[rows, c : c + LANES] = one
            cross[rows, NF + c : NF + c + LANES] = two
        return carry

    loop(pairs, 2, group)


def first_kernel(scale, n_white, pair_first, *rest):
    whites = rest[: 2 * n_white]
    out = rest[2 * n_white]
    hots = station_tables(column(pair_first[...]), whites[0::2])
    first_rows(hots, whites[0::2], scale, out.at[0])
    first_rows(hots, whites[1::2], scale, out.at[1])


def late_kernel(groups, n_pieces, n_dest, first_pair, early, first, hot, t_odd, t_even, *rest):
    pieces = rest[:n_pieces]
    send, keep = rest[n_pieces : n_pieces + 2]
    incoming, second, x_odd, x_even = rest[n_pieces + 2 :]
    pairs = send.shape[1]
    second_rows(groups, pieces, hot, first_pair, incoming, second)

    def group(i, carry):
        rows = pl.ds(pl.multiple_of(i * ROWS, ROWS), ROWS)
        full = pl.ds(pl.multiple_of(first_pair + i * ROWS, ROWS), ROWS)
        for c in range(0, NF, LANES):
            start = (early[full, c : c + LANES], early[full, NF + c : NF + c + LANES])
            one, two = add_products(first, second, full, rows, c, start)
            out = x_odd if c < QB else x_even
            at = c % QB
            out[rows, at : at + LANES] = one.astype(BF16)
            out[rows, QB + at : QB + at + LANES] = two.astype(BF16)
        return carry

    loop(pairs, 2, group)
    lag_rows = NL // n_dest
    me = lax.axis_index("tm")
    dims = (((1,), (1,)), ((), ()))
    for out, order in ((send, range(1, n_dest, 2)), (keep, range(0, n_dest, 2))):
        spots = [
            pl.ds(pl.multiple_of(jnp.bitwise_xor(me, r) * lag_rows, lag_rows), lag_rows) for r in order
        ]
        odd = jnp.concatenate([t_odd[at, :] for at in spots], axis=0)
        even = jnp.concatenate([t_even[at, :] for at in spots], axis=0)
        value = lax.dot_general(odd, x_odd[...], dims, preferred_element_type=F32)
        value = value + lax.dot_general(even, x_even[...], dims, preferred_element_type=F32)
        out[...] = value.astype(out.dtype)


def merge_kernel(lag_rows, keep, received, send, kept):
    for k in range(keep.shape[0] // lag_rows):
        rows = slice(k * lag_rows, (k + 1) * lag_rows)
        out, j = (send, k // 2) if k % 2 else (kept, k // 2)
        value = keep[rows, :] + received[rows, :].astype(F32)
        out[j * lag_rows : (j + 1) * lag_rows, :] = value.astype(out.dtype)


def finish_kernel(*refs):
    out = refs[-1]
    at = 0
    for keep, received in zip(refs[0:-1:2], refs[1:-1:2]):
        width = keep.shape[1]
        out[:, at : at + width] = keep[...] + received[...].astype(F32)
        at += width


def in_vmem(*arrays):
    return [pltpu.with_memory_space_constraint(a, pltpu.VMEM) for a in arrays]


def in_smem(*arrays):
    return [pltpu.with_memory_space_constraint(a, pltpu.SMEM) for a in arrays]


def in_hbm(*arrays):
    return [pltpu.with_memory_space_constraint(a, pltpu.HBM) for a in arrays]


def params(mib):
    return pltpu.CompilerParams(vmem_limit_bytes=mib << 20)


def cost(flops, moved):
    return pl.CostEstimate(flops=int(flops), bytes_accessed=int(moved), transcendentals=0)


def on_device(traces, offsets, pair_first, pair_slot, send_rows):
    stations, block_len = traces.shape
    n_tm = lax.axis_size("tm")
    n_sta = lax.axis_size("sta")
    windows = offsets.shape[0]
    pairs = pair_first.shape[0]
    cap = send_rows.shape[1] // n_sta

    sizes = (stations * 5 // 8, stations * 3 // 8)
    n_chunks = len(sizes)
    main, = in_vmem(traces)
    routes = swap_routes(n_tm)
    small = [jnp.asarray(x) for x in small_tables()] + [jnp.asarray(taper_row()), send_rows]
    packed = pl.pallas_call(
        functools.partial(pack_kernel, sizes),
        out_shape=[
            pltpu.VMEM((sizes[i // 2] + (ROWS if i < 2 else 0), HALF), BF16)
            for i in range(2 * n_chunks)
        ]
        + [pltpu.SMEM(offsets.shape, jnp.int32)]
        + [pltpu.VMEM(x.shape, x.dtype) for x in small],
        in_specs=[ANY] * (2 + N_SMALL),
        out_specs=[VMEM] * (2 * n_chunks) + [SMEM] + [VMEM] * N_SMALL,
        scratch_shapes=[pltpu.SemaphoreType.DMA((2 * n_chunks + 1 + N_SMALL,))],
        compiler_params=params(1),
        cost_estimate=cost(0, 4 << 20),
        name="pack_edges",
    )(*in_hbm(offsets, traces, *small))
    starts = packed[2 * n_chunks]
    cos_t, sin_t, taper, send_rows = packed[2 * n_chunks + 1 :]
    packed = packed[: 2 * n_chunks]
    edges = [lax.ppermute(x, "tm", routes[i % 2]) for i, x in enumerate(packed)]

    near = [0, 1, n_sta - 1] if n_sta > 2 else list(range(n_sta))
    far = [d for d in range(n_sta) if d not in near]
    groups = (near, far, n_sta, cap)
    width = -(-(len(near) * cap + len(far) * CAP_FAR) // LANES) * LANES
    first_row, slot_row = pair_first[None, :], pair_slot[None, :]

    buffers = [pltpu.VMEM((2 * (CAP_FAR if d in far else cap), 2 * NF), BF16) for d in near + far]
    dft_flops = 2 * 2 * HALF * 2 * QB * 2
    spectrum = pltpu.VMEM((stations, 2 * NF), BF16)
    table = pltpu.VMEM((HALF, 2 * QB), BF16)
    local = pl.pallas_call(
        functools.partial(local_kernel, groups),
        out_shape=[table] * 2 + [spectrum] * 2 + buffers,
        in_specs=[SMEM] + [VMEM] * 5,
        out_specs=[VMEM] * (4 + len(buffers)),
        scratch_shapes=scratches(n_sta, cap, UNIT),
        compiler_params=params(18),
        cost_estimate=cost(dft_flops * stations, 8 << 20),
        name="local_windows",
    )(*in_smem(starts), *in_vmem(main, cos_t, sin_t, taper, send_rows))
    t_odd, t_even, white0, white3 = local[:4]

    def exchange(pieces):
        got = []
        for d, piece in zip(near + far, pieces):
            if d == 0:
                got.append(piece)
            else:
                route = [(i, (i + d) % n_sta) for i in range(n_sta)]
                got.append(lax.ppermute(piece, "sta", route))
        return got

    early_in = exchange(local[4:])
    scale = 1.0 / math.sqrt(NF * windows * n_tm)
    pair_scratch = [
        pltpu.VMEM((2, width, 2 * NF), BF16),
        pltpu.VMEM((2, pairs, 2 * NF), F32),
        pltpu.VMEM((2, pairs, 2 * NF), F32),
    ]
    early, hot = pl.pallas_call(
        functools.partial(early_kernel, groups, len(buffers), scale),
        out_shape=[pltpu.VMEM((pairs, 2 * NF), F32), pltpu.VMEM((pairs, width), BF16)],
        in_specs=[VMEM] * (4 + len(buffers)),
        out_specs=[VMEM] * 2,
        scratch_shapes=pair_scratch,
        compiler_params=params(16),
        cost_estimate=cost(2 * 2 * pairs * (stations + width) * 2 * NF, 4 << 20),
        name="early_pairs",
    )(first_row, slot_row, *in_vmem(white0, white3, *early_in))

    whites = []
    late_out = None
    for i in range(n_chunks):
        last = i == n_chunks - 1
        rows = sizes[i]
        chunk = pltpu.VMEM((rows, 2 * NF), BF16)
        result = pl.pallas_call(
            functools.partial(rim_kernel, groups, sum(sizes[:i]), i, last),
            out_shape=[chunk] * 2 + (buffers if last else []),
            in_specs=[SMEM] + [VMEM] * (7 + 4 * i + (1 if last else 0)),
            out_specs=[VMEM] * (2 + (len(buffers) if last else 0)),
            scratch_shapes=scratches(n_sta, cap, 2 * rows),
            compiler_params=params(22),
            cost_estimate=cost(dft_flops * rows, 4 << 20),
            name="rim_windows_%d" % i,
        )(
            *in_smem(starts),
            *in_vmem(main, *edges[2 * i : 2 * i + 2], *(edges[:2] * i)),
            *in_vmem(taper, t_odd, t_even, send_rows, *whites),
            *in_vmem(*([hot] if last else [])),
        )
        whites = whites + list(result[:2])
        late_out = result[2:]
    late_in = exchange(late_out)
    first = pl.pallas_call(
        functools.partial(first_kernel, scale, n_chunks),
        out_shape=pltpu.VMEM((2, pairs, 2 * NF), F32),
        in_specs=[VMEM] * (1 + 2 * n_chunks),
        out_specs=VMEM,
        compiler_params=params(4),
        cost_estimate=cost(2 * 2 * pairs * stations * 2 * NF, 4 << 20),
        name="first_pairs",
    )(first_row, *in_vmem(*whites))

    lag_rows = NL // n_tm
    n_half = 2
    half = pairs // n_half
    steps = [1 << k for k in range(n_tm.bit_length() - 1)]
    done = []
    parts = []
    for h in range(n_half):
        parts.append(
            pl.pallas_call(
                functools.partial(late_kernel, groups, len(buffers), n_tm, h * half),
                out_shape=[pltpu.VMEM((NL // 2, half), BF16), pltpu.VMEM((NL // 2, half), F32)],
                in_specs=[VMEM] * (5 + len(buffers)),
                out_specs=[VMEM] * 2,
                scratch_shapes=[
                    pltpu.VMEM((2, width, 2 * NF), BF16),
                    pltpu.VMEM((2, half, 2 * NF), F32),
                    pltpu.VMEM((half, NF), BF16),
                    pltpu.VMEM((half, NF), BF16),
                ],
                compiler_params=params(10),
                cost_estimate=cost(2 * 2 * half * width * 2 * NF + 2 * NL * half * 2 * NF, 3 << 20),
                name="late_pairs_%d" % h,
            )(*in_vmem(early, first, hot, t_odd, t_even, *late_in))
        )
    for step in steps:
        route = [(i, i ^ step) for i in range(n_tm)]
        received = [lax.ppermute(send, "tm", route) for send, _ in parts]
        if step == steps[-1]:
            done = [x for (_, keep), got in zip(parts, received) for x in (keep, got)]
            break
        merged = []
        for h in range(n_half):
            keep = parts[h][1]
            rows = keep.shape[0] // 2
            merged.append(
                pl.pallas_call(
                    functools.partial(merge_kernel, lag_rows),
                    out_shape=[pltpu.VMEM((rows, half), BF16), pltpu.VMEM((rows, half), F32)],
                    in_specs=[VMEM] * 2,
                    out_specs=[VMEM] * 2,
                    compiler_params=params(1),
                    cost_estimate=cost(rows * half, 1 << 20),
                    name="merge_%d_%d" % (step, h),
                )(*in_vmem(keep, received[h]))
            )
        parts = merged
    return pl.pallas_call(
        finish_kernel,
        out_shape=jax.ShapeDtypeStruct((lag_rows, pairs), F32),
        in_specs=[VMEM] * len(done),
        out_specs=VMEM,
        compiler_params=params(2),
        cost_estimate=cost(lag_rows * pairs, 1 << 20),
        name="finish",
    )(*in_vmem(*done))


def solution(mesh):
    in_specs = (P("sta", ("day", "tm")), P(("day", "tm")), P("sta"), P("sta"), P("sta", None))
    out_specs = P(("day", "tm"), "sta")
    return jax.shard_map(
        on_device, mesh=mesh, in_specs=in_specs, out_specs=out_specs, check_vma=False
    )
```

```python
import functools
import math

import jax
import jax.numpy as jnp
import numpy as np
from jax import lax
from jax.experimental import pallas as pl
from jax.experimental.pallas import tpu as pltpu
from jax.sharding import PartitionSpec as P

WIN = 2048
NF = 512
NL = 1024
FLOOR = 0.1
STEP = 1024
HALF = 1024
CAP_FAR = 8
LANES = 128
CHUNKS = WIN // LANES
HC = CHUNKS // 2
QB = NF // 2
ROOT = 1.0 / math.sqrt(WIN)
F32 = jnp.float32
BF16 = jnp.bfloat16
ROWS = 16
N_SMALL = 4
UNIT = 512
VMEM = pl.BlockSpec(memory_space=pltpu.VMEM)
SMEM = pl.BlockSpec(memory_space=pltpu.SMEM)
ANY = pl.BlockSpec(memory_space=pltpu.HBM)


def loop(count, most, body):
    trips = count // ROWS
    unroll = max(u for u in range(1, most + 1) if trips % u == 0)
    lax.fori_loop(0, trips, body, 0, unroll=unroll)


def small_tables():
    step = np.arange(32)[:, None]
    half = np.arange(QB)
    freq = np.concatenate([2 * half + 1, 2 * half + 2])[None, :]
    angles = np.concatenate([32 * step, step], axis=0) * freq % WIN * (2.0 * np.pi / WIN)
    return np.cos(angles).astype(np.float32), np.sin(angles).astype(np.float32)


def taper_row():
    index = np.arange(WIN)
    return (0.5 - 0.5 * np.cos(2.0 * np.pi * index / WIN)).astype(np.float32)[None, :]


def fill_tables(cos_ref, sin_ref, odd_ref, even_ref):
    def block(a, carry):
        ca = cos_ref[pl.ds(a, 1), :]
        sa = sin_ref[pl.ds(a, 1), :]
        cb = cos_ref[32:64, :]
        sb = sin_ref[32:64, :]
        c = (ca * cb - sa * sb).astype(BF16)
        s = (-(sa * cb + ca * sb)).astype(BF16)
        rows = pl.ds(pl.multiple_of(a * 32, 32), 32)
        odd_ref[rows, :QB] = c[:, :QB]
        odd_ref[rows, QB:] = s[:, :QB]
        even_ref[rows, :QB] = c[:, QB:]
        even_ref[rows, QB:] = s[:, QB:]
        return carry

    lax.fori_loop(0, HALF // 32, block, 0)


def prepare(pick, start, count, to, taper_ref, scratch):
    turned_ref, rolled_ref, sums_ref, even_ref, odd_ref = scratch[:5]
    q = start // LANES
    s = start % LANES
    shift = (LANES - s) % LANES
    spots, signs = [], []
    for c in range(CHUNKS):
        j = (c - q + CHUNKS) % CHUNKS
        turned_ref[:, c * LANES : (c + 1) * LANES] = taper_ref[
            :, pl.ds(pl.multiple_of(j * LANES, LANES), LANES)
        ]
        if c < HC:
            spots.append(j % HC)
            signs.append(jnp.where(j < HC, 1.0, -1.0).astype(F32))
    keep = lax.broadcasted_iota(jnp.int32, (ROWS, LANES), 1) < LANES - s

    def turn(i, carry):
        rows = pl.ds(pl.multiple_of(i * ROWS, ROWS), ROWS)
        rolled = [pltpu.roll(pick(rows, c).astype(F32), shift, 1) for c in range(CHUNKS)]
        turned = [jnp.where(keep, rolled[c], rolled[(c + 1) % CHUNKS]) for c in range(CHUNKS)]
        for c in range(CHUNKS):
            rolled_ref[c, rows, :] = turned[c]
        while len(turned) > 1:
            turned = [turned[2 * k] + turned[2 * k + 1] for k in range(len(turned) // 2)]
        sums_ref[rows, :] = turned[0]
        return carry

    loop(count, 4, turn)

    def average(i, carry):
        rows = pl.ds(pl.multiple_of(i * ROWS, ROWS), ROWS)
        mean = jnp.sum(sums_ref[rows, :], axis=1, keepdims=True) * (1.0 / WIN)
        sums_ref[rows, :] = jnp.broadcast_to(mean, (ROWS, LANES))
        return carry

    loop(count, 10, average)

    def fold(i, carry):
        rows = pl.ds(pl.multiple_of(i * ROWS, ROWS), ROWS)
        put = pl.ds(pl.multiple_of(to + i * ROWS, ROWS), ROWS)
        mean = sums_ref[rows, :]
        for c in range(HC):
            low = rolled_ref[c, rows, :]
            high = rolled_ref[c + HC, rows, :]
            low = ((low - mean) * turned_ref[:, c * LANES : (c + 1) * LANES]).astype(BF16)
            high = (high - mean) * turned_ref[:, (c + HC) * LANES : (c + HC + 1) * LANES]
            high = high.astype(BF16)
            even_ref[spots[c], put, :] = low + high
            odd_ref[spots[c], put, :] = (low - high) * signs[c].astype(BF16)
        return carry

    loop(count, 4, fold)


def transform(count, t_odd, t_even, scratch):
    even_ref, odd_ref, spec = scratch[3:6]
    odd = jnp.concatenate([odd_ref[c, :count] for c in range(HC)], axis=1)
    spec[:count, : 2 * QB] = jnp.dot(odd, t_odd[...], preferred_element_type=F32)
    even = jnp.concatenate([even_ref[c, :count] for c in range(HC)], axis=1)
    spec[:count, 2 * QB :] = jnp.dot(even, t_even[...], preferred_element_type=F32)


def whiten_rows(first_row, count, live, out_ref, scratch):
    spec_ref = scratch[5]
    lane = lax.broadcasted_iota(jnp.int32, (ROWS, QB), 1)
    not_first = lane > 0
    not_last = lane < QB - 1
    numerator = live * (5.0 * ROOT)

    def up(x):
        return jnp.where(not_first, pltpu.roll(x, 1, 1), 0.0)

    def down(x):
        return jnp.where(not_last, pltpu.roll(x, QB - 1, 1), 0.0)

    def amplitude(re, im):
        power = (re * re + im * im) * (1.0 / WIN) + 1e-06
        return power * lax.rsqrt(power)

    def group(i, carry):
        rows = pl.ds(pl.multiple_of(first_row + i * ROWS, ROWS), ROWS)
        o_re = spec_ref[rows, 0:QB]
        o_im = spec_ref[rows, QB : 2 * QB]
        e_re = spec_ref[rows, 2 * QB : 3 * QB]
        e_im = spec_ref[rows, 3 * QB :]
        odd = amplitude(o_re, o_im)
        even = amplitude(e_re, e_im)
        both = odd + even
        inv_odd = numerator / jnp.maximum(up(both) + both + down(odd), 5.0 * FLOOR)
        inv_even = numerator / jnp.maximum(up(even) + both + down(both), 5.0 * FLOOR)
        to = pl.ds(pl.multiple_of(i * ROWS, ROWS), ROWS)
        out_ref[to, 0:QB] = (o_re * inv_odd).astype(BF16)
        out_ref[to, QB : 2 * QB] = (e_re * inv_even).astype(BF16)
        out_ref[to, 2 * QB : 3 * QB] = (o_im * inv_odd).astype(BF16)
        out_ref[to, 3 * QB :] = (e_im * inv_even).astype(BF16)
        return carry

    loop(count, 8, group)


def slots(c):
    return c * LANES + lax.broadcasted_iota(jnp.int32, (ROWS, LANES), 1)


def part(ref, offset, rows, c):
    return ref[rows, offset + c * LANES : offset + (c + 1) * LANES].astype(F32)


def shifted_rows(ref, first):
    def get(rows, offset, c):
        at = pl.ds(pl.multiple_of(rows.start + first, ROWS), ROWS)
        return part(ref, offset, at, c)

    return get


def column(row):
    n = row.shape[1]
    return jnp.transpose(jnp.broadcast_to(row.astype(F32), (LANES, n)))


def one_hot(col, width, first=0):
    pieces = []
    for at in range(0, width, LANES):
        lane = lax.broadcasted_iota(jnp.int32, col.shape, 1) + (first + at)
        pieces.append(jnp.where(lane.astype(F32) == col, 1.0, 0.0).astype(BF16))
    hot = pieces[0] if len(pieces) == 1 else jnp.concatenate(pieces, axis=1)
    return hot[:, :width]


def write_rows(send_rows, spectra, near, far, n_sta, cap, refs):
    g = lax.axis_index("sta")
    lane = lax.broadcasted_iota(jnp.int32, (1, n_sta * cap), 1)
    col = column(send_rows[...])
    hots = one_hot(col, sum(p.shape[0] for p in spectra[0]))
    for w in range(2):
        result = None
        at = 0
        for piece in spectra[w]:
            n = piece.shape[0]
            term = jnp.dot(hots[:, at : at + n], piece[...], preferred_element_type=F32)
            result = term if result is None else result + term
            at += n
        refs[-1][w] = result.astype(BF16)
    rows = refs[-1]
    for ref, d in zip(refs, near + far):
        first = pl.multiple_of(lax.rem(g + d, n_sta) * cap, cap)
        for w in range(2):
            if d in far:
                ref[w * CAP_FAR : (w + 1) * CAP_FAR, :] = rows[w, pl.ds(first, CAP_FAR), :]
            else:
                ref[w * cap : (w + 1) * cap, :] = rows[w, pl.ds(first, cap), :]


def scratches(n_sta, cap, rows):
    return [
        pltpu.VMEM((1, WIN), F32),
        pltpu.VMEM((CHUNKS, rows, LANES), F32),
        pltpu.VMEM((rows, LANES), F32),
        pltpu.VMEM((HC, rows, LANES), BF16),
        pltpu.VMEM((HC, rows, LANES), BF16),
        pltpu.VMEM((rows, 2 * NF), F32),
        pltpu.VMEM((2, n_sta * cap, 2 * NF), BF16),
    ]


def local_kernel(groups, offsets, main, cos_t, sin_t, taper, send_rows, *rest):
    t_odd, t_even, white0, white3 = rest[:4]
    scratch = rest[-7:]
    sends = rest[4:-7] + (scratch[6],)
    fill_tables(cos_t, sin_t, t_odd, t_even)
    start0 = offsets[0]
    start3 = offsets[2] - 2 * STEP
    live3 = jnp.where(lax.axis_index("tm") == lax.axis_size("tm") - 1, 1.0, 0.0).astype(F32)
    stations = main.shape[0]
    for first in range(0, stations, UNIT):
        count = min(UNIT, stations - first)
        get = shifted_rows(main, first)

        def pick0(rows, c):
            if c >= HC:
                return get(rows, HALF, c - HC)
            return jnp.where(slots(c) >= start0, get(rows, 0, c), get(rows, 2 * HALF, c))

        def pick3(rows, c):
            if c >= HC:
                return jnp.zeros((ROWS, LANES), F32)
            return jnp.where(slots(c) >= start3, get(rows, 2 * HALF, c), 0.0)

        for pick, start, live, white in ((pick0, start0, 1.0, white0), (pick3, start3, live3, white3)):
            prepare(pick, start, count, 0, taper, scratch)
            transform(count, t_odd, t_even, scratch)
            whiten_rows(0, count, live, white.at[first : first + count], scratch)
    write_rows(send_rows, ((white0,), (white3,)), *groups, sends)


def swap_routes(n):
    routes = []
    for first in (0, 1):
        partner = list(range(n))
        for i in range(first, n - 1, 2):
            partner[i], partner[i + 1] = i + 1, i
        routes.append(list(enumerate(partner)))
    return routes


def pack_kernel(sizes, offsets, main, *rest):
    n_out = 2 * len(sizes)
    small = rest[:N_SMALL]
    outs = rest[N_SMALL : N_SMALL + n_out]
    offsets_out = rest[N_SMALL + n_out]
    small_out = rest[N_SMALL + n_out + 1 : -1]
    sems = rest[-1]
    t = lax.axis_index("tm")
    n = lax.axis_size("tm")

    def edge(i):
        chunk, swap = i // 2, i % 2
        at = jnp.where(t % 2 == swap, 2 * HALF, 0)
        lanes = pl.ds(pl.multiple_of(at, LANES), HALF)
        source = main.at[pl.ds(sum(sizes[:chunk]), sizes[chunk]), lanes]
        return pltpu.make_async_copy(source, outs[i].at[pl.ds(0, sizes[chunk])], sems.at[i])

    first = pltpu.make_async_copy(offsets, offsets_out, sems.at[n_out])
    first.start()
    copies = []
    for i in range(n_out):
        if n % 2 == i % 2:
            copies.append(edge(i))
            copies[-1].start()
        else:
            @pl.when(t == n - 1)
            def _():
                outs[i][0 : sizes[i // 2], :] = jnp.zeros((sizes[i // 2], HALF), BF16)

            @pl.when(t < n - 1)
            def _():
                edge(i).start()
    for k in range(N_SMALL):
        copies.append(pltpu.make_async_copy(small[k], small_out[k], sems.at[n_out + 1 + k]))
        copies[-1].start()
    first.wait()
    start = offsets_out[2] - 2 * STEP
    high, low = start // 8, start % 8
    lane = lax.broadcasted_iota(jnp.int32, (ROWS, HALF), 1)
    for i in range(2):
        outs[i][sizes[0] :, :] = jnp.where(lane < NF, high, low).astype(F32).astype(BF16)
    for copy in copies:
        copy.wait()
    for i in range(n_out):
        if n % 2 != i % 2:
            @pl.when(t < n - 1)
            def _():
                edge(i).wait()


def sent_start(ref):
    rows = ref.shape[0] - ROWS
    high = jnp.max(ref[rows:, 0:LANES].astype(F32))
    low = jnp.max(ref[rows:, HALF - LANES :].astype(F32))
    return (high * 8.0 + low).astype(jnp.int32)


def rim_kernel(groups, first, earlier, last, offsets, main, *rest):
    recv = rest[:2]
    heads = rest[2:4] if earlier else recv
    rest = rest[2 + 2 * earlier :]
    taper, t_odd, t_even, send_rows = rest[:4]
    rest = rest[4:]
    older = rest[: 2 * earlier]
    whites = rest[2 * earlier : 2 * earlier + 2]
    scratch = rest[-7:]
    sends = rest[2 * earlier + 2 : -7] + (scratch[6],)
    count = whites[0].shape[0]
    t = lax.axis_index("tm")
    lane = lax.broadcasted_iota(jnp.int32, (ROWS, LANES), 1)
    for swap in range(2):
        ahead = t % 2 == swap
        start = jnp.where(ahead, offsets[1] - STEP, sent_start(heads[swap]))
        sign = jnp.where(ahead, 1, -1)
        least = jnp.where(ahead, 0, 1)
        whole = jnp.where(ahead, 2 * HALF, 0)
        base = (lane - start) * sign

        def pick(rows, c):
            at = pl.ds(pl.multiple_of(rows.start + first, ROWS), ROWS)
            if c >= HC:
                return main[at, pl.ds(pl.multiple_of(whole + (c - HC) * LANES, LANES), LANES)].astype(F32)
            own = part(main, HALF, at, c)
            return jnp.where(base >= least - sign * (c * LANES), own, part(recv[swap], 0, rows, c))

        prepare(pick, start, count, swap * count, taper, scratch)
    transform(2 * count, t_odd, t_even, scratch)
    live = jnp.where(t > 0, 1.0, 0.0).astype(F32)
    whiten_rows(0, count, 1.0, whites[0], scratch)
    whiten_rows(count, count, live, whites[1], scratch)
    if last:
        write_rows(send_rows, (older[0::2] + whites[:1], older[1::2] + whites[1:]), *groups, sends)


def slot_table(groups, pair_slot, width):
    near, far, n_sta, cap = groups
    g = lax.axis_index("sta")
    slot = pair_slot[...]
    distance = (g - slot // cap + n_sta) % n_sta
    place = jnp.zeros_like(slot)
    at = 0
    for d in near + far:
        place = jnp.where(distance == d, at + slot % cap, place)
        at += CAP_FAR if d in far else cap
    return one_hot(column(place), width)


def second_rows(groups, pieces, hot, first_pair, incoming, out):
    near, far, n_sta, cap = groups
    width = incoming.shape[1]
    for w in range(2):
        at = 0
        for i, d in enumerate(near + far):
            n = CAP_FAR if d in far else cap
            incoming[w, at : at + n, :] = pieces[i][w * n : (w + 1) * n, :]
            at += n
        if at < width:
            incoming[w, at:, :] = jnp.zeros((width - at, 2 * NF), BF16)
    for w in range(2):
        for c in range(0, 2 * NF, NF):
            rows = hot[first_pair : first_pair + out.shape[1], :]
            out[w, :, c : c + NF] = jnp.dot(rows, incoming[w, :, c : c + NF], preferred_element_type=F32)


def first_rows(hots, spectra, scale, out):
    lane = lax.broadcasted_iota(jnp.int32, (1, QB), 1)
    s = jnp.where(lane % 2 == 0, scale, -scale).astype(F32)
    for c in range(0, 2 * NF, QB):
        total = None
        for hot, piece in zip(hots, spectra):
            term = jnp.dot(hot, piece[:, c : c + QB], preferred_element_type=F32)
            total = term if total is None else total + term
        out[:, c : c + QB] = total * (s if c % NF == 0 else -s)


def station_tables(col, spectra):
    hots, at = [], 0
    for piece in spectra:
        hots.append(one_hot(col, piece.shape[0], at))
        at += piece.shape[0]
    return hots


def add_products(first, second, first_at, second_at, c, start):
    re_lanes = slice(c, c + LANES)
    im_lanes = slice(NF + c, NF + c + LANES)
    one, two = start
    for w in range(2):
        a_i, b_i = first[w, first_at, re_lanes], first[w, first_at, im_lanes]
        a_j, b_j = second[w, second_at, re_lanes], second[w, second_at, im_lanes]
        re = a_i * a_j + b_i * b_j
        im = b_i * a_j - a_i * b_j
        if c < QB:
            one, two = one + im, two - re
        else:
            one, two = one + re, two + im
    return one, two


def early_kernel(groups, n_pieces, n_white, scale, pair_first, pair_slot, white0, white3, *rest):
    whites = rest[: 2 * n_white]
    rest = rest[2 * n_white :]
    pieces = rest[:n_pieces]
    cross, later, hot = rest[n_pieces : n_pieces + 3]
    incoming, first, second = rest[n_pieces + 3 :]
    pairs = pair_first.shape[1]
    col = column(pair_first[...])
    hots = station_tables(col, (white0,))
    first_rows(hots, (white0,), scale, first.at[0])
    first_rows(hots, (white3,), scale, first.at[1])
    hot[...] = slot_table(groups, pair_slot, hot.shape[1])
    second_rows(groups, pieces, hot, 0, incoming, second)

    def group(i, carry):
        rows = pl.ds(pl.multiple_of(i * ROWS, ROWS), ROWS)
        for c in range(0, NF, LANES):
            one, two = add_products(first, second, rows, rows, c, (0.0, 0.0))
            cross[rows, c : c + LANES] = one
            cross[rows, NF + c : NF + c + LANES] = two
        return carry

    loop(pairs, 2, group)
    hots = station_tables(col, whites[0::2])
    first_rows(hots, whites[0::2], scale, later.at[0])
    first_rows(hots, whites[1::2], scale, later.at[1])


def late_kernel(groups, n_pieces, n_dest, first_pair, early, first, hot, t_odd, t_even, *rest):
    pieces = rest[:n_pieces]
    send, keep = rest[n_pieces : n_pieces + 2]
    incoming, second, x_odd, x_even = rest[n_pieces + 2 :]
    pairs = send.shape[1]
    second_rows(groups, pieces, hot, first_pair, incoming, second)

    def group(i, carry):
        rows = pl.ds(pl.multiple_of(i * ROWS, ROWS), ROWS)
        full = pl.ds(pl.multiple_of(first_pair + i * ROWS, ROWS), ROWS)
        for c in range(0, NF, LANES):
            start = (early[full, c : c + LANES], early[full, NF + c : NF + c + LANES])
            one, two = add_products(first, second, full, rows, c, start)
            out = x_odd if c < QB else x_even
            at = c % QB
            out[rows, at : at + LANES] = one.astype(BF16)
            out[rows, QB + at : QB + at + LANES] = two.astype(BF16)
        return carry

    loop(pairs, 2, group)
    lag_rows = NL // n_dest
    me = lax.axis_index("tm")
    dims = (((1,), (1,)), ((), ()))
    for out, order in ((send, range(1, n_dest, 2)), (keep, range(0, n_dest, 2))):
        spots = [
            pl.ds(pl.multiple_of(jnp.bitwise_xor(me, r) * lag_rows, lag_rows), lag_rows) for r in order
        ]
        odd = jnp.concatenate([t_odd[at, :] for at in spots], axis=0)
        even = jnp.concatenate([t_even[at, :] for at in spots], axis=0)
        value = lax.dot_general(odd, x_odd[...], dims, preferred_element_type=F32)
        value = value + lax.dot_general(even, x_even[...], dims, preferred_element_type=F32)
        out[...] = value.astype(out.dtype)


def merge_kernel(lag_rows, keep, received, send, kept):
    for k in range(keep.shape[0] // lag_rows):
        rows = slice(k * lag_rows, (k + 1) * lag_rows)
        out, j = (send, k // 2) if k % 2 else (kept, k // 2)
        value = keep[rows, :] + received[rows, :].astype(F32)
        out[j * lag_rows : (j + 1) * lag_rows, :] = value.astype(out.dtype)


def finish_kernel(*refs):
    out = refs[-1]
    at = 0
    for keep, received in zip(refs[0:-1:2], refs[1:-1:2]):
        width = keep.shape[1]
        out[:, at : at + width] = keep[...] + received[...].astype(F32)
        at += width


def in_vmem(*arrays):
    return [pltpu.with_memory_space_constraint(a, pltpu.VMEM) for a in arrays]


def in_smem(*arrays):
    return [pltpu.with_memory_space_constraint(a, pltpu.SMEM) for a in arrays]


def in_hbm(*arrays):
    return [pltpu.with_memory_space_constraint(a, pltpu.HBM) for a in arrays]


def params(mib):
    return pltpu.CompilerParams(vmem_limit_bytes=mib << 20)


def cost(flops, moved):
    return pl.CostEstimate(flops=int(flops), bytes_accessed=int(moved), transcendentals=0)


def on_device(traces, offsets, pair_first, pair_slot, send_rows):
    stations, block_len = traces.shape
    n_tm = lax.axis_size("tm")
    n_sta = lax.axis_size("sta")
    windows = offsets.shape[0]
    pairs = pair_first.shape[0]
    cap = send_rows.shape[1] // n_sta

    sizes = (stations // 2, stations // 2)
    n_chunks = len(sizes)
    main, = in_vmem(traces)
    routes = swap_routes(n_tm)
    small = [jnp.asarray(x) for x in small_tables()] + [jnp.asarray(taper_row()), send_rows]
    packed = pl.pallas_call(
        functools.partial(pack_kernel, sizes),
        out_shape=[
            pltpu.VMEM((sizes[i // 2] + (ROWS if i < 2 else 0), HALF), BF16)
            for i in range(2 * n_chunks)
        ]
        + [pltpu.SMEM(offsets.shape, jnp.int32)]
        + [pltpu.VMEM(x.shape, x.dtype) for x in small],
        in_specs=[ANY] * (2 + N_SMALL),
        out_specs=[VMEM] * (2 * n_chunks) + [SMEM] + [VMEM] * N_SMALL,
        scratch_shapes=[pltpu.SemaphoreType.DMA((2 * n_chunks + 1 + N_SMALL,))],
        compiler_params=params(1),
        cost_estimate=cost(0, 4 << 20),
        name="pack_edges",
    )(*in_hbm(offsets, traces, *small))
    starts = packed[2 * n_chunks]
    cos_t, sin_t, taper, send_rows = packed[2 * n_chunks + 1 :]
    packed = packed[: 2 * n_chunks]
    edges = [lax.ppermute(x, "tm", routes[i % 2]) for i, x in enumerate(packed)]

    near = [0, 1, n_sta - 1] if n_sta > 2 else list(range(n_sta))
    far = [d for d in range(n_sta) if d not in near]
    groups = (near, far, n_sta, cap)
    width = -(-(len(near) * cap + len(far) * CAP_FAR) // LANES) * LANES
    first_row, slot_row = pair_first[None, :], pair_slot[None, :]

    buffers = [pltpu.VMEM((2 * (CAP_FAR if d in far else cap), 2 * NF), BF16) for d in near + far]
    dft_flops = 2 * 2 * HALF * 2 * QB * 2
    spectrum = pltpu.VMEM((stations, 2 * NF), BF16)
    table = pltpu.VMEM((HALF, 2 * QB), BF16)
    local = pl.pallas_call(
        functools.partial(local_kernel, groups),
        out_shape=[table] * 2 + [spectrum] * 2 + buffers,
        in_specs=[SMEM] + [VMEM] * 5,
        out_specs=[VMEM] * (4 + len(buffers)),
        scratch_shapes=scratches(n_sta, cap, UNIT),
        compiler_params=params(18),
        cost_estimate=cost(dft_flops * stations, 8 << 20),
        name="local_windows",
    )(*in_smem(starts), *in_vmem(main, cos_t, sin_t, taper, send_rows))
    t_odd, t_even, white0, white3 = local[:4]

    def exchange(pieces):
        got = []
        for d, piece in zip(near + far, pieces):
            if d == 0:
                got.append(piece)
            else:
                route = [(i, (i + d) % n_sta) for i in range(n_sta)]
                got.append(lax.ppermute(piece, "sta", route))
        return got

    early_in = exchange(local[4:])
    scale = 1.0 / math.sqrt(NF * windows * n_tm)
    pair_scratch = [
        pltpu.VMEM((2, width, 2 * NF), BF16),
        pltpu.VMEM((2, pairs, 2 * NF), F32),
        pltpu.VMEM((2, pairs, 2 * NF), F32),
    ]
    whites = []
    late_out = None
    for i in range(n_chunks):
        last = i == n_chunks - 1
        rows = sizes[i]
        chunk = pltpu.VMEM((rows, 2 * NF), BF16)
        result = pl.pallas_call(
            functools.partial(rim_kernel, groups, sum(sizes[:i]), i, last),
            out_shape=[chunk] * 2 + (buffers if last else []),
            in_specs=[SMEM] + [VMEM] * (7 + 4 * i),
            out_specs=[VMEM] * (2 + (len(buffers) if last else 0)),
            scratch_shapes=scratches(n_sta, cap, 2 * rows),
            compiler_params=params(22),
            cost_estimate=cost(dft_flops * rows, 4 << 20),
            name="rim_windows_%d" % i,
        )(
            *in_smem(starts),
            *in_vmem(main, *edges[2 * i : 2 * i + 2], *(edges[:2] * i)),
            *in_vmem(taper, t_odd, t_even, send_rows, *whites),
        )
        whites = whites + list(result[:2])
        late_out = result[2:]
    late_in = exchange(late_out)
    early, first, hot = pl.pallas_call(
        functools.partial(early_kernel, groups, len(buffers), n_chunks, scale),
        out_shape=[
            pltpu.VMEM((pairs, 2 * NF), F32),
            pltpu.VMEM((2, pairs, 2 * NF), F32),
            pltpu.VMEM((pairs, width), BF16),
        ],
        in_specs=[VMEM] * (4 + 2 * n_chunks + len(buffers)),
        out_specs=[VMEM] * 3,
        scratch_shapes=pair_scratch,
        compiler_params=params(16),
        cost_estimate=cost(2 * 2 * pairs * (2 * stations + width) * 2 * NF, 4 << 20),
        name="early_pairs",
    )(first_row, slot_row, *in_vmem(white0, white3, *whites, *early_in))

    lag_rows = NL // n_tm
    n_half = 2
    half = pairs // n_half
    steps = [1 << k for k in range(n_tm.bit_length() - 1)]
    done = []
    parts = []
    for h in range(n_half):
        parts.append(
            pl.pallas_call(
                functools.partial(late_kernel, groups, len(buffers), n_tm, h * half),
                out_shape=[pltpu.VMEM((NL // 2, half), BF16), pltpu.VMEM((NL // 2, half), F32)],
                in_specs=[VMEM] * (5 + len(buffers)),
                out_specs=[VMEM] * 2,
                scratch_shapes=[
                    pltpu.VMEM((2, width, 2 * NF), BF16),
                    pltpu.VMEM((2, half, 2 * NF), F32),
                    pltpu.VMEM((half, NF), BF16),
                    pltpu.VMEM((half, NF), BF16),
                ],
                compiler_params=params(10),
                cost_estimate=cost(2 * 2 * half * width * 2 * NF + 2 * NL * half * 2 * NF, 3 << 20),
                name="late_pairs_%d" % h,
            )(*in_vmem(early, first, hot, t_odd, t_even, *late_in))
        )
    for step in steps:
        route = [(i, i ^ step) for i in range(n_tm)]
        received = [lax.ppermute(send, "tm", route) for send, _ in parts]
        if step == steps[-1]:
            done = [x for (_, keep), got in zip(parts, received) for x in (keep, got)]
            break
        merged = []
        for h in range(n_half):
            keep = parts[h][1]
            rows = keep.shape[0] // 2
            merged.append(
                pl.pallas_call(
                    functools.partial(merge_kernel, lag_rows),
                    out_shape=[pltpu.VMEM((rows, half), BF16), pltpu.VMEM((rows, half), F32)],
                    in_specs=[VMEM] * 2,
                    out_specs=[VMEM] * 2,
                    compiler_params=params(1),
                    cost_estimate=cost(rows * half, 1 << 20),
                    name="merge_%d_%d" % (step, h),
                )(*in_vmem(keep, received[h]))
            )
        parts = merged
    return pl.pallas_call(
        finish_kernel,
        out_shape=jax.ShapeDtypeStruct((lag_rows, pairs), F32),
        in_specs=[VMEM] * len(done),
        out_specs=VMEM,
        compiler_params=params(2),
        cost_estimate=cost(lag_rows * pairs, 1 << 20),
        name="finish",
    )(*in_vmem(*done))


def solution(mesh):
    in_specs = (P("sta", ("day", "tm")), P(("day", "tm")), P("sta"), P("sta"), P("sta", None))
    out_specs = P(("day", "tm"), "sta")
    return jax.shard_map(
        on_device, mesh=mesh, in_specs=in_specs, out_specs=out_specs, check_vma=False
    )
```

```python
import functools
import math

import jax
import jax.numpy as jnp
import numpy as np
from jax import lax
from jax.experimental import pallas as pl
from jax.experimental.pallas import tpu as pltpu
from jax.sharding import PartitionSpec as P


WIN = 2048
NF = 512
NL = 1024
FLOOR = 0.1
STEP = 1024
HALF = 1024
CAP_FAR = 8
LANES = 128
CHUNKS = WIN // LANES
HC = CHUNKS // 2
QB = NF // 2
ROOT = 1.0 / math.sqrt(WIN)
F32 = jnp.float32
BF16 = jnp.bfloat16
ROWS = 16
UNIT = 512
VMEM = pl.BlockSpec(memory_space=pltpu.VMEM)
SMEM = pl.BlockSpec(memory_space=pltpu.SMEM)
ANY = pl.BlockSpec(memory_space=pltpu.HBM)


def loop(count, most, body):
    trips = count // ROWS
    unroll = max(u for u in range(1, most + 1) if trips % u == 0)
    lax.fori_loop(0, trips, body, 0, unroll=unroll)


def small_tables():
    step = np.arange(32)[:, None]
    half = np.arange(QB)
    freq = np.concatenate([2 * half + 1, 2 * half + 2])[None, :]
    angles = np.concatenate([32 * step, step], axis=0) * freq % WIN * (2.0 * np.pi / WIN)
    return np.cos(angles).astype(np.float32), np.sin(angles).astype(np.float32)


def taper_row():
    index = np.arange(WIN)
    return (0.5 - 0.5 * np.cos(2.0 * np.pi * index / WIN)).astype(np.float32)[None, :]


def fill_tables(cos_ref, sin_ref, odd_ref, even_ref):
    def block(a, carry):
        ca = cos_ref[pl.ds(a, 1), :]
        sa = sin_ref[pl.ds(a, 1), :]
        cb = cos_ref[32:64, :]
        sb = sin_ref[32:64, :]
        c = (ca * cb - sa * sb).astype(BF16)
        s = (-(sa * cb + ca * sb)).astype(BF16)
        rows = pl.ds(pl.multiple_of(a * 32, 32), 32)
        odd_ref[rows, :QB] = c[:, :QB]
        odd_ref[rows, QB:] = s[:, :QB]
        even_ref[rows, :QB] = c[:, QB:]
        even_ref[rows, QB:] = s[:, QB:]
        return carry

    lax.fori_loop(0, HALF // 32, block, 0)


def prepare(pick, start, count, to, taper_ref, scratch):
    turned_ref, rolled_ref, sums_ref, even_ref, odd_ref = scratch[:5]
    q = start // LANES
    s = start % LANES
    shift = (LANES - s) % LANES
    spots, signs = [], []
    for c in range(CHUNKS):
        j = (c - q + CHUNKS) % CHUNKS
        turned_ref[:, c * LANES : (c + 1) * LANES] = taper_ref[
            :, pl.ds(pl.multiple_of(j * LANES, LANES), LANES)
        ]
        if c < HC:
            spots.append(j % HC)
            signs.append(jnp.where(j < HC, 1.0, -1.0).astype(F32))
    keep = lax.broadcasted_iota(jnp.int32, (ROWS, LANES), 1) < LANES - s

    def turn(i, carry):
        rows = pl.ds(pl.multiple_of(i * ROWS, ROWS), ROWS)
        rolled = [pltpu.roll(pick(rows, c).astype(F32), shift, 1) for c in range(CHUNKS)]
        turned = [jnp.where(keep, rolled[c], rolled[(c + 1) % CHUNKS]) for c in range(CHUNKS)]
        for c in range(CHUNKS):
            rolled_ref[c, rows, :] = turned[c]
        while len(turned) > 1:
            turned = [turned[2 * k] + turned[2 * k + 1] for k in range(len(turned) // 2)]
        sums_ref[rows, :] = turned[0]
        return carry

    loop(count, 4, turn)

    def average(i, carry):
        rows = pl.ds(pl.multiple_of(i * ROWS, ROWS), ROWS)
        mean = jnp.sum(sums_ref[rows, :], axis=1, keepdims=True) * (1.0 / WIN)
        sums_ref[rows, :] = jnp.broadcast_to(mean, (ROWS, LANES))
        return carry

    loop(count, 10, average)

    def fold(i, carry):
        rows = pl.ds(pl.multiple_of(i * ROWS, ROWS), ROWS)
        put = pl.ds(pl.multiple_of(to + i * ROWS, ROWS), ROWS)
        mean = sums_ref[rows, :]
        for c in range(HC):
            low = rolled_ref[c, rows, :]
            high = rolled_ref[c + HC, rows, :]
            low = ((low - mean) * turned_ref[:, c * LANES : (c + 1) * LANES]).astype(BF16)
            high = (high - mean) * turned_ref[:, (c + HC) * LANES : (c + HC + 1) * LANES]
            high = high.astype(BF16)
            even_ref[spots[c], put, :] = low + high
            odd_ref[spots[c], put, :] = (low - high) * signs[c].astype(BF16)
        return carry

    loop(count, 4, fold)


def transform(count, t_odd, t_even, scratch):
    even_ref, odd_ref, spec = scratch[3:6]
    odd = jnp.concatenate([odd_ref[c, :count] for c in range(HC)], axis=1)
    spec[:count, : 2 * QB] = jnp.dot(odd, t_odd[...], preferred_element_type=F32)
    even = jnp.concatenate([even_ref[c, :count] for c in range(HC)], axis=1)
    spec[:count, 2 * QB :] = jnp.dot(even, t_even[...], preferred_element_type=F32)


def whiten_rows(first_row, count, live, out_ref, scratch):
    spec_ref = scratch[5]
    lane = lax.broadcasted_iota(jnp.int32, (ROWS, QB), 1)
    not_first = lane > 0
    not_last = lane < QB - 1
    numerator = live * (5.0 * ROOT)

    def up(x):
        return jnp.where(not_first, pltpu.roll(x, 1, 1), 0.0)

    def down(x):
        return jnp.where(not_last, pltpu.roll(x, QB - 1, 1), 0.0)

    def amplitude(re, im):
        power = (re * re + im * im) * (1.0 / WIN) + 1e-06
        return power * lax.rsqrt(power)

    def group(i, carry):
        rows = pl.ds(pl.multiple_of(first_row + i * ROWS, ROWS), ROWS)
        o_re = spec_ref[rows, 0:QB]
        o_im = spec_ref[rows, QB : 2 * QB]
        e_re = spec_ref[rows, 2 * QB : 3 * QB]
        e_im = spec_ref[rows, 3 * QB :]
        odd = amplitude(o_re, o_im)
        even = amplitude(e_re, e_im)
        both = odd + even
        inv_odd = numerator / jnp.maximum(up(both) + both + down(odd), 5.0 * FLOOR)
        inv_even = numerator / jnp.maximum(up(even) + both + down(both), 5.0 * FLOOR)
        to = pl.ds(pl.multiple_of(i * ROWS, ROWS), ROWS)
        out_ref[to, 0:QB] = (o_re * inv_odd).astype(BF16)
        out_ref[to, QB : 2 * QB] = (e_re * inv_even).astype(BF16)
        out_ref[to, 2 * QB : 3 * QB] = (o_im * inv_odd).astype(BF16)
        out_ref[to, 3 * QB :] = (e_im * inv_even).astype(BF16)
        return carry

    loop(count, 8, group)


def slots(c):
    return c * LANES + lax.broadcasted_iota(jnp.int32, (ROWS, LANES), 1)


def part(ref, offset, rows, c):
    return ref[rows, offset + c * LANES : offset + (c + 1) * LANES].astype(F32)


def shifted_rows(ref, first):
    def get(rows, offset, c):
        at = pl.ds(pl.multiple_of(rows.start + first, ROWS), ROWS)
        return part(ref, offset, at, c)

    return get


def column(row):
    n = row.shape[1]
    return jnp.transpose(jnp.broadcast_to(row.astype(F32), (LANES, n)))


def one_hot(col, width, first=0):
    pieces = []
    for at in range(0, width, LANES):
        lane = lax.broadcasted_iota(jnp.int32, col.shape, 1) + (first + at)
        pieces.append(jnp.where(lane.astype(F32) == col, 1.0, 0.0).astype(BF16))
    hot = pieces[0] if len(pieces) == 1 else jnp.concatenate(pieces, axis=1)
    return hot[:, :width]


def outgoing(send_rows, first, spectra, before, out):
    col = column(send_rows[...])
    hot = one_hot(col, spectra[0].shape[0], first)
    for w in range(2):
        value = jnp.dot(hot, spectra[w][...], preferred_element_type=F32)
        out[w] = value if before is None else before[w] + value


def write_rows(groups, rows, refs):
    near, far, n_sta, cap = groups
    g = lax.axis_index("sta")
    for ref, d in zip(refs, near + far):
        first = pl.multiple_of(peer(d, g, n_sta) * cap, cap)
        n = CAP_FAR if d in far else cap
        for w in range(2):
            ref[w * n : (w + 1) * n, :] = rows[w, pl.ds(first, n), :].astype(BF16)


def scratches(n_sta, cap, rows):
    return [
        pltpu.VMEM((1, WIN), F32),
        pltpu.VMEM((CHUNKS, rows, LANES), F32),
        pltpu.VMEM((rows, LANES), F32),
        pltpu.VMEM((HC, rows, LANES), BF16),
        pltpu.VMEM((HC, rows, LANES), BF16),
        pltpu.VMEM((rows, 2 * NF), F32),
        pltpu.VMEM((2, n_sta * cap, 2 * NF), F32),
    ]


def local_kernel(groups, offsets, main, cos_t, sin_t, taper, send_rows, *rest):
    t_odd, t_even, white0, white3 = rest[:4]
    scratch = rest[-7:]
    sends = rest[4:-7]
    fill_tables(cos_t, sin_t, t_odd, t_even)
    start0 = offsets[0]
    start3 = offsets[2] - 2 * STEP
    live3 = jnp.where(lax.axis_index("tm") == lax.axis_size("tm") - 1, 1.0, 0.0).astype(F32)
    stations = main.shape[0]
    for first in range(0, stations, UNIT):
        count = min(UNIT, stations - first)
        get = shifted_rows(main, first)

        def pick0(rows, c):
            if c >= HC:
                return get(rows, HALF, c - HC)
            return jnp.where(slots(c) >= start0, get(rows, 0, c), get(rows, 2 * HALF, c))

        def pick3(rows, c):
            if c >= HC:
                return jnp.zeros((ROWS, LANES), F32)
            return jnp.where(slots(c) >= start3, get(rows, 2 * HALF, c), 0.0)

        for pick, start, live, white in ((pick0, start0, 1.0, white0), (pick3, start3, live3, white3)):
            prepare(pick, start, count, 0, taper, scratch)
            transform(count, t_odd, t_even, scratch)
            whiten_rows(0, count, live, white.at[first : first + count], scratch)
    outgoing(send_rows, 0, (white0, white3), None, scratch[6])
    write_rows(groups, scratch[6], sends)


def peer(d, g, n):
    if d == "own":
        return g
    if d == "even":
        return g + 1 - 2 * (g % 2)
    if d == "odd":
        return (g - 1 + 2 * (g % 2) + n) % n
    return (g + d) % n


def swap_routes(n):
    routes = []
    for first in (0, 1):
        partner = list(range(n))
        for i in range(first, n - 1, 2):
            partner[i], partner[i + 1] = i + 1, i
        routes.append(list(enumerate(partner)))
    return routes


def pack_kernel(first, count, n_small, head, offsets, main, *rest):
    small = rest[:n_small]
    outs = rest[n_small : n_small + 2]
    small_out = rest[n_small + 2 : 2 * n_small + 2]
    offsets_out = rest[2 * n_small + 2]
    sems = rest[-1]
    t = lax.axis_index("tm")
    n = lax.axis_size("tm")

    def edge(swap):
        at = jnp.where(t % 2 == swap, 2 * HALF, 0)
        lanes = pl.ds(pl.multiple_of(at, LANES), HALF)
        source = main.at[pl.ds(first, count), lanes]
        return pltpu.make_async_copy(source, outs[swap].at[pl.ds(0, count)], sems.at[swap])

    copies = []
    for swap in range(2):
        if n % 2 == swap:
            copies.append(edge(swap))
            copies[-1].start()
        else:
            @pl.when(t == n - 1)
            def _():
                outs[swap][0:count, :] = jnp.zeros((count, HALF), BF16)

            @pl.when(t < n - 1)
            def _():
                edge(swap).start()
    for k in range(n_small):
        copies.append(pltpu.make_async_copy(small[k], small_out[k], sems.at[3 + k]))
        copies[-1].start()
    if head:
        numbers = pltpu.make_async_copy(offsets, offsets_out, sems.at[2])
        numbers.start()
        numbers.wait()
        start = offsets_out[2] - 2 * STEP
        high, low = start // 8, start % 8
        lane = lax.broadcasted_iota(jnp.int32, (ROWS, HALF), 1)
        for out in outs:
            out[count:, :] = jnp.where(lane < NF, high, low).astype(F32).astype(BF16)
    for copy in copies:
        copy.wait()
    for swap in range(2):
        if n % 2 != swap:
            @pl.when(t < n - 1)
            def _():
                edge(swap).wait()


def sent_start(ref):
    rows = ref.shape[0] - ROWS
    high = jnp.max(ref[rows:, 0:LANES].astype(F32))
    low = jnp.max(ref[rows:, HALF - LANES :].astype(F32))
    return (high * 8.0 + low).astype(jnp.int32)


def rim_kernel(groups, first, earlier, last, offsets, main, *rest):
    recv = rest[:2]
    heads = rest[2:4] if earlier else recv
    rest = rest[4 if earlier else 2 :]
    taper, t_odd, t_even, send_rows = rest[:4]
    rest = rest[4:]
    before = rest[0] if earlier else None
    rest = rest[1:] if earlier else rest
    whites = rest[:2]
    scratch = rest[-7:]
    sends = rest[2:-7]
    count = whites[0].shape[0]
    t = lax.axis_index("tm")
    lane = lax.broadcasted_iota(jnp.int32, (ROWS, LANES), 1)
    for swap in range(2):
        ahead = t % 2 == swap
        start = jnp.where(ahead, offsets[1] - STEP, sent_start(heads[swap]))
        sign = jnp.where(ahead, 1, -1)
        least = jnp.where(ahead, 0, 1)
        whole = jnp.where(ahead, 2 * HALF, 0)
        base = (lane - start) * sign

        def pick(rows, c):
            at = pl.ds(pl.multiple_of(rows.start + first, ROWS), ROWS)
            if c >= HC:
                return main[at, pl.ds(pl.multiple_of(whole + (c - HC) * LANES, LANES), LANES)].astype(F32)
            own = part(main, HALF, at, c)
            return jnp.where(base >= least - sign * (c * LANES), own, part(recv[swap], 0, rows, c))

        prepare(pick, start, count, swap * count, taper, scratch)
    transform(2 * count, t_odd, t_even, scratch)
    live = jnp.where(t > 0, 1.0, 0.0).astype(F32)
    whiten_rows(0, count, 1.0, whites[0], scratch)
    whiten_rows(count, count, live, whites[1], scratch)
    if last:
        outgoing(send_rows, first, whites, before, scratch[6])
        write_rows(groups, scratch[6], sends)
    else:
        outgoing(send_rows, first, whites, before, sends[0])


def slot_table(groups, pair_slot, width):
    near, far, n_sta, cap = groups
    g = lax.axis_index("sta")
    slot = pair_slot[...]
    place = jnp.zeros_like(slot)
    at = 0
    for d in near + far:
        source = (g - d + n_sta) % n_sta if d in far else peer(d, g, n_sta)
        place = jnp.where(slot // cap == source, at + slot % cap, place)
        at += CAP_FAR if d in far else cap
    return one_hot(column(place), width)


def second_rows(groups, pieces, hot, first_pair, incoming, out):
    near, far, _, cap = groups
    width = incoming.shape[1]
    for w in range(2):
        at = 0
        for i, d in enumerate(near + far):
            n = CAP_FAR if d in far else cap
            incoming[w, at : at + n, :] = pieces[i][w * n : (w + 1) * n, :]
            at += n
        if at < width:
            incoming[w, at:, :] = jnp.zeros((width - at, 2 * NF), BF16)
    for w in range(2):
        for c in range(0, 2 * NF, NF):
            rows = hot[first_pair : first_pair + out.shape[1], :]
            out[w, :, c : c + NF] = jnp.dot(rows, incoming[w, :, c : c + NF], preferred_element_type=F32)


def first_rows(hots, spectra, scale, out):
    lane = lax.broadcasted_iota(jnp.int32, (1, QB), 1)
    s = jnp.where(lane % 2 == 0, scale, -scale).astype(F32)
    for c in range(0, 2 * NF, QB):
        total = None
        for hot, piece in zip(hots, spectra):
            term = jnp.dot(hot, piece[:, c : c + QB], preferred_element_type=F32)
            total = term if total is None else total + term
        out[:, c : c + QB] = total * (s if c % NF == 0 else -s)


def station_tables(col, spectra):
    hots, at = [], 0
    for piece in spectra:
        hots.append(one_hot(col, piece.shape[0], at))
        at += piece.shape[0]
    return hots


def add_products(first, second, first_at, second_at, c, start):
    re_lanes = slice(c, c + LANES)
    im_lanes = slice(NF + c, NF + c + LANES)
    one, two = start
    for w in range(2):
        a_i, b_i = first[w, first_at, re_lanes], first[w, first_at, im_lanes]
        a_j, b_j = second[w, second_at, re_lanes], second[w, second_at, im_lanes]
        re = a_i * a_j + b_i * b_j
        im = b_i * a_j - a_i * b_j
        if c < QB:
            one, two = one + im, two - re
        else:
            one, two = one + re, two + im
    return one, two


def early_kernel(groups, n_pieces, n_white, scale, pair_first, pair_slot, white0, white3, *rest):
    whites = rest[: 2 * n_white]
    rest = rest[2 * n_white :]
    pieces = rest[:n_pieces]
    cross, later, hot = rest[n_pieces : n_pieces + 3]
    incoming, first, second = rest[n_pieces + 3 :]
    pairs = pair_first.shape[1]
    col = column(pair_first[...])
    hots = station_tables(col, (white0,))
    first_rows(hots, (white0,), scale, first.at[0])
    first_rows(hots, (white3,), scale, first.at[1])
    hot[...] = slot_table(groups, pair_slot, hot.shape[1])
    second_rows(groups, pieces, hot, 0, incoming, second)

    def group(i, carry):
        rows = pl.ds(pl.multiple_of(i * ROWS, ROWS), ROWS)
        for c in range(0, NF, LANES):
            one, two = add_products(first, second, rows, rows, c, (0.0, 0.0))
            cross[rows, c : c + LANES] = one
            cross[rows, NF + c : NF + c + LANES] = two
        return carry

    loop(pairs, 2, group)
    hots = station_tables(col, whites[0::2])
    first_rows(hots, whites[0::2], scale, later.at[0])
    first_rows(hots, whites[1::2], scale, later.at[1])


def late_kernel(groups, n_pieces, n_dest, first_pair, early, first, hot, t_odd, t_even, *rest):
    pieces = rest[:n_pieces]
    send, keep = rest[n_pieces : n_pieces + 2]
    incoming, second, x_odd, x_even = rest[n_pieces + 2 :]
    pairs = send.shape[1]
    second_rows(groups, pieces, hot, first_pair, incoming, second)

    def group(i, carry):
        rows = pl.ds(pl.multiple_of(i * ROWS, ROWS), ROWS)
        full = pl.ds(pl.multiple_of(first_pair + i * ROWS, ROWS), ROWS)
        for c in range(0, NF, LANES):
            start = (early[full, c : c + LANES], early[full, NF + c : NF + c + LANES])
            one, two = add_products(first, second, full, rows, c, start)
            out = x_odd if c < QB else x_even
            at = c % QB
            out[rows, at : at + LANES] = one.astype(BF16)
            out[rows, QB + at : QB + at + LANES] = two.astype(BF16)
        return carry

    loop(pairs, 2, group)
    lag_rows = NL // n_dest
    me = lax.axis_index("tm")
    dims = (((1,), (1,)), ((), ()))
    for out, order in ((send, range(1, n_dest, 2)), (keep, range(0, n_dest, 2))):
        spots = [
            pl.ds(pl.multiple_of(jnp.bitwise_xor(me, r) * lag_rows, lag_rows), lag_rows) for r in order
        ]
        odd = jnp.concatenate([t_odd[at, :] for at in spots], axis=0)
        even = jnp.concatenate([t_even[at, :] for at in spots], axis=0)
        value = lax.dot_general(odd, x_odd[...], dims, preferred_element_type=F32)
        value = value + lax.dot_general(even, x_even[...], dims, preferred_element_type=F32)
        out[...] = value.astype(out.dtype)


def merge_kernel(lag_rows, keep, received, send, kept):
    for k in range(keep.shape[0] // lag_rows):
        rows = slice(k * lag_rows, (k + 1) * lag_rows)
        out, j = (send, k // 2) if k % 2 else (kept, k // 2)
        value = keep[rows, :] + received[rows, :].astype(F32)
        out[j * lag_rows : (j + 1) * lag_rows, :] = value.astype(out.dtype)


def finish_kernel(*refs):
    out = refs[-1]
    at = 0
    for keep, received in zip(refs[0:-1:2], refs[1:-1:2]):
        width = keep.shape[1]
        out[:, at : at + width] = keep[...] + received[...].astype(F32)
        at += width


def in_vmem(*arrays):
    return [pltpu.with_memory_space_constraint(a, pltpu.VMEM) for a in arrays]


def in_smem(*arrays):
    return [pltpu.with_memory_space_constraint(a, pltpu.SMEM) for a in arrays]


def in_hbm(*arrays):
    return [pltpu.with_memory_space_constraint(a, pltpu.HBM) for a in arrays]


def params(mib):
    return pltpu.CompilerParams(vmem_limit_bytes=mib << 20)


def cost(flops, moved):
    return pl.CostEstimate(flops=int(flops), bytes_accessed=int(moved), transcendentals=0)


def on_device(traces, offsets, pair_first, pair_slot, send_rows):
    stations, _ = traces.shape
    n_tm = lax.axis_size("tm")
    n_sta = lax.axis_size("sta")
    windows = offsets.shape[0]
    pairs = pair_first.shape[0]
    cap = send_rows.shape[1] // n_sta

    sizes = (stations * 5 // 8, stations * 3 // 8)
    n_chunks = len(sizes)
    main, = in_vmem(traces)
    routes = swap_routes(n_tm)
    small = [jnp.asarray(x) for x in small_tables()] + [jnp.asarray(taper_row()), send_rows]
    edges = []
    for i, rows in enumerate(sizes):
        head = i == 0
        extra = [] if head else small
        packed = pl.pallas_call(
            functools.partial(pack_kernel, sum(sizes[:i]), rows, len(extra), head),
            out_shape=[pltpu.VMEM((rows + (ROWS if head else 0), HALF), BF16)] * 2
            + [pltpu.VMEM(x.shape, x.dtype) for x in extra]
            + [pltpu.SMEM(offsets.shape, jnp.int32)],
            in_specs=[ANY] * (2 + len(extra)),
            out_specs=[VMEM] * (2 + len(extra)) + [SMEM],
            scratch_shapes=[pltpu.SemaphoreType.DMA((3 + len(extra),))],
            compiler_params=params(1),
            cost_estimate=cost(0, 2 << 20),
        )(*in_hbm(offsets, traces, *extra))
        if head:
            starts = packed[-1]
        else:
            cos_t, sin_t, taper, send_rows = packed[2:-1]
        got = [None, None]
        for swap in (1, 0):
            got[swap] = lax.ppermute(packed[swap], "tm", routes[swap])
        edges += got

    near = ["own", "even", "odd"]
    far = list(range(2, n_sta - 1))
    groups = (near, far, n_sta, cap)
    width = -(-(len(near) * cap + len(far) * CAP_FAR) // LANES) * LANES
    first_row, slot_row = pair_first[None, :], pair_slot[None, :]

    buffers = [pltpu.VMEM((2 * (CAP_FAR if d in far else cap), 2 * NF), BF16) for d in near + far]
    dft_flops = 2 * 2 * HALF * 2 * QB * 2
    spectrum = pltpu.VMEM((stations, 2 * NF), BF16)
    table = pltpu.VMEM((HALF, 2 * QB), BF16)
    local = pl.pallas_call(
        functools.partial(local_kernel, groups),
        out_shape=[table] * 2 + [spectrum] * 2 + buffers,
        in_specs=[SMEM] + [VMEM] * 5,
        out_specs=[VMEM] * (4 + len(buffers)),
        scratch_shapes=scratches(n_sta, cap, UNIT),
        compiler_params=params(18),
        cost_estimate=cost(dft_flops * stations, 8 << 20),
        name="local_windows",
    )(*in_smem(starts), *in_vmem(main, cos_t, sin_t, taper, send_rows))
    t_odd, t_even, white0, white3 = local[:4]

    def exchange(pieces):
        got = list(pieces)
        for i, d in sorted(enumerate(near + far), key=lambda x: (2, 1, 0)[near.index(x[1])] if x[1] in near else 3):
            if d != "own":
                route = [(k, peer(d, k, n_sta)) for k in range(n_sta)]
                got[i] = lax.ppermute(pieces[i], "sta", route)
        return got

    early_in = exchange(local[4:])
    scale = 1.0 / math.sqrt(NF * windows * n_tm)
    pair_scratch = [
        pltpu.VMEM((2, width, 2 * NF), BF16),
        pltpu.VMEM((2, pairs, 2 * NF), F32),
        pltpu.VMEM((2, pairs, 2 * NF), F32),
    ]
    whites = []
    late_out = []
    outgoing_rows = pltpu.VMEM((2, n_sta * cap, 2 * NF), F32)
    for i in range(n_chunks):
        last = i == n_chunks - 1
        rows = sizes[i]
        chunk = pltpu.VMEM((rows, 2 * NF), BF16)
        result = pl.pallas_call(
            functools.partial(rim_kernel, groups, sum(sizes[:i]), i, last),
            out_shape=[chunk] * 2 + (buffers if last else [outgoing_rows]),
            in_specs=[SMEM] + [VMEM] * (7 + 3 * min(i, 1)),
            out_specs=[VMEM] * (2 + (len(buffers) if last else 1)),
            scratch_shapes=scratches(n_sta, cap, 2 * rows),
            compiler_params=params(22),
            cost_estimate=cost(dft_flops * rows, 4 << 20),
        )(
            *in_smem(starts),
            *in_vmem(main, *edges[2 * i : 2 * i + 2], *(edges[:2] if i else [])),
            *in_vmem(taper, t_odd, t_even, send_rows, *late_out),
        )
        whites = whites + list(result[:2])
        late_out = result[2:]
    late_in = exchange(late_out)
    early, first, hot = pl.pallas_call(
        functools.partial(early_kernel, groups, len(buffers), n_chunks, scale),
        out_shape=[
            pltpu.VMEM((pairs, 2 * NF), F32),
            pltpu.VMEM((2, pairs, 2 * NF), F32),
            pltpu.VMEM((pairs, width), BF16),
        ],
        in_specs=[VMEM] * (4 + 2 * n_chunks + len(buffers)),
        out_specs=[VMEM] * 3,
        scratch_shapes=pair_scratch,
        compiler_params=params(16),
        cost_estimate=cost(2 * 2 * pairs * (2 * stations + width) * 2 * NF, 4 << 20),
        name="early_pairs",
    )(first_row, slot_row, *in_vmem(white0, white3, *whites, *early_in))

    lag_rows = NL // n_tm
    n_half = 2
    half = pairs // n_half
    steps = [1 << k for k in range(n_tm.bit_length() - 1)]
    done = []
    parts = []
    for h in range(n_half):
        parts.append(
            pl.pallas_call(
                functools.partial(late_kernel, groups, len(buffers), n_tm, h * half),
                out_shape=[pltpu.VMEM((NL // 2, half), BF16), pltpu.VMEM((NL // 2, half), F32)],
                in_specs=[VMEM] * (5 + len(buffers)),
                out_specs=[VMEM] * 2,
                scratch_shapes=[
                    pltpu.VMEM((2, width, 2 * NF), BF16),
                    pltpu.VMEM((2, half, 2 * NF), F32),
                    pltpu.VMEM((half, NF), BF16),
                    pltpu.VMEM((half, NF), BF16),
                ],
                compiler_params=params(10),
                cost_estimate=cost(2 * 2 * half * width * 2 * NF + 2 * NL * half * 2 * NF, 3 << 20),
            )(*in_vmem(early, first, hot, t_odd, t_even, *late_in))
        )
    for step in steps:
        route = [(i, i ^ step) for i in range(n_tm)]
        received = [lax.ppermute(send, "tm", route) for send, _ in parts]
        if step == steps[-1]:
            done = [x for (_, keep), got in zip(parts, received) for x in (keep, got)]
            break
        merged = []
        for h in range(n_half):
            keep = parts[h][1]
            rows = keep.shape[0] // 2
            merged.append(
                pl.pallas_call(
                    functools.partial(merge_kernel, lag_rows),
                    out_shape=[pltpu.VMEM((rows, half), BF16), pltpu.VMEM((rows, half), F32)],
                    in_specs=[VMEM] * 2,
                    out_specs=[VMEM] * 2,
                    compiler_params=params(1),
                    cost_estimate=cost(rows * half, 1 << 20),
                )(*in_vmem(keep, received[h]))
            )
        parts = merged
    return pl.pallas_call(
        finish_kernel,
        out_shape=jax.ShapeDtypeStruct((lag_rows, pairs), F32),
        in_specs=[VMEM] * len(done),
        out_specs=VMEM,
        compiler_params=params(2),
        cost_estimate=cost(lag_rows * pairs, 1 << 20),
        name="finish",
    )(*in_vmem(*done))


def solution(mesh):
    in_specs = (P("sta", ("day", "tm")), P(("day", "tm")), P("sta"), P("sta"), P("sta", None))
    out_specs = P(("day", "tm"), "sta")
    return jax.shard_map(
        on_device, mesh=mesh, in_specs=in_specs, out_specs=out_specs, check_vma=False
    )
```

```python
import functools
import math

import jax
import jax.numpy as jnp
import numpy as np
from jax import lax
from jax.experimental import pallas as pl
from jax.experimental.pallas import tpu as pltpu
from jax.sharding import PartitionSpec as P


WIN = 2048
NF = 512
NL = 1024
FLOOR = 0.1
STEP = 1024
HALF = 1024
CAP_FAR = 8
LANES = 128
CHUNKS = WIN // LANES
HC = CHUNKS // 2
QB = NF // 2
ROOT = 1.0 / math.sqrt(WIN)
F32 = jnp.float32
BF16 = jnp.bfloat16
ROWS = 16
UNIT = 512
VMEM = pl.BlockSpec(memory_space=pltpu.VMEM)
SMEM = pl.BlockSpec(memory_space=pltpu.SMEM)
ANY = pl.BlockSpec(memory_space=pltpu.HBM)


def loop(count, most, body):
    trips = count // ROWS
    unroll = max(u for u in range(1, most + 1) if trips % u == 0)
    lax.fori_loop(0, trips, body, 0, unroll=unroll)


def small_tables():
    step = np.arange(32)[:, None]
    half = np.arange(QB)
    freq = np.concatenate([2 * half + 1, 2 * half + 2])[None, :]
    angles = np.concatenate([32 * step, step], axis=0) * freq % WIN * (2.0 * np.pi / WIN)
    return np.cos(angles).astype(np.float32), np.sin(angles).astype(np.float32)


def taper_row():
    index = np.arange(WIN)
    return (0.5 - 0.5 * np.cos(2.0 * np.pi * index / WIN)).astype(np.float32)[None, :]


def fill_tables(cos_ref, sin_ref, odd_ref, even_ref):
    def block(a, carry):
        ca = cos_ref[pl.ds(a, 1), :]
        sa = sin_ref[pl.ds(a, 1), :]
        cb = cos_ref[32:64, :]
        sb = sin_ref[32:64, :]
        c = (ca * cb - sa * sb).astype(BF16)
        s = (-(sa * cb + ca * sb)).astype(BF16)
        rows = pl.ds(pl.multiple_of(a * 32, 32), 32)
        odd_ref[rows, :QB] = c[:, :QB]
        odd_ref[rows, QB:] = s[:, :QB]
        even_ref[rows, :QB] = c[:, QB:]
        even_ref[rows, QB:] = s[:, QB:]
        return carry

    lax.fori_loop(0, HALF // 32, block, 0)


def prepare(pick, start, count, to, taper_ref, scratch):
    rolled_ref, sums_ref, even_ref, odd_ref = scratch[:4]
    q = start // LANES
    s = start % LANES
    shift = (LANES - s) % LANES
    places = [(c + q) % CHUNKS for c in range(CHUNKS)]
    keep = lax.broadcasted_iota(jnp.int32, (ROWS, LANES), 1) < LANES - s

    def turn(i, carry):
        rows = pl.ds(pl.multiple_of(i * ROWS, ROWS), ROWS)
        rolled = [pltpu.roll(pick(rows, c).astype(F32), shift, 1) for c in range(CHUNKS)]
        turned = [jnp.where(keep, rolled[c], rolled[(c + 1) % CHUNKS]) for c in range(CHUNKS)]
        for c in range(CHUNKS):
            rolled_ref[c, rows, :] = turned[c]
        while len(turned) > 1:
            turned = [turned[2 * k] + turned[2 * k + 1] for k in range(len(turned) // 2)]
        sums_ref[rows, :] = turned[0]
        return carry

    loop(count, 4, turn)

    def average(i, carry):
        rows = pl.ds(pl.multiple_of(i * ROWS, ROWS), ROWS)
        mean = jnp.sum(sums_ref[rows, :], axis=1, keepdims=True) * (1.0 / WIN)
        sums_ref[rows, :] = jnp.broadcast_to(mean, (ROWS, LANES))
        return carry

    loop(count, 16, average)

    def fold(i, carry):
        rows = pl.ds(pl.multiple_of(i * ROWS, ROWS), ROWS)
        put = pl.ds(pl.multiple_of(to + i * ROWS, ROWS), ROWS)
        mean = sums_ref[rows, :]
        for c in range(HC):
            low = rolled_ref[places[c], rows, :]
            high = rolled_ref[places[c + HC], rows, :]
            low = ((low - mean) * taper_ref[:, c * LANES : (c + 1) * LANES]).astype(BF16)
            high = (high - mean) * taper_ref[:, (c + HC) * LANES : (c + HC + 1) * LANES]
            high = high.astype(BF16)
            even_ref[c, put, :] = low + high
            odd_ref[c, put, :] = low - high
        return carry

    loop(count, 4, fold)


def transform(count, t_odd, t_even, scratch):
    even_ref, odd_ref, spec = scratch[2:5]
    odd = jnp.concatenate([odd_ref[c, :count] for c in range(HC)], axis=1)
    spec[:count, : 2 * QB] = jnp.dot(odd, t_odd[...], preferred_element_type=F32)
    even = jnp.concatenate([even_ref[c, :count] for c in range(HC)], axis=1)
    spec[:count, 2 * QB :] = jnp.dot(even, t_even[...], preferred_element_type=F32)


def whiten_rows(first_row, count, live, out_ref, scratch):
    spec_ref = scratch[4]
    lane = lax.broadcasted_iota(jnp.int32, (ROWS, LANES), 1)
    not_first = lane > 0
    not_last = lane < LANES - 1
    numerator = live * (5.0 * ROOT)

    def up(x):
        a, b = (pltpu.roll(h, 1, 1) for h in x)
        return jnp.where(not_first, a, 0.0), jnp.where(not_first, b, a)

    def down(x):
        a, b = (pltpu.roll(h, LANES - 1, 1) for h in x)
        return jnp.where(not_last, a, b), jnp.where(not_last, b, 0.0)

    def amplitude(re, im):
        power = (re * re + im * im) * (1.0 / WIN) + 1e-06
        return power * lax.rsqrt(power)

    def inverse(*terms):
        return [
            numerator / jnp.maximum(a + b + c, 5.0 * FLOOR) for a, b, c in zip(*terms)
        ]

    def group(i, carry):
        rows = pl.ds(pl.multiple_of(first_row + i * ROWS, ROWS), ROWS)
        to = pl.ds(pl.multiple_of(i * ROWS, ROWS), ROWS)
        parts = [
            [spec_ref[rows, k * QB + h * LANES : k * QB + (h + 1) * LANES] for h in range(2)]
            for k in range(4)
        ]
        odd = [amplitude(parts[0][h], parts[1][h]) for h in range(2)]
        even = [amplitude(parts[2][h], parts[3][h]) for h in range(2)]
        both = [odd[h] + even[h] for h in range(2)]
        inv_odd = inverse(up(both), both, down(odd))
        inv_even = inverse(up(even), both, down(both))
        for h in range(2):
            at = h * LANES
            for k, j, inv in ((0, 0, inv_odd), (1, 2, inv_odd), (2, 1, inv_even), (3, 3, inv_even)):
                out_ref[to, j * QB + at : j * QB + at + LANES] = (parts[k][h] * inv[h]).astype(BF16)
        return carry

    loop(count, 12, group)


def slots(c):
    return c * LANES + lax.broadcasted_iota(jnp.int32, (ROWS, LANES), 1)


def part(ref, offset, rows, c):
    return ref[rows, offset + c * LANES : offset + (c + 1) * LANES].astype(F32)


def shifted_rows(ref, first):
    def get(rows, offset, c):
        at = pl.ds(pl.multiple_of(rows.start + first, ROWS), ROWS)
        return part(ref, offset, at, c)

    return get


def column(row):
    n = row.shape[1]
    return jnp.transpose(jnp.broadcast_to(row.astype(F32), (LANES, n)))


def one_hot(col, width, first=0):
    pieces = []
    for at in range(0, width, LANES):
        lane = lax.broadcasted_iota(jnp.int32, col.shape, 1) + (first + at)
        pieces.append(jnp.where(lane.astype(F32) == col, 1.0, 0.0).astype(BF16))
    hot = pieces[0] if len(pieces) == 1 else jnp.concatenate(pieces, axis=1)
    return hot[:, :width]


def outgoing(send_rows, first, spectra, before, out):
    col = column(send_rows[...])
    hot = one_hot(col, spectra[0].shape[0], first)
    for w in range(2):
        value = jnp.dot(hot, spectra[w][...], preferred_element_type=F32)
        out[w] = value if before is None else before[w] + value


def write_rows(groups, rows, refs):
    near, far, n_sta, cap = groups
    g = lax.axis_index("sta")
    for ref, d in zip(refs, near + far):
        first = pl.multiple_of(peer(d, g, n_sta) * cap, cap)
        n = CAP_FAR if d in far else cap
        for w in range(2):
            ref[w * n : (w + 1) * n, :] = rows[w, pl.ds(first, n), :].astype(BF16)


def scratches(n_sta, cap, rows):
    return [
        pltpu.VMEM((CHUNKS, rows, LANES), F32),
        pltpu.VMEM((rows, LANES), F32),
        pltpu.VMEM((HC, rows, LANES), BF16),
        pltpu.VMEM((HC, rows, LANES), BF16),
        pltpu.VMEM((rows, 2 * NF), F32),
        pltpu.VMEM((2, n_sta * cap, 2 * NF), F32),
    ]


def local_kernel(groups, offsets, main, cos_t, sin_t, taper, send_rows, *rest):
    t_odd, t_even, white0, white3 = rest[:4]
    scratch = rest[-6:]
    sends = rest[4:-6]
    fill_tables(cos_t, sin_t, t_odd, t_even)
    start0 = offsets[0]
    start3 = offsets[2] - 2 * STEP
    live3 = jnp.where(lax.axis_index("tm") == lax.axis_size("tm") - 1, 1.0, 0.0).astype(F32)
    stations = main.shape[0]
    for first in range(0, stations, UNIT):
        count = min(UNIT, stations - first)
        get = shifted_rows(main, first)

        def pick0(rows, c):
            if c >= HC:
                return get(rows, HALF, c - HC)
            return jnp.where(slots(c) >= start0, get(rows, 0, c), get(rows, 2 * HALF, c))

        def pick3(rows, c):
            if c >= HC:
                return jnp.zeros((ROWS, LANES), F32)
            return jnp.where(slots(c) >= start3, get(rows, 2 * HALF, c), 0.0)

        for pick, start, live, white in ((pick0, start0, 1.0, white0), (pick3, start3, live3, white3)):
            prepare(pick, start, count, 0, taper, scratch)
            transform(count, t_odd, t_even, scratch)
            whiten_rows(0, count, live, white.at[first : first + count], scratch)
    outgoing(send_rows, 0, (white0, white3), None, scratch[5])
    write_rows(groups, scratch[5], sends)


def peer(d, g, n):
    if d == "own":
        return g
    if d == "even":
        return g + 1 - 2 * (g % 2)
    if d == "odd":
        return (g - 1 + 2 * (g % 2) + n) % n
    return (g + d) % n


def swap_routes(n):
    routes = []
    for first in (0, 1):
        partner = list(range(n))
        for i in range(first, n - 1, 2):
            partner[i], partner[i + 1] = i + 1, i
        routes.append(list(enumerate(partner)))
    return routes


def pack_kernel(first, count, n_small, head, offsets, main, *rest):
    small = rest[:n_small]
    outs = rest[n_small : n_small + 2]
    small_out = rest[n_small + 2 : 2 * n_small + 2]
    offsets_out = rest[2 * n_small + 2]
    sems = rest[-1]
    t = lax.axis_index("tm")
    n = lax.axis_size("tm")

    def edge(swap):
        at = jnp.where(t % 2 == swap, 2 * HALF, 0)
        lanes = pl.ds(pl.multiple_of(at, LANES), HALF)
        source = main.at[pl.ds(first, count), lanes]
        return pltpu.make_async_copy(source, outs[swap].at[pl.ds(0, count)], sems.at[swap])

    copies = []
    for swap in range(2):
        if n % 2 == swap:
            copies.append(edge(swap))
            copies[-1].start()
        else:
            @pl.when(t == n - 1)
            def _():
                outs[swap][0:count, :] = jnp.zeros((count, HALF), BF16)

            @pl.when(t < n - 1)
            def _():
                edge(swap).start()
    for k in range(n_small):
        copies.append(pltpu.make_async_copy(small[k], small_out[k], sems.at[3 + k]))
        copies[-1].start()
    if head:
        numbers = pltpu.make_async_copy(offsets, offsets_out, sems.at[2])
        numbers.start()
        numbers.wait()
        start = offsets_out[2] - 2 * STEP
        high, low = start // 8, start % 8
        lane = lax.broadcasted_iota(jnp.int32, (ROWS, HALF), 1)
        for out in outs:
            out[count:, :] = jnp.where(lane < NF, high, low).astype(F32).astype(BF16)
    for copy in copies:
        copy.wait()
    for swap in range(2):
        if n % 2 != swap:
            @pl.when(t < n - 1)
            def _():
                edge(swap).wait()


def sent_start(ref):
    rows = ref.shape[0] - ROWS
    high = jnp.max(ref[rows:, 0:LANES].astype(F32))
    low = jnp.max(ref[rows:, HALF - LANES :].astype(F32))
    return (high * 8.0 + low).astype(jnp.int32)


def rim_kernel(groups, first, earlier, last, offsets, main, *rest):
    recv = rest[:2]
    heads = rest[2:4] if earlier else recv
    rest = rest[4 if earlier else 2 :]
    taper, t_odd, t_even, send_rows = rest[:4]
    rest = rest[4:]
    before = rest[0] if earlier else None
    rest = rest[2:] if earlier else rest
    whites = rest[:2]
    scratch = rest[-6:]
    sends = rest[2:-6]
    count = whites[0].shape[0]
    t = lax.axis_index("tm")
    lane = lax.broadcasted_iota(jnp.int32, (ROWS, LANES), 1)
    for swap in range(2):
        ahead = t % 2 == swap
        start = jnp.where(ahead, offsets[1] - STEP, sent_start(heads[swap]))
        sign = jnp.where(ahead, 1, -1)
        least = jnp.where(ahead, 0, 1)
        whole = jnp.where(ahead, 2 * HALF, 0)
        base = (lane - start) * sign

        def pick(rows, c):
            at = pl.ds(pl.multiple_of(rows.start + first, ROWS), ROWS)
            if c >= HC:
                return main[at, pl.ds(pl.multiple_of(whole + (c - HC) * LANES, LANES), LANES)].astype(F32)
            own = part(main, HALF, at, c)
            return jnp.where(base >= least - sign * (c * LANES), own, part(recv[swap], 0, rows, c))

        prepare(pick, start, count, swap * count, taper, scratch)
    transform(2 * count, t_odd, t_even, scratch)
    live = jnp.where(t > 0, 1.0, 0.0).astype(F32)
    whiten_rows(0, count, 1.0, whites[0], scratch)
    whiten_rows(count, count, live, whites[1], scratch)
    if last:
        outgoing(send_rows, first, whites, before, scratch[5])
        write_rows(groups, scratch[5], sends)
    else:
        outgoing(send_rows, first, whites, before, sends[0])


def slot_table(groups, pair_slot, width):
    near, far, n_sta, cap = groups
    g = lax.axis_index("sta")
    slot = pair_slot[...]
    place = jnp.zeros_like(slot)
    at = 0
    for d in near + far:
        source = (g - d + n_sta) % n_sta if d in far else peer(d, g, n_sta)
        place = jnp.where(slot // cap == source, at + slot % cap, place)
        at += CAP_FAR if d in far else cap
    return one_hot(column(place), width)


def second_rows(groups, pieces, hot, first_pair, incoming, out):
    near, far, _, cap = groups
    width = incoming.shape[1]
    for w in range(2):
        at = 0
        for i, d in enumerate(near + far):
            n = CAP_FAR if d in far else cap
            incoming[w, at : at + n, :] = pieces[i][w * n : (w + 1) * n, :]
            at += n
        if at < width:
            incoming[w, at:, :] = jnp.zeros((width - at, 2 * NF), BF16)
    for w in range(2):
        for c in range(0, 2 * NF, NF):
            rows = hot[first_pair : first_pair + out.shape[1], :]
            out[w, :, c : c + NF] = jnp.dot(rows, incoming[w, :, c : c + NF], preferred_element_type=F32)


def first_rows(hots, spectra, scale, out):
    lane = lax.broadcasted_iota(jnp.int32, (1, QB), 1)
    s = jnp.where(lane % 2 == 0, scale, -scale).astype(F32)
    for c in range(0, 2 * NF, QB):
        total = None
        for hot, piece in zip(hots, spectra):
            term = jnp.dot(hot, piece[:, c : c + QB], preferred_element_type=F32)
            total = term if total is None else total + term
        out[:, c : c + QB] = total * (s if c % NF == 0 else -s)


def station_tables(col, spectra):
    hots, at = [], 0
    for piece in spectra:
        hots.append(one_hot(col, piece.shape[0], at))
        at += piece.shape[0]
    return hots


def add_products(first, second, first_at, second_at, c, start):
    re_lanes = slice(c, c + LANES)
    im_lanes = slice(NF + c, NF + c + LANES)
    one, two = start
    for w in range(2):
        a_i, b_i = first[w, first_at, re_lanes], first[w, first_at, im_lanes]
        a_j, b_j = second[w, second_at, re_lanes], second[w, second_at, im_lanes]
        re = a_i * a_j + b_i * b_j
        im = b_i * a_j - a_i * b_j
        if c < QB:
            one, two = one + im, two - re
        else:
            one, two = one + re, two + im
    return one, two


def early_kernel(groups, n_pieces, scale, pair_first, pair_slot, white0, white3, *rest):
    pieces = rest[:n_pieces]
    cross, hot = rest[n_pieces + 1 : n_pieces + 3]
    incoming, first, second = rest[n_pieces + 3 :]
    pairs = pair_first.shape[1]
    hots = station_tables(column(pair_first[...]), (white0,))
    first_rows(hots, (white0,), scale, first.at[0])
    first_rows(hots, (white3,), scale, first.at[1])
    hot[...] = slot_table(groups, pair_slot, hot.shape[1])
    second_rows(groups, pieces, hot, 0, incoming, second)

    def group(i, carry):
        rows = pl.ds(pl.multiple_of(i * ROWS, ROWS), ROWS)
        for c in range(0, NF, LANES):
            one, two = add_products(first, second, rows, rows, c, (0.0, 0.0))
            cross[rows, c : c + LANES] = one
            cross[rows, NF + c : NF + c + LANES] = two
        return carry

    loop(pairs, 2, group)


def first_kernel(scale, n_white, pair_first, *rest):
    whites = rest[: 2 * n_white]
    out = rest[2 * n_white]
    hots = station_tables(column(pair_first[...]), whites[0::2])
    first_rows(hots, whites[0::2], scale, out.at[0])
    first_rows(hots, whites[1::2], scale, out.at[1])


def late_kernel(groups, n_pieces, n_dest, first_pair, early, first, hot, t_odd, t_even, *rest):
    pieces = rest[:n_pieces]
    send, keep = rest[n_pieces : n_pieces + 2]
    incoming, second, x_odd, x_even = rest[n_pieces + 2 :]
    pairs = send.shape[1]
    second_rows(groups, pieces, hot, first_pair, incoming, second)

    def group(i, carry):
        rows = pl.ds(pl.multiple_of(i * ROWS, ROWS), ROWS)
        full = pl.ds(pl.multiple_of(first_pair + i * ROWS, ROWS), ROWS)
        for c in range(0, NF, LANES):
            start = (early[full, c : c + LANES], early[full, NF + c : NF + c + LANES])
            one, two = add_products(first, second, full, rows, c, start)
            out = x_odd if c < QB else x_even
            at = c % QB
            out[rows, at : at + LANES] = one.astype(BF16)
            out[rows, QB + at : QB + at + LANES] = two.astype(BF16)
        return carry

    loop(pairs, 2, group)
    lag_rows = NL // n_dest
    me = lax.axis_index("tm")
    dims = (((1,), (1,)), ((), ()))
    for out, order in ((send, range(1, n_dest, 2)), (keep, range(0, n_dest, 2))):
        spots = [
            pl.ds(pl.multiple_of(jnp.bitwise_xor(me, r) * lag_rows, lag_rows), lag_rows) for r in order
        ]
        odd = jnp.concatenate([t_odd[at, :] for at in spots], axis=0)
        even = jnp.concatenate([t_even[at, :] for at in spots], axis=0)
        value = lax.dot_general(odd, x_odd[...], dims, preferred_element_type=F32)
        value = value + lax.dot_general(even, x_even[...], dims, preferred_element_type=F32)
        out[...] = value.astype(out.dtype)


def merge_kernel(lag_rows, keep, received, send, kept):
    for k in range(keep.shape[0] // lag_rows):
        rows = slice(k * lag_rows, (k + 1) * lag_rows)
        out, j = (send, k // 2) if k % 2 else (kept, k // 2)
        value = keep[rows, :] + received[rows, :].astype(F32)
        out[j * lag_rows : (j + 1) * lag_rows, :] = value.astype(out.dtype)


def finish_kernel(*refs):
    out = refs[-1]
    at = 0
    for keep, received in zip(refs[0:-1:2], refs[1:-1:2]):
        width = keep.shape[1]
        out[:, at : at + width] = keep[...] + received[...].astype(F32)
        at += width


def in_vmem(*arrays):
    return [pltpu.with_memory_space_constraint(a, pltpu.VMEM) for a in arrays]


def in_smem(*arrays):
    return [pltpu.with_memory_space_constraint(a, pltpu.SMEM) for a in arrays]


def in_hbm(*arrays):
    return [pltpu.with_memory_space_constraint(a, pltpu.HBM) for a in arrays]


def params(mib):
    return pltpu.CompilerParams(vmem_limit_bytes=mib << 20)


def cost(flops, moved):
    return pl.CostEstimate(flops=int(flops), bytes_accessed=int(moved), transcendentals=0)


def on_device(traces, offsets, pair_first, pair_slot, send_rows):
    stations, _ = traces.shape
    n_tm = lax.axis_size("tm")
    n_sta = lax.axis_size("sta")
    windows = offsets.shape[0]
    pairs = pair_first.shape[0]
    cap = send_rows.shape[1] // n_sta

    sizes = (stations * 5 // 8, stations * 3 // 8)
    n_chunks = len(sizes)
    main, = in_vmem(traces)
    routes = swap_routes(n_tm)
    small = [jnp.asarray(x) for x in small_tables()] + [jnp.asarray(taper_row()), send_rows]
    edges = []
    for i, rows in enumerate(sizes):
        head = i == 0
        extra = [] if head else small
        packed = pl.pallas_call(
            functools.partial(pack_kernel, sum(sizes[:i]), rows, len(extra), head),
            out_shape=[pltpu.VMEM((rows + (ROWS if head else 0), HALF), BF16)] * 2
            + [pltpu.VMEM(x.shape, x.dtype) for x in extra]
            + [pltpu.SMEM(offsets.shape, jnp.int32)],
            in_specs=[ANY] * (2 + len(extra)),
            out_specs=[VMEM] * (2 + len(extra)) + [SMEM],
            scratch_shapes=[pltpu.SemaphoreType.DMA((3 + len(extra),))],
            compiler_params=params(1),
            cost_estimate=cost(0, 2 << 20),
        )(*in_hbm(offsets, traces, *extra))
        if head:
            starts = packed[-1]
        else:
            cos_t, sin_t, taper, send_rows = packed[2:-1]
        got = [None, None]
        for swap in (1, 0):
            got[swap] = lax.ppermute(packed[swap], "tm", routes[swap])
        edges += got

    near = ["own", "even", "odd"]
    far = list(range(2, n_sta - 1))
    groups = (near, far, n_sta, cap)
    width = -(-(len(near) * cap + len(far) * CAP_FAR) // LANES) * LANES
    first_row, slot_row = pair_first[None, :], pair_slot[None, :]

    buffers = [pltpu.VMEM((2 * (CAP_FAR if d in far else cap), 2 * NF), BF16) for d in near + far]
    dft_flops = 2 * 2 * HALF * 2 * QB * 2
    spectrum = pltpu.VMEM((stations, 2 * NF), BF16)
    table = pltpu.VMEM((HALF, 2 * QB), BF16)
    local = pl.pallas_call(
        functools.partial(local_kernel, groups),
        out_shape=[table] * 2 + [spectrum] * 2 + buffers,
        in_specs=[SMEM] + [VMEM] * 5,
        out_specs=[VMEM] * (4 + len(buffers)),
        scratch_shapes=scratches(n_sta, cap, UNIT),
        compiler_params=params(18),
        cost_estimate=cost(dft_flops * stations, 8 << 20),
        name="local_windows",
    )(*in_smem(starts), *in_vmem(main, cos_t, sin_t, taper, send_rows))
    t_odd, t_even, white0, white3 = local[:4]

    def exchange(pieces):
        got = list(pieces)
        for i, d in sorted(enumerate(near + far), key=lambda x: (2, 1, 0)[near.index(x[1])] if x[1] in near else 3):
            if d != "own":
                route = [(k, peer(d, k, n_sta)) for k in range(n_sta)]
                got[i] = lax.ppermute(pieces[i], "sta", route)
        return got

    early_in = exchange(local[4:])
    scale = 1.0 / math.sqrt(NF * windows * n_tm)
    pair_scratch = [
        pltpu.VMEM((2, width, 2 * NF), BF16),
        pltpu.VMEM((2, pairs, 2 * NF), F32),
        pltpu.VMEM((2, pairs, 2 * NF), F32),
    ]
    whites = []
    late_out = []
    outgoing_rows = pltpu.VMEM((2, n_sta * cap, 2 * NF), F32)
    for i in range(n_chunks):
        last = i == n_chunks - 1
        rows = sizes[i]
        chunk = pltpu.VMEM((rows, 2 * NF), BF16)
        result = pl.pallas_call(
            functools.partial(rim_kernel, groups, sum(sizes[:i]), i, last),
            out_shape=[chunk] * 2 + (buffers if last else [outgoing_rows]),
            in_specs=[SMEM] + [VMEM] * (7 + 4 * min(i, 1)),
            out_specs=[VMEM] * (2 + (len(buffers) if last else 1)),
            scratch_shapes=scratches(n_sta, cap, 2 * rows),
            compiler_params=params(22),
            cost_estimate=cost(dft_flops * rows, 4 << 20),
        )(
            *in_smem(starts),
            *in_vmem(main, *edges[2 * i : 2 * i + 2], *(edges[:2] if i else [])),
            *in_vmem(taper, t_odd, t_even, send_rows, *late_out, *([hot] if i else [])),
        )
        whites = whites + list(result[:2])
        late_out = result[2:]
        if i == 0:
            early, hot = pl.pallas_call(
                functools.partial(early_kernel, groups, len(buffers), scale),
                out_shape=[pltpu.VMEM((pairs, 2 * NF), F32), pltpu.VMEM((pairs, width), BF16)],
                in_specs=[VMEM] * (5 + len(buffers)),
                out_specs=[VMEM] * 2,
                scratch_shapes=pair_scratch,
                compiler_params=params(16),
                cost_estimate=cost(2 * 2 * pairs * (stations + width) * 2 * NF, 4 << 20),
                name="early_pairs",
            )(first_row, slot_row, *in_vmem(white0, white3, *early_in, *late_out))
    late_in = exchange(late_out)
    first = pl.pallas_call(
        functools.partial(first_kernel, scale, n_chunks),
        out_shape=pltpu.VMEM((2, pairs, 2 * NF), F32),
        in_specs=[VMEM] * (1 + 2 * n_chunks),
        out_specs=VMEM,
        compiler_params=params(4),
        cost_estimate=cost(2 * 2 * pairs * stations * 2 * NF, 4 << 20),
        name="first_pairs",
    )(first_row, *in_vmem(*whites))

    lag_rows = NL // n_tm
    n_half = 2
    half = pairs // n_half
    steps = [1 << k for k in range(n_tm.bit_length() - 1)]
    done = []
    parts = []
    for h in range(n_half):
        parts.append(
            pl.pallas_call(
                functools.partial(late_kernel, groups, len(buffers), n_tm, h * half),
                out_shape=[pltpu.VMEM((NL // 2, half), BF16), pltpu.VMEM((NL // 2, half), F32)],
                in_specs=[VMEM] * (5 + len(buffers)),
                out_specs=[VMEM] * 2,
                scratch_shapes=[
                    pltpu.VMEM((2, width, 2 * NF), BF16),
                    pltpu.VMEM((2, half, 2 * NF), F32),
                    pltpu.VMEM((half, NF), BF16),
                    pltpu.VMEM((half, NF), BF16),
                ],
                compiler_params=params(10),
                cost_estimate=cost(2 * 2 * half * width * 2 * NF + 2 * NL * half * 2 * NF, 3 << 20),
            )(*in_vmem(early, first, hot, t_odd, t_even, *late_in))
        )
    for step in steps:
        route = [(i, i ^ step) for i in range(n_tm)]
        received = [lax.ppermute(send, "tm", route) for send, _ in parts]
        if step == steps[-1]:
            done = [x for (_, keep), got in zip(parts, received) for x in (keep, got)]
            break
        merged = []
        for h in range(n_half):
            keep = parts[h][1]
            rows = keep.shape[0] // 2
            merged.append(
                pl.pallas_call(
                    functools.partial(merge_kernel, lag_rows),
                    out_shape=[pltpu.VMEM((rows, half), BF16), pltpu.VMEM((rows, half), F32)],
                    in_specs=[VMEM] * 2,
                    out_specs=[VMEM] * 2,
                    compiler_params=params(1),
                    cost_estimate=cost(rows * half, 1 << 20),
                )(*in_vmem(keep, received[h]))
            )
        parts = merged
    return pl.pallas_call(
        finish_kernel,
        out_shape=jax.ShapeDtypeStruct((lag_rows, pairs), F32),
        in_specs=[VMEM] * len(done),
        out_specs=VMEM,
        compiler_params=params(2),
        cost_estimate=cost(lag_rows * pairs, 1 << 20),
        name="finish",
    )(*in_vmem(*done))


def solution(mesh):
    in_specs = (P("sta", ("day", "tm")), P(("day", "tm")), P("sta"), P("sta"), P("sta", None))
    out_specs = P(("day", "tm"), "sta")
    return jax.shard_map(
        on_device, mesh=mesh, in_specs=in_specs, out_specs=out_specs, check_vma=False
    )
```

```python
import functools
import math

import jax
import jax.numpy as jnp
import numpy as np
from jax import lax
from jax.experimental import pallas as pl
from jax.experimental.pallas import tpu as pltpu
from jax.sharding import PartitionSpec as P


WIN = 2048
NF = 512
NL = 1024
FLOOR = 0.1
STEP = 1024
HALF = 1024
CAP_FAR = 8
LANES = 128
CHUNKS = WIN // LANES
HC = CHUNKS // 2
QB = NF // 2
ROOT = 1.0 / math.sqrt(WIN)
F32 = jnp.float32
BF16 = jnp.bfloat16
ROWS = 16
UNIT = 512
VMEM = pl.BlockSpec(memory_space=pltpu.VMEM)
SMEM = pl.BlockSpec(memory_space=pltpu.SMEM)
ANY = pl.BlockSpec(memory_space=pltpu.HBM)


def loop(count, most, body):
    trips = count // ROWS
    unroll = max(u for u in range(1, most + 1) if trips % u == 0)
    lax.fori_loop(0, trips, body, 0, unroll=unroll)


def small_tables():
    step = np.arange(32)[:, None]
    half = np.arange(QB)
    freq = np.concatenate([2 * half + 1, 2 * half + 2])[None, :]
    angles = np.concatenate([32 * step, step], axis=0) * freq % WIN * (2.0 * np.pi / WIN)
    return np.cos(angles).astype(np.float32), np.sin(angles).astype(np.float32)


def taper_row():
    index = np.arange(WIN)
    return (0.5 - 0.5 * np.cos(2.0 * np.pi * index / WIN)).astype(np.float32)[None, :]


def fill_tables(cos_ref, sin_ref, odd_ref, even_ref):
    def block(a, carry):
        ca = cos_ref[pl.ds(a, 1), :]
        sa = sin_ref[pl.ds(a, 1), :]
        cb = cos_ref[32:64, :]
        sb = sin_ref[32:64, :]
        c = (ca * cb - sa * sb).astype(BF16)
        s = (-(sa * cb + ca * sb)).astype(BF16)
        rows = pl.ds(pl.multiple_of(a * 32, 32), 32)
        odd_ref[rows, :QB] = c[:, :QB]
        odd_ref[rows, QB:] = s[:, :QB]
        even_ref[rows, :QB] = c[:, QB:]
        even_ref[rows, QB:] = s[:, QB:]
        return carry

    lax.fori_loop(0, HALF // 32, block, 0)


def prepare(pick, start, count, to, taper_ref, scratch):
    rolled_ref, sums_ref, even_ref, odd_ref = scratch[:4]
    q = start // LANES
    s = start % LANES
    shift = (LANES - s) % LANES
    places = [(c + q) % CHUNKS for c in range(CHUNKS)]
    keep = lax.broadcasted_iota(jnp.int32, (ROWS, LANES), 1) < LANES - s

    def turn(i, carry):
        rows = pl.ds(pl.multiple_of(i * ROWS, ROWS), ROWS)
        rolled = [pltpu.roll(pick(rows, c).astype(F32), shift, 1) for c in range(CHUNKS)]
        turned = [jnp.where(keep, rolled[c], rolled[(c + 1) % CHUNKS]) for c in range(CHUNKS)]
        for c in range(CHUNKS):
            rolled_ref[c, rows, :] = turned[c]
        while len(turned) > 1:
            turned = [turned[2 * k] + turned[2 * k + 1] for k in range(len(turned) // 2)]
        sums_ref[rows, :] = turned[0]
        return carry

    loop(count, 4, turn)

    def average(i, carry):
        rows = pl.ds(pl.multiple_of(i * ROWS, ROWS), ROWS)
        mean = jnp.sum(sums_ref[rows, :], axis=1, keepdims=True) * (1.0 / WIN)
        sums_ref[rows, :] = jnp.broadcast_to(mean, (ROWS, LANES))
        return carry

    loop(count, 16, average)

    def fold(i, carry):
        rows = pl.ds(pl.multiple_of(i * ROWS, ROWS), ROWS)
        put = pl.ds(pl.multiple_of(to + i * ROWS, ROWS), ROWS)
        mean = sums_ref[rows, :]
        for c in range(HC):
            low = rolled_ref[places[c], rows, :]
            high = rolled_ref[places[c + HC], rows, :]
            low = ((low - mean) * taper_ref[:, c * LANES : (c + 1) * LANES]).astype(BF16)
            high = (high - mean) * taper_ref[:, (c + HC) * LANES : (c + HC + 1) * LANES]
            high = high.astype(BF16)
            even_ref[c, put, :] = low + high
            odd_ref[c, put, :] = low - high
        return carry

    loop(count, 4, fold)


def transform(count, t_odd, t_even, scratch):
    even_ref, odd_ref, spec = scratch[2:5]
    odd = jnp.concatenate([odd_ref[c, :count] for c in range(HC)], axis=1)
    spec[:count, : 2 * QB] = jnp.dot(odd, t_odd[...], preferred_element_type=F32)
    even = jnp.concatenate([even_ref[c, :count] for c in range(HC)], axis=1)
    spec[:count, 2 * QB :] = jnp.dot(even, t_even[...], preferred_element_type=F32)


def whiten_rows(first_row, count, live, out_ref, scratch):
    spec_ref = scratch[4]
    lane = lax.broadcasted_iota(jnp.int32, (ROWS, LANES), 1)
    not_first = lane > 0
    not_last = lane < LANES - 1
    numerator = live * (5.0 * ROOT)

    def up(x):
        a, b = (pltpu.roll(h, 1, 1) for h in x)
        return jnp.where(not_first, a, 0.0), jnp.where(not_first, b, a)

    def down(x):
        a, b = (pltpu.roll(h, LANES - 1, 1) for h in x)
        return jnp.where(not_last, a, b), jnp.where(not_last, b, 0.0)

    def amplitude(re, im):
        power = (re * re + im * im) * (1.0 / WIN) + 1e-06
        return power * lax.rsqrt(power)

    def inverse(*terms):
        return [
            numerator / jnp.maximum(a + b + c, 5.0 * FLOOR) for a, b, c in zip(*terms)
        ]

    def group(i, carry):
        rows = pl.ds(pl.multiple_of(first_row + i * ROWS, ROWS), ROWS)
        to = pl.ds(pl.multiple_of(i * ROWS, ROWS), ROWS)
        parts = [
            [spec_ref[rows, k * QB + h * LANES : k * QB + (h + 1) * LANES] for h in range(2)]
            for k in range(4)
        ]
        odd = [amplitude(parts[0][h], parts[1][h]) for h in range(2)]
        even = [amplitude(parts[2][h], parts[3][h]) for h in range(2)]
        both = [odd[h] + even[h] for h in range(2)]
        inv_odd = inverse(up(both), both, down(odd))
        inv_even = inverse(up(even), both, down(both))
        for h in range(2):
            at = h * LANES
            for k, j, inv in ((0, 0, inv_odd), (1, 2, inv_odd), (2, 1, inv_even), (3, 3, inv_even)):
                out_ref[to, j * QB + at : j * QB + at + LANES] = (parts[k][h] * inv[h]).astype(BF16)
        return carry

    loop(count, 12, group)


def slots(c):
    return c * LANES + lax.broadcasted_iota(jnp.int32, (ROWS, LANES), 1)


def part(ref, offset, rows, c):
    return ref[rows, offset + c * LANES : offset + (c + 1) * LANES].astype(F32)


def shifted_rows(ref, first):
    def get(rows, offset, c):
        at = pl.ds(pl.multiple_of(rows.start + first, ROWS), ROWS)
        return part(ref, offset, at, c)

    return get


def column(row):
    n = row.shape[1]
    return jnp.transpose(jnp.broadcast_to(row.astype(F32), (LANES, n)))


def one_hot(col, width, first=0):
    pieces = []
    for at in range(0, width, LANES):
        lane = lax.broadcasted_iota(jnp.int32, col.shape, 1) + (first + at)
        pieces.append(jnp.where(lane.astype(F32) == col, 1.0, 0.0).astype(BF16))
    hot = pieces[0] if len(pieces) == 1 else jnp.concatenate(pieces, axis=1)
    return hot[:, :width]


def outgoing(send_rows, first, spectra, before, out):
    col = column(send_rows[...])
    hot = one_hot(col, spectra[0].shape[0], first)
    for w in range(2):
        value = jnp.dot(hot, spectra[w][...], preferred_element_type=F32)
        out[w] = value if before is None else before[w] + value


def write_rows(groups, rows, refs):
    near, far, n_sta, cap = groups
    g = lax.axis_index("sta")
    for ref, d in zip(refs, near + far):
        first = pl.multiple_of(peer(d, g, n_sta) * cap, cap)
        n = CAP_FAR if d in far else cap
        for w in range(2):
            ref[w * n : (w + 1) * n, :] = rows[w, pl.ds(first, n), :].astype(BF16)


def scratches(n_sta, cap, rows):
    return [
        pltpu.VMEM((CHUNKS, rows, LANES), F32),
        pltpu.VMEM((rows, LANES), F32),
        pltpu.VMEM((HC, rows, LANES), BF16),
        pltpu.VMEM((HC, rows, LANES), BF16),
        pltpu.VMEM((rows, 2 * NF), F32),
        pltpu.VMEM((2, n_sta * cap, 2 * NF), F32),
    ]


def local_kernel(groups, offsets, main, cos_t, sin_t, taper, send_rows, *rest):
    t_odd, t_even, white0, white3 = rest[:4]
    scratch = rest[-6:]
    sends = rest[4:-6]
    fill_tables(cos_t, sin_t, t_odd, t_even)
    start0 = offsets[0]
    start3 = offsets[2] - 2 * STEP
    live3 = jnp.where(lax.axis_index("tm") == lax.axis_size("tm") - 1, 1.0, 0.0).astype(F32)
    stations = main.shape[0]
    for first in range(0, stations, UNIT):
        count = min(UNIT, stations - first)
        get = shifted_rows(main, first)

        def pick0(rows, c):
            if c >= HC:
                return get(rows, HALF, c - HC)
            return jnp.where(slots(c) >= start0, get(rows, 0, c), get(rows, 2 * HALF, c))

        def pick3(rows, c):
            if c >= HC:
                return jnp.zeros((ROWS, LANES), F32)
            return jnp.where(slots(c) >= start3, get(rows, 2 * HALF, c), 0.0)

        for pick, start, live, white in ((pick0, start0, 1.0, white0), (pick3, start3, live3, white3)):
            prepare(pick, start, count, 0, taper, scratch)
            transform(count, t_odd, t_even, scratch)
            whiten_rows(0, count, live, white.at[first : first + count], scratch)
    outgoing(send_rows, 0, (white0, white3), None, scratch[5])
    write_rows(groups, scratch[5], sends)


def peer(d, g, n):
    if d == "own":
        return g
    if d == "even":
        return g + 1 - 2 * (g % 2)
    if d == "odd":
        return (g - 1 + 2 * (g % 2) + n) % n
    return (g + d) % n


def swap_routes(n):
    routes = []
    for first in (0, 1):
        partner = list(range(n))
        for i in range(first, n - 1, 2):
            partner[i], partner[i + 1] = i + 1, i
        routes.append(list(enumerate(partner)))
    return routes


def pack_kernel(first, count, n_small, head, offsets, main, *rest):
    small = rest[:n_small]
    outs = rest[n_small : n_small + 2]
    small_out = rest[n_small + 2 : 2 * n_small + 2]
    offsets_out = rest[2 * n_small + 2]
    sems = rest[-1]
    t = lax.axis_index("tm")
    n = lax.axis_size("tm")

    def edge(swap):
        at = jnp.where(t % 2 == swap, 2 * HALF, 0)
        lanes = pl.ds(pl.multiple_of(at, LANES), HALF)
        source = main.at[pl.ds(first, count), lanes]
        return pltpu.make_async_copy(source, outs[swap].at[pl.ds(0, count)], sems.at[swap])

    copies = []
    for swap in range(2):
        if n % 2 == swap:
            copies.append(edge(swap))
            copies[-1].start()
        else:
            @pl.when(t == n - 1)
            def _():
                outs[swap][0:count, :] = jnp.zeros((count, HALF), BF16)

            @pl.when(t < n - 1)
            def _():
                edge(swap).start()
    for k in range(n_small):
        copies.append(pltpu.make_async_copy(small[k], small_out[k], sems.at[3 + k]))
        copies[-1].start()
    if head:
        numbers = pltpu.make_async_copy(offsets, offsets_out, sems.at[2])
        numbers.start()
        numbers.wait()
        start = offsets_out[2] - 2 * STEP
        high, low = start // 8, start % 8
        lane = lax.broadcasted_iota(jnp.int32, (ROWS, HALF), 1)
        for out in outs:
            out[count:, :] = jnp.where(lane < NF, high, low).astype(F32).astype(BF16)
    for copy in copies:
        copy.wait()
    for swap in range(2):
        if n % 2 != swap:
            @pl.when(t < n - 1)
            def _():
                edge(swap).wait()


def sent_start(ref):
    rows = ref.shape[0] - ROWS
    high = jnp.max(ref[rows:, 0:LANES].astype(F32))
    low = jnp.max(ref[rows:, HALF - LANES :].astype(F32))
    return (high * 8.0 + low).astype(jnp.int32)


def rim_kernel(groups, first, earlier, last, offsets, main, *rest):
    recv = rest[:2]
    heads = rest[2:4] if earlier else recv
    rest = rest[4 if earlier else 2 :]
    taper, t_odd, t_even, send_rows = rest[:4]
    rest = rest[4:]
    before = rest[0] if earlier else None
    rest = rest[1:] if earlier else rest
    whites = rest[:2]
    scratch = rest[-6:]
    sends = rest[2:-6]
    count = whites[0].shape[0]
    t = lax.axis_index("tm")
    lane = lax.broadcasted_iota(jnp.int32, (ROWS, LANES), 1)
    for swap in range(2):
        ahead = t % 2 == swap
        start = jnp.where(ahead, offsets[1] - STEP, sent_start(heads[swap]))
        sign = jnp.where(ahead, 1, -1)
        least = jnp.where(ahead, 0, 1)
        whole = jnp.where(ahead, 2 * HALF, 0)
        base = (lane - start) * sign

        def pick(rows, c):
            at = pl.ds(pl.multiple_of(rows.start + first, ROWS), ROWS)
            if c >= HC:
                return main[at, pl.ds(pl.multiple_of(whole + (c - HC) * LANES, LANES), LANES)].astype(F32)
            own = part(main, HALF, at, c)
            return jnp.where(base >= least - sign * (c * LANES), own, part(recv[swap], 0, rows, c))

        prepare(pick, start, count, swap * count, taper, scratch)
    transform(2 * count, t_odd, t_even, scratch)
    live = jnp.where(t > 0, 1.0, 0.0).astype(F32)
    whiten_rows(0, count, 1.0, whites[0], scratch)
    whiten_rows(count, count, live, whites[1], scratch)
    if last:
        outgoing(send_rows, first, whites, before, scratch[5])
        write_rows(groups, scratch[5], sends)
    else:
        outgoing(send_rows, first, whites, before, sends[0])


def slot_table(groups, pair_slot, width):
    near, far, n_sta, cap = groups
    g = lax.axis_index("sta")
    slot = pair_slot[...]
    place = jnp.zeros_like(slot)
    at = 0
    for d in near + far:
        source = (g - d + n_sta) % n_sta if d in far else peer(d, g, n_sta)
        place = jnp.where(slot // cap == source, at + slot % cap, place)
        at += CAP_FAR if d in far else cap
    return one_hot(column(place), width)


def second_rows(groups, pieces, hot, first_pair, incoming, out):
    near, far, _, cap = groups
    width = incoming.shape[1]
    for w in range(2):
        at = 0
        for i, d in enumerate(near + far):
            n = CAP_FAR if d in far else cap
            incoming[w, at : at + n, :] = pieces[i][w * n : (w + 1) * n, :]
            at += n
        if at < width:
            incoming[w, at:, :] = jnp.zeros((width - at, 2 * NF), BF16)
    for w in range(2):
        for c in range(0, 2 * NF, NF):
            rows = hot[first_pair : first_pair + out.shape[1], :]
            out[w, :, c : c + NF] = jnp.dot(rows, incoming[w, :, c : c + NF], preferred_element_type=F32)


def first_rows(hots, spectra, scale, out):
    lane = lax.broadcasted_iota(jnp.int32, (1, QB), 1)
    s = jnp.where(lane % 2 == 0, scale, -scale).astype(F32)
    for c in range(0, 2 * NF, QB):
        total = None
        for hot, piece in zip(hots, spectra):
            term = jnp.dot(hot, piece[:, c : c + QB], preferred_element_type=F32)
            total = term if total is None else total + term
        out[:, c : c + QB] = total * (s if c % NF == 0 else -s)


def station_tables(col, spectra):
    hots, at = [], 0
    for piece in spectra:
        hots.append(one_hot(col, piece.shape[0], at))
        at += piece.shape[0]
    return hots


def add_products(first, second, first_at, second_at, c, start):
    re_lanes = slice(c, c + LANES)
    im_lanes = slice(NF + c, NF + c + LANES)
    one, two = start
    for w in range(2):
        a_i, b_i = first[w, first_at, re_lanes], first[w, first_at, im_lanes]
        a_j, b_j = second[w, second_at, re_lanes], second[w, second_at, im_lanes]
        re = a_i * a_j + b_i * b_j
        im = b_i * a_j - a_i * b_j
        if c < QB:
            one, two = one + im, two - re
        else:
            one, two = one + re, two + im
    return one, two


def early_kernel(groups, n_pieces, n_white, scale, pair_first, pair_slot, white0, white3, *rest):
    whites = rest[: 2 * n_white]
    rest = rest[2 * n_white :]
    pieces = rest[:n_pieces]
    cross, later, hot = rest[n_pieces : n_pieces + 3]
    incoming, first, second = rest[n_pieces + 3 :]
    pairs = pair_first.shape[1]
    col = column(pair_first[...])
    hots = station_tables(col, (white0,))
    first_rows(hots, (white0,), scale, first.at[0])
    first_rows(hots, (white3,), scale, first.at[1])
    hot[...] = slot_table(groups, pair_slot, hot.shape[1])
    second_rows(groups, pieces, hot, 0, incoming, second)

    def group(i, carry):
        rows = pl.ds(pl.multiple_of(i * ROWS, ROWS), ROWS)
        for c in range(0, NF, LANES):
            one, two = add_products(first, second, rows, rows, c, (0.0, 0.0))
            cross[rows, c : c + LANES] = one
            cross[rows, NF + c : NF + c + LANES] = two
        return carry

    loop(pairs, 2, group)
    hots = station_tables(col, whites[0::2])
    first_rows(hots, whites[0::2], scale, later.at[0])
    first_rows(hots, whites[1::2], scale, later.at[1])


def late_kernel(groups, n_pieces, n_dest, first_pair, early, first, hot, t_odd, t_even, *rest):
    pieces = rest[:n_pieces]
    send, keep = rest[n_pieces : n_pieces + 2]
    incoming, second, x_odd, x_even = rest[n_pieces + 2 :]
    pairs = send.shape[1]
    second_rows(groups, pieces, hot, first_pair, incoming, second)

    def group(i, carry):
        rows = pl.ds(pl.multiple_of(i * ROWS, ROWS), ROWS)
        full = pl.ds(pl.multiple_of(first_pair + i * ROWS, ROWS), ROWS)
        for c in range(0, NF, LANES):
            start = (early[full, c : c + LANES], early[full, NF + c : NF + c + LANES])
            one, two = add_products(first, second, full, rows, c, start)
            out = x_odd if c < QB else x_even
            at = c % QB
            out[rows, at : at + LANES] = one.astype(BF16)
            out[rows, QB + at : QB + at + LANES] = two.astype(BF16)
        return carry

    loop(pairs, 2, group)
    lag_rows = NL // n_dest
    me = lax.axis_index("tm")
    dims = (((1,), (1,)), ((), ()))
    for out, order in ((send, range(1, n_dest, 2)), (keep, range(0, n_dest, 2))):
        spots = [
            pl.ds(pl.multiple_of(jnp.bitwise_xor(me, r) * lag_rows, lag_rows), lag_rows) for r in order
        ]
        odd = jnp.concatenate([t_odd[at, :] for at in spots], axis=0)
        even = jnp.concatenate([t_even[at, :] for at in spots], axis=0)
        value = lax.dot_general(odd, x_odd[...], dims, preferred_element_type=F32)
        value = value + lax.dot_general(even, x_even[...], dims, preferred_element_type=F32)
        out[...] = value.astype(out.dtype)


def merge_kernel(lag_rows, keep, received, send, kept):
    for k in range(keep.shape[0] // lag_rows):
        rows = slice(k * lag_rows, (k + 1) * lag_rows)
        out, j = (send, k // 2) if k % 2 else (kept, k // 2)
        value = keep[rows, :] + received[rows, :].astype(F32)
        out[j * lag_rows : (j + 1) * lag_rows, :] = value.astype(out.dtype)


def finish_kernel(*refs):
    out = refs[-1]
    at = 0
    for keep, received in zip(refs[0:-1:2], refs[1:-1:2]):
        width = keep.shape[1]
        out[:, at : at + width] = keep[...] + received[...].astype(F32)
        at += width


def in_vmem(*arrays):
    return [pltpu.with_memory_space_constraint(a, pltpu.VMEM) for a in arrays]


def in_smem(*arrays):
    return [pltpu.with_memory_space_constraint(a, pltpu.SMEM) for a in arrays]


def in_hbm(*arrays):
    return [pltpu.with_memory_space_constraint(a, pltpu.HBM) for a in arrays]


def params(mib):
    return pltpu.CompilerParams(vmem_limit_bytes=mib << 20)


def cost(flops, moved):
    return pl.CostEstimate(flops=int(flops), bytes_accessed=int(moved), transcendentals=0)


def on_device(traces, offsets, pair_first, pair_slot, send_rows):
    stations, _ = traces.shape
    n_tm = lax.axis_size("tm")
    n_sta = lax.axis_size("sta")
    windows = offsets.shape[0]
    pairs = pair_first.shape[0]
    cap = send_rows.shape[1] // n_sta

    sizes = (stations * 5 // 8, stations * 3 // 8)
    n_chunks = len(sizes)
    main, = in_vmem(traces)
    routes = swap_routes(n_tm)
    small = [jnp.asarray(x) for x in small_tables()] + [jnp.asarray(taper_row()), send_rows]
    edges = []
    for i, rows in enumerate(sizes):
        head = i == 0
        extra = [] if head else small
        packed = pl.pallas_call(
            functools.partial(pack_kernel, sum(sizes[:i]), rows, len(extra), head),
            out_shape=[pltpu.VMEM((rows + (ROWS if head else 0), HALF), BF16)] * 2
            + [pltpu.VMEM(x.shape, x.dtype) for x in extra]
            + [pltpu.SMEM(offsets.shape, jnp.int32)],
            in_specs=[ANY] * (2 + len(extra)),
            out_specs=[VMEM] * (2 + len(extra)) + [SMEM],
            scratch_shapes=[pltpu.SemaphoreType.DMA((3 + len(extra),))],
            compiler_params=params(1),
            cost_estimate=cost(0, 2 << 20),
        )(*in_hbm(offsets, traces, *extra))
        if head:
            starts = packed[-1]
        else:
            cos_t, sin_t, taper, send_rows = packed[2:-1]
        got = [None, None]
        for swap in (0, 1):
            got[swap] = lax.ppermute(packed[swap], "tm", routes[swap])
        edges += got

    near = ["own", "even", "odd"]
    far = list(range(2, n_sta - 1))
    groups = (near, far, n_sta, cap)
    width = -(-(len(near) * cap + len(far) * CAP_FAR) // LANES) * LANES
    first_row, slot_row = pair_first[None, :], pair_slot[None, :]

    buffers = [pltpu.VMEM((2 * (CAP_FAR if d in far else cap), 2 * NF), BF16) for d in near + far]
    dft_flops = 2 * 2 * HALF * 2 * QB * 2
    spectrum = pltpu.VMEM((stations, 2 * NF), BF16)
    table = pltpu.VMEM((HALF, 2 * QB), BF16)
    local = pl.pallas_call(
        functools.partial(local_kernel, groups),
        out_shape=[table] * 2 + [spectrum] * 2 + buffers,
        in_specs=[SMEM] + [VMEM] * 5,
        out_specs=[VMEM] * (4 + len(buffers)),
        scratch_shapes=scratches(n_sta, cap, UNIT),
        compiler_params=params(18),
        cost_estimate=cost(dft_flops * stations, 8 << 20),
        name="local_windows",
    )(*in_smem(starts), *in_vmem(main, cos_t, sin_t, taper, send_rows))
    t_odd, t_even, white0, white3 = local[:4]

    def exchange(pieces):
        got = list(pieces)
        for i, d in enumerate(near + far):
            if d != "own":
                route = [(k, peer(d, k, n_sta)) for k in range(n_sta)]
                got[i] = lax.ppermute(pieces[i], "sta", route)
        return got

    early_in = exchange(local[4:])
    scale = 1.0 / math.sqrt(NF * windows * n_tm)
    pair_scratch = [
        pltpu.VMEM((2, width, 2 * NF), BF16),
        pltpu.VMEM((2, pairs, 2 * NF), F32),
        pltpu.VMEM((2, pairs, 2 * NF), F32),
    ]
    whites = []
    late_out = []
    outgoing_rows = pltpu.VMEM((2, n_sta * cap, 2 * NF), F32)
    for i in range(n_chunks):
        last = i == n_chunks - 1
        rows = sizes[i]
        chunk = pltpu.VMEM((rows, 2 * NF), BF16)
        result = pl.pallas_call(
            functools.partial(rim_kernel, groups, sum(sizes[:i]), i, last),
            out_shape=[chunk] * 2 + (buffers if last else [outgoing_rows]),
            in_specs=[SMEM] + [VMEM] * (7 + 3 * min(i, 1)),
            out_specs=[VMEM] * (2 + (len(buffers) if last else 1)),
            scratch_shapes=scratches(n_sta, cap, 2 * rows),
            compiler_params=params(22),
            cost_estimate=cost(dft_flops * rows, 4 << 20),
        )(
            *in_smem(starts),
            *in_vmem(main, *edges[2 * i : 2 * i + 2], *(edges[:2] if i else [])),
            *in_vmem(taper, t_odd, t_even, send_rows, *late_out),
        )
        whites = whites + list(result[:2])
        late_out = result[2:]
    late_in = exchange(late_out)
    early, first, hot = pl.pallas_call(
        functools.partial(early_kernel, groups, len(buffers), n_chunks, scale),
        out_shape=[
            pltpu.VMEM((pairs, 2 * NF), F32),
            pltpu.VMEM((2, pairs, 2 * NF), F32),
            pltpu.VMEM((pairs, width), BF16),
        ],
        in_specs=[VMEM] * (4 + 2 * n_chunks + len(buffers)),
        out_specs=[VMEM] * 3,
        scratch_shapes=pair_scratch,
        compiler_params=params(16),
        cost_estimate=cost(2 * 2 * pairs * (2 * stations + width) * 2 * NF, 4 << 20),
        name="early_pairs",
    )(first_row, slot_row, *in_vmem(white0, white3, *whites, *early_in))

    lag_rows = NL // n_tm
    n_half = 2
    half = pairs // n_half
    steps = [1 << k for k in range(n_tm.bit_length() - 1)]
    done = []
    parts = []
    for h in range(n_half):
        parts.append(
            pl.pallas_call(
                functools.partial(late_kernel, groups, len(buffers), n_tm, h * half),
                out_shape=[pltpu.VMEM((NL // 2, half), BF16), pltpu.VMEM((NL // 2, half), F32)],
                in_specs=[VMEM] * (5 + len(buffers)),
                out_specs=[VMEM] * 2,
                scratch_shapes=[
                    pltpu.VMEM((2, width, 2 * NF), BF16),
                    pltpu.VMEM((2, half, 2 * NF), F32),
                    pltpu.VMEM((half, NF), BF16),
                    pltpu.VMEM((half, NF), BF16),
                ],
                compiler_params=params(10),
                cost_estimate=cost(2 * 2 * half * width * 2 * NF + 2 * NL * half * 2 * NF, 3 << 20),
            )(*in_vmem(early, first, hot, t_odd, t_even, *late_in))
        )
    for step in steps:
        route = [(i, i ^ step) for i in range(n_tm)]
        received = [lax.ppermute(send, "tm", route) for send, _ in parts]
        if step == steps[-1]:
            done = [x for (_, keep), got in zip(parts, received) for x in (keep, got)]
            break
        merged = []
        for h in range(n_half):
            keep = parts[h][1]
            rows = keep.shape[0] // 2
            merged.append(
                pl.pallas_call(
                    functools.partial(merge_kernel, lag_rows),
                    out_shape=[pltpu.VMEM((rows, half), BF16), pltpu.VMEM((rows, half), F32)],
                    in_specs=[VMEM] * 2,
                    out_specs=[VMEM] * 2,
                    compiler_params=params(1),
                    cost_estimate=cost(rows * half, 1 << 20),
                )(*in_vmem(keep, received[h]))
            )
        parts = merged
    return pl.pallas_call(
        finish_kernel,
        out_shape=jax.ShapeDtypeStruct((lag_rows, pairs), F32),
        in_specs=[VMEM] * len(done),
        out_specs=VMEM,
        compiler_params=params(2),
        cost_estimate=cost(lag_rows * pairs, 1 << 20),
        name="finish",
    )(*in_vmem(*done))


def solution(mesh):
    in_specs = (P("sta", ("day", "tm")), P(("day", "tm")), P("sta"), P("sta"), P("sta", None))
    out_specs = P(("day", "tm"), "sta")
    return jax.shard_map(
        on_device, mesh=mesh, in_specs=in_specs, out_specs=out_specs, check_vma=False
    )
```

```python
import functools
import math

import jax
import jax.numpy as jnp
import numpy as np
from jax import lax
from jax.experimental import pallas as pl
from jax.experimental.pallas import tpu as pltpu
from jax.sharding import PartitionSpec as P


WIN = 2048
NF = 512
NL = 1024
FLOOR = 0.1
STEP = 1024
HALF = 1024
CAP_FAR = 8
LANES = 128
CHUNKS = WIN // LANES
HC = CHUNKS // 2
QB = NF // 2
ROOT = 1.0 / math.sqrt(WIN)
F32 = jnp.float32
BF16 = jnp.bfloat16
ROWS = 16
UNIT = 512
VMEM = pl.BlockSpec(memory_space=pltpu.VMEM)
SMEM = pl.BlockSpec(memory_space=pltpu.SMEM)
ANY = pl.BlockSpec(memory_space=pltpu.HBM)


def loop(count, most, body):
    trips = count // ROWS
    unroll = max(u for u in range(1, most + 1) if trips % u == 0)
    lax.fori_loop(0, trips, body, 0, unroll=unroll)


def small_tables():
    step = np.arange(32)[:, None]
    half = np.arange(QB)
    freq = np.concatenate([2 * half + 1, 2 * half + 2])[None, :]
    angles = np.concatenate([32 * step, step], axis=0) * freq % WIN * (2.0 * np.pi / WIN)
    return np.cos(angles).astype(np.float32), np.sin(angles).astype(np.float32)


def taper_row():
    index = np.arange(WIN)
    return (0.5 - 0.5 * np.cos(2.0 * np.pi * index / WIN)).astype(np.float32)[None, :]


def fill_tables(cos_ref, sin_ref, odd_ref, even_ref):
    def block(a, carry):
        ca = cos_ref[pl.ds(a, 1), :]
        sa = sin_ref[pl.ds(a, 1), :]
        cb = cos_ref[32:64, :]
        sb = sin_ref[32:64, :]
        c = (ca * cb - sa * sb).astype(BF16)
        s = (-(sa * cb + ca * sb)).astype(BF16)
        rows = pl.ds(pl.multiple_of(a * 32, 32), 32)
        odd_ref[rows, :QB] = c[:, :QB]
        odd_ref[rows, QB:] = s[:, :QB]
        even_ref[rows, :QB] = c[:, QB:]
        even_ref[rows, QB:] = s[:, QB:]
        return carry

    lax.fori_loop(0, HALF // 32, block, 0)


def prepare(pick, start, count, to, taper_ref, scratch):
    rolled_ref, sums_ref, even_ref, odd_ref = scratch[:4]
    q = start // LANES
    s = start % LANES
    shift = (LANES - s) % LANES
    places = [(c + q) % CHUNKS for c in range(CHUNKS)]
    keep = lax.broadcasted_iota(jnp.int32, (ROWS, LANES), 1) < LANES - s

    def turn(i, carry):
        rows = pl.ds(pl.multiple_of(i * ROWS, ROWS), ROWS)
        rolled = [pltpu.roll(pick(rows, c).astype(F32), shift, 1) for c in range(CHUNKS)]
        turned = [jnp.where(keep, rolled[c], rolled[(c + 1) % CHUNKS]) for c in range(CHUNKS)]
        for c in range(CHUNKS):
            rolled_ref[c, rows, :] = turned[c]
        while len(turned) > 1:
            turned = [turned[2 * k] + turned[2 * k + 1] for k in range(len(turned) // 2)]
        sums_ref[rows, :] = turned[0]
        return carry

    loop(count, 4, turn)

    def average(i, carry):
        rows = pl.ds(pl.multiple_of(i * ROWS, ROWS), ROWS)
        mean = jnp.sum(sums_ref[rows, :], axis=1, keepdims=True) * (1.0 / WIN)
        sums_ref[rows, :] = jnp.broadcast_to(mean, (ROWS, LANES))
        return carry

    loop(count, 16, average)

    def fold(i, carry):
        rows = pl.ds(pl.multiple_of(i * ROWS, ROWS), ROWS)
        put = pl.ds(pl.multiple_of(to + i * ROWS, ROWS), ROWS)
        mean = sums_ref[rows, :]
        for c in range(HC):
            low = rolled_ref[places[c], rows, :]
            high = rolled_ref[places[c + HC], rows, :]
            low = ((low - mean) * taper_ref[:, c * LANES : (c + 1) * LANES]).astype(BF16)
            high = (high - mean) * taper_ref[:, (c + HC) * LANES : (c + HC + 1) * LANES]
            high = high.astype(BF16)
            even_ref[c, put, :] = low + high
            odd_ref[c, put, :] = low - high
        return carry

    loop(count, 4, fold)


def transform(count, t_odd, t_even, scratch):
    even_ref, odd_ref, spec = scratch[2:5]
    odd = jnp.concatenate([odd_ref[c, :count] for c in range(HC)], axis=1)
    spec[:count, : 2 * QB] = jnp.dot(odd, t_odd[...], preferred_element_type=F32)
    even = jnp.concatenate([even_ref[c, :count] for c in range(HC)], axis=1)
    spec[:count, 2 * QB :] = jnp.dot(even, t_even[...], preferred_element_type=F32)


def whiten_rows(first_row, count, live, out_ref, scratch):
    spec_ref = scratch[4]
    lane = lax.broadcasted_iota(jnp.int32, (ROWS, LANES), 1)
    not_first = lane > 0
    not_last = lane < LANES - 1
    numerator = live * (5.0 * ROOT)

    def up(x):
        a, b = (pltpu.roll(h, 1, 1) for h in x)
        return jnp.where(not_first, a, 0.0), jnp.where(not_first, b, a)

    def down(x):
        a, b = (pltpu.roll(h, LANES - 1, 1) for h in x)
        return jnp.where(not_last, a, b), jnp.where(not_last, b, 0.0)

    def amplitude(re, im):
        power = (re * re + im * im) * (1.0 / WIN) + 1e-06
        return power * lax.rsqrt(power)

    def inverse(*terms):
        return [
            numerator / jnp.maximum(a + b + c, 5.0 * FLOOR) for a, b, c in zip(*terms)
        ]

    def group(i, carry):
        rows = pl.ds(pl.multiple_of(first_row + i * ROWS, ROWS), ROWS)
        to = pl.ds(pl.multiple_of(i * ROWS, ROWS), ROWS)
        parts = [
            [spec_ref[rows, k * QB + h * LANES : k * QB + (h + 1) * LANES] for h in range(2)]
            for k in range(4)
        ]
        odd = [amplitude(parts[0][h], parts[1][h]) for h in range(2)]
        even = [amplitude(parts[2][h], parts[3][h]) for h in range(2)]
        both = [odd[h] + even[h] for h in range(2)]
        inv_odd = inverse(up(both), both, down(odd))
        inv_even = inverse(up(even), both, down(both))
        for h in range(2):
            at = h * LANES
            for k, j, inv in ((0, 0, inv_odd), (1, 2, inv_odd), (2, 1, inv_even), (3, 3, inv_even)):
                out_ref[to, j * QB + at : j * QB + at + LANES] = (parts[k][h] * inv[h]).astype(BF16)
        return carry

    loop(count, 12, group)


def slots(c):
    return c * LANES + lax.broadcasted_iota(jnp.int32, (ROWS, LANES), 1)


def part(ref, offset, rows, c):
    return ref[rows, offset + c * LANES : offset + (c + 1) * LANES].astype(F32)


def shifted_rows(ref, first):
    def get(rows, offset, c):
        at = pl.ds(pl.multiple_of(rows.start + first, ROWS), ROWS)
        return part(ref, offset, at, c)

    return get


def column(row):
    n = row.shape[1]
    return jnp.transpose(jnp.broadcast_to(row.astype(F32), (LANES, n)))


def one_hot(col, width, first=0):
    pieces = []
    for at in range(0, width, LANES):
        lane = lax.broadcasted_iota(jnp.int32, col.shape, 1) + (first + at)
        pieces.append(jnp.where(lane.astype(F32) == col, 1.0, 0.0).astype(BF16))
    hot = pieces[0] if len(pieces) == 1 else jnp.concatenate(pieces, axis=1)
    return hot[:, :width]


def outgoing(send_rows, first, spectra, before, out):
    col = column(send_rows[...])
    hot = one_hot(col, spectra[0].shape[0], first)
    for w in range(2):
        value = jnp.dot(hot, spectra[w][...], preferred_element_type=F32)
        out[w] = value if before is None else before[w] + value


def write_rows(groups, rows, refs):
    near, far, n_sta, cap = groups
    g = lax.axis_index("sta")
    for ref, d in zip(refs, near + far):
        first = pl.multiple_of(peer(d, g, n_sta) * cap, cap)
        n = CAP_FAR if d in far else cap
        for w in range(2):
            ref[w * n : (w + 1) * n, :] = rows[w, pl.ds(first, n), :].astype(BF16)


def scratches(n_sta, cap, rows):
    return [
        pltpu.VMEM((CHUNKS, rows, LANES), F32),
        pltpu.VMEM((rows, LANES), F32),
        pltpu.VMEM((HC, rows, LANES), BF16),
        pltpu.VMEM((HC, rows, LANES), BF16),
        pltpu.VMEM((rows, 2 * NF), F32),
        pltpu.VMEM((2, n_sta * cap, 2 * NF), F32),
    ]


def local_kernel(groups, offsets, main, cos_t, sin_t, taper, send_rows, *rest):
    t_odd, t_even, white0, white3 = rest[:4]
    scratch = rest[-6:]
    sends = rest[4:-6]
    fill_tables(cos_t, sin_t, t_odd, t_even)
    start0 = offsets[0]
    start3 = offsets[2] - 2 * STEP
    live3 = jnp.where(lax.axis_index("tm") == lax.axis_size("tm") - 1, 1.0, 0.0).astype(F32)
    stations = main.shape[0]
    for first in range(0, stations, UNIT):
        count = min(UNIT, stations - first)
        get = shifted_rows(main, first)

        def pick0(rows, c):
            if c >= HC:
                return get(rows, HALF, c - HC)
            return jnp.where(slots(c) >= start0, get(rows, 0, c), get(rows, 2 * HALF, c))

        def pick3(rows, c):
            if c >= HC:
                return jnp.zeros((ROWS, LANES), F32)
            return jnp.where(slots(c) >= start3, get(rows, 2 * HALF, c), 0.0)

        for pick, start, live, white in ((pick0, start0, 1.0, white0), (pick3, start3, live3, white3)):
            prepare(pick, start, count, 0, taper, scratch)
            transform(count, t_odd, t_even, scratch)
            whiten_rows(0, count, live, white.at[first : first + count], scratch)
    outgoing(send_rows, 0, (white0, white3), None, scratch[5])
    write_rows(groups, scratch[5], sends)


def peer(d, g, n):
    if d == "own":
        return g
    if d == "even":
        return g + 1 - 2 * (g % 2)
    if d == "odd":
        return (g - 1 + 2 * (g % 2) + n) % n
    return (g + d) % n


def swap_routes(n):
    routes = []
    for first in (0, 1):
        partner = list(range(n))
        for i in range(first, n - 1, 2):
            partner[i], partner[i + 1] = i + 1, i
        routes.append(list(enumerate(partner)))
    return routes


def pack_kernel(first, count, n_small, head, offsets, main, *rest):
    small = rest[:n_small]
    outs = rest[n_small : n_small + 2]
    small_out = rest[n_small + 2 : 2 * n_small + 2]
    offsets_out = rest[2 * n_small + 2]
    sems = rest[-1]
    t = lax.axis_index("tm")
    n = lax.axis_size("tm")

    def edge(swap):
        at = jnp.where(t % 2 == swap, 2 * HALF, 0)
        lanes = pl.ds(pl.multiple_of(at, LANES), HALF)
        source = main.at[pl.ds(first, count), lanes]
        return pltpu.make_async_copy(source, outs[swap].at[pl.ds(0, count)], sems.at[swap])

    copies = []
    for swap in range(2):
        if n % 2 == swap:
            copies.append(edge(swap))
            copies[-1].start()
        else:
            @pl.when(t == n - 1)
            def _():
                outs[swap][0:count, :] = jnp.zeros((count, HALF), BF16)

            @pl.when(t < n - 1)
            def _():
                edge(swap).start()
    for k in range(n_small):
        copies.append(pltpu.make_async_copy(small[k], small_out[k], sems.at[3 + k]))
        copies[-1].start()
    if head:
        numbers = pltpu.make_async_copy(offsets, offsets_out, sems.at[2])
        numbers.start()
        numbers.wait()
        start = offsets_out[2] - 2 * STEP
        high, low = start // 8, start % 8
        lane = lax.broadcasted_iota(jnp.int32, (ROWS, HALF), 1)
        for out in outs:
            out[count:, :] = jnp.where(lane < NF, high, low).astype(F32).astype(BF16)
    for copy in copies:
        copy.wait()
    for swap in range(2):
        if n % 2 != swap:
            @pl.when(t < n - 1)
            def _():
                edge(swap).wait()


def sent_start(ref):
    rows = ref.shape[0] - ROWS
    high = jnp.max(ref[rows:, 0:LANES].astype(F32))
    low = jnp.max(ref[rows:, HALF - LANES :].astype(F32))
    return (high * 8.0 + low).astype(jnp.int32)


def rim_kernel(groups, first, earlier, last, offsets, main, *rest):
    recv = rest[:2]
    heads = rest[2:4] if earlier else recv
    rest = rest[4 if earlier else 2 :]
    taper, t_odd, t_even, send_rows = rest[:4]
    rest = rest[4:]
    before = rest[0] if earlier else None
    rest = rest[1:] if earlier else rest
    whites = rest[:2]
    scratch = rest[-6:]
    sends = rest[2:-6]
    count = whites[0].shape[0]
    t = lax.axis_index("tm")
    lane = lax.broadcasted_iota(jnp.int32, (ROWS, LANES), 1)
    for swap in range(2):
        ahead = t % 2 == swap
        start = jnp.where(ahead, offsets[1] - STEP, sent_start(heads[swap]))
        sign = jnp.where(ahead, 1, -1)
        least = jnp.where(ahead, 0, 1)
        whole = jnp.where(ahead, 2 * HALF, 0)
        base = (lane - start) * sign

        def pick(rows, c):
            at = pl.ds(pl.multiple_of(rows.start + first, ROWS), ROWS)
            if c >= HC:
                return main[at, pl.ds(pl.multiple_of(whole + (c - HC) * LANES, LANES), LANES)].astype(F32)
            own = part(main, HALF, at, c)
            return jnp.where(base >= least - sign * (c * LANES), own, part(recv[swap], 0, rows, c))

        prepare(pick, start, count, swap * count, taper, scratch)
    transform(2 * count, t_odd, t_even, scratch)
    live = jnp.where(t > 0, 1.0, 0.0).astype(F32)
    whiten_rows(0, count, 1.0, whites[0], scratch)
    whiten_rows(count, count, live, whites[1], scratch)
    if last:
        outgoing(send_rows, first, whites, before, scratch[5])
        write_rows(groups, scratch[5], sends)
    else:
        outgoing(send_rows, first, whites, before, sends[0])


def slot_table(groups, pair_slot, width):
    near, far, n_sta, cap = groups
    g = lax.axis_index("sta")
    slot = pair_slot[...]
    place = jnp.zeros_like(slot)
    at = 0
    for d in near + far:
        source = (g - d + n_sta) % n_sta if d in far else peer(d, g, n_sta)
        place = jnp.where(slot // cap == source, at + slot % cap, place)
        at += CAP_FAR if d in far else cap
    return one_hot(column(place), width)


def second_rows(groups, pieces, hot, first_pair, incoming, out):
    near, far, _, cap = groups
    width = incoming.shape[1]
    for w in range(2):
        at = 0
        for i, d in enumerate(near + far):
            n = CAP_FAR if d in far else cap
            incoming[w, at : at + n, :] = pieces[i][w * n : (w + 1) * n, :]
            at += n
        if at < width:
            incoming[w, at:, :] = jnp.zeros((width - at, 2 * NF), BF16)
    for w in range(2):
        for c in range(0, 2 * NF, NF):
            rows = hot[first_pair : first_pair + out.shape[1], :]
            out[w, :, c : c + NF] = jnp.dot(rows, incoming[w, :, c : c + NF], preferred_element_type=F32)


def first_rows(hots, spectra, scale, out):
    lane = lax.broadcasted_iota(jnp.int32, (1, QB), 1)
    s = jnp.where(lane % 2 == 0, scale, -scale).astype(F32)
    for c in range(0, 2 * NF, QB):
        total = None
        for hot, piece in zip(hots, spectra):
            term = jnp.dot(hot, piece[:, c : c + QB], preferred_element_type=F32)
            total = term if total is None else total + term
        out[:, c : c + QB] = total * (s if c % NF == 0 else -s)


def station_tables(col, spectra):
    hots, at = [], 0
    for piece in spectra:
        hots.append(one_hot(col, piece.shape[0], at))
        at += piece.shape[0]
    return hots


def add_products(first, second, first_at, second_at, c, start):
    re_lanes = slice(c, c + LANES)
    im_lanes = slice(NF + c, NF + c + LANES)
    one, two = start
    for w in range(2):
        a_i, b_i = first[w, first_at, re_lanes], first[w, first_at, im_lanes]
        a_j, b_j = second[w, second_at, re_lanes], second[w, second_at, im_lanes]
        re = a_i * a_j + b_i * b_j
        im = b_i * a_j - a_i * b_j
        if c < QB:
            one, two = one + im, two - re
        else:
            one, two = one + re, two + im
    return one, two


def early_kernel(groups, n_pieces, n_white, scale, pair_first, pair_slot, white0, white3, *rest):
    whites = rest[: 2 * n_white]
    rest = rest[2 * n_white :]
    pieces = rest[:n_pieces]
    cross, later, hot = rest[n_pieces : n_pieces + 3]
    incoming, first, second = rest[n_pieces + 3 :]
    pairs = pair_first.shape[1]
    col = column(pair_first[...])
    hots = station_tables(col, (white0,))
    first_rows(hots, (white0,), scale, first.at[0])
    first_rows(hots, (white3,), scale, first.at[1])
    hot[...] = slot_table(groups, pair_slot, hot.shape[1])
    second_rows(groups, pieces, hot, 0, incoming, second)

    def group(i, carry):
        rows = pl.ds(pl.multiple_of(i * ROWS, ROWS), ROWS)
        for c in range(0, NF, LANES):
            one, two = add_products(first, second, rows, rows, c, (0.0, 0.0))
            cross[rows, c : c + LANES] = one
            cross[rows, NF + c : NF + c + LANES] = two
        return carry

    loop(pairs, 2, group)
    hots = station_tables(col, whites[0::2])
    first_rows(hots, whites[0::2], scale, later.at[0])
    first_rows(hots, whites[1::2], scale, later.at[1])


def late_kernel(groups, n_pieces, n_dest, orders, first_pair, early, first, hot, t_odd, t_even, *rest):
    pieces = rest[:n_pieces]
    outs = rest[n_pieces : n_pieces + len(orders)]
    incoming, second, x_odd, x_even = rest[n_pieces + len(orders) :]
    pairs = x_odd.shape[0]
    second_rows(groups, pieces, hot, first_pair, incoming, second)

    def group(i, carry):
        rows = pl.ds(pl.multiple_of(i * ROWS, ROWS), ROWS)
        full = pl.ds(pl.multiple_of(first_pair + i * ROWS, ROWS), ROWS)
        for c in range(0, NF, LANES):
            start = (early[full, c : c + LANES], early[full, NF + c : NF + c + LANES])
            one, two = add_products(first, second, full, rows, c, start)
            out = x_odd if c < QB else x_even
            at = c % QB
            out[rows, at : at + LANES] = one.astype(BF16)
            out[rows, QB + at : QB + at + LANES] = two.astype(BF16)
        return carry

    loop(pairs, 2, group)
    lag_rows = NL // n_dest
    me = lax.axis_index("tm")
    dims = (((1,), (1,)), ((), ()))
    for out, order in zip(outs, orders):
        spots = [
            pl.ds(pl.multiple_of(jnp.bitwise_xor(me, r) * lag_rows, lag_rows), lag_rows) for r in order
        ]
        odd = jnp.concatenate([t_odd[at, :] for at in spots], axis=0)
        even = jnp.concatenate([t_even[at, :] for at in spots], axis=0)
        value = lax.dot_general(odd, x_odd[...], dims, preferred_element_type=F32)
        value = value + lax.dot_general(even, x_even[...], dims, preferred_element_type=F32)
        out[...] = value.astype(out.dtype)


def merge_kernel(lag_rows, keep, received, send, kept):
    for k in range(keep.shape[0] // lag_rows):
        rows = slice(k * lag_rows, (k + 1) * lag_rows)
        out, j = (send, k // 2) if k % 2 else (kept, k // 2)
        value = keep[rows, :] + received[rows, :].astype(F32)
        out[j * lag_rows : (j + 1) * lag_rows, :] = value.astype(out.dtype)


def finish_kernel(counts, *refs):
    out = refs[-1]
    at = 0
    refs = list(refs[:-1])
    for n in counts:
        total = refs[0][...]
        for received in refs[1:n]:
            total = total + received[...].astype(F32)
        out[:, at : at + total.shape[1]] = total
        at += total.shape[1]
        refs = refs[n:]


def in_vmem(*arrays):
    return [pltpu.with_memory_space_constraint(a, pltpu.VMEM) for a in arrays]


def in_smem(*arrays):
    return [pltpu.with_memory_space_constraint(a, pltpu.SMEM) for a in arrays]


def in_hbm(*arrays):
    return [pltpu.with_memory_space_constraint(a, pltpu.HBM) for a in arrays]


def params(mib):
    return pltpu.CompilerParams(vmem_limit_bytes=mib << 20)


def cost(flops, moved):
    return pl.CostEstimate(flops=int(flops), bytes_accessed=int(moved), transcendentals=0)


def on_device(traces, offsets, pair_first, pair_slot, send_rows):
    stations, _ = traces.shape
    n_tm = lax.axis_size("tm")
    n_sta = lax.axis_size("sta")
    windows = offsets.shape[0]
    pairs = pair_first.shape[0]
    cap = send_rows.shape[1] // n_sta

    sizes = (stations * 5 // 8, stations * 3 // 8)
    n_chunks = len(sizes)
    main, = in_vmem(traces)
    routes = swap_routes(n_tm)
    small = [jnp.asarray(x) for x in small_tables()] + [jnp.asarray(taper_row()), send_rows]
    edges = []
    for i, rows in enumerate(sizes):
        head = i == 0
        extra = [] if head else small
        packed = pl.pallas_call(
            functools.partial(pack_kernel, sum(sizes[:i]), rows, len(extra), head),
            out_shape=[pltpu.VMEM((rows + (ROWS if head else 0), HALF), BF16)] * 2
            + [pltpu.VMEM(x.shape, x.dtype) for x in extra]
            + [pltpu.SMEM(offsets.shape, jnp.int32)],
            in_specs=[ANY] * (2 + len(extra)),
            out_specs=[VMEM] * (2 + len(extra)) + [SMEM],
            scratch_shapes=[pltpu.SemaphoreType.DMA((3 + len(extra),))],
            compiler_params=params(1),
            cost_estimate=cost(0, 2 << 20),
        )(*in_hbm(offsets, traces, *extra))
        if head:
            starts = packed[-1]
        else:
            cos_t, sin_t, taper, send_rows = packed[2:-1]
        got = [None, None]
        for swap in (0, 1):
            got[swap] = lax.ppermute(packed[swap], "tm", routes[swap])
        edges += got

    near = ["own", "even", "odd"]
    far = list(range(2, n_sta - 1))
    groups = (near, far, n_sta, cap)
    width = -(-(len(near) * cap + len(far) * CAP_FAR) // LANES) * LANES
    first_row, slot_row = pair_first[None, :], pair_slot[None, :]

    buffers = [pltpu.VMEM((2 * (CAP_FAR if d in far else cap), 2 * NF), BF16) for d in near + far]
    dft_flops = 2 * 2 * HALF * 2 * QB * 2
    spectrum = pltpu.VMEM((stations, 2 * NF), BF16)
    table = pltpu.VMEM((HALF, 2 * QB), BF16)
    local = pl.pallas_call(
        functools.partial(local_kernel, groups),
        out_shape=[table] * 2 + [spectrum] * 2 + buffers,
        in_specs=[SMEM] + [VMEM] * 5,
        out_specs=[VMEM] * (4 + len(buffers)),
        scratch_shapes=scratches(n_sta, cap, UNIT),
        compiler_params=params(18),
        cost_estimate=cost(dft_flops * stations, 8 << 20),
        name="local_windows",
    )(*in_smem(starts), *in_vmem(main, cos_t, sin_t, taper, send_rows))
    t_odd, t_even, white0, white3 = local[:4]

    def exchange(pieces):
        got = list(pieces)
        for i, d in enumerate(near + far):
            if d != "own":
                route = [(k, peer(d, k, n_sta)) for k in range(n_sta)]
                got[i] = lax.ppermute(pieces[i], "sta", route)
        return got

    early_in = exchange(local[4:])
    scale = 1.0 / math.sqrt(NF * windows * n_tm)
    pair_scratch = [
        pltpu.VMEM((2, width, 2 * NF), BF16),
        pltpu.VMEM((2, pairs, 2 * NF), F32),
        pltpu.VMEM((2, pairs, 2 * NF), F32),
    ]
    whites = []
    late_out = []
    outgoing_rows = pltpu.VMEM((2, n_sta * cap, 2 * NF), F32)
    for i in range(n_chunks):
        last = i == n_chunks - 1
        rows = sizes[i]
        chunk = pltpu.VMEM((rows, 2 * NF), BF16)
        result = pl.pallas_call(
            functools.partial(rim_kernel, groups, sum(sizes[:i]), i, last),
            out_shape=[chunk] * 2 + (buffers if last else [outgoing_rows]),
            in_specs=[SMEM] + [VMEM] * (7 + 3 * min(i, 1)),
            out_specs=[VMEM] * (2 + (len(buffers) if last else 1)),
            scratch_shapes=scratches(n_sta, cap, 2 * rows),
            compiler_params=params(22),
            cost_estimate=cost(dft_flops * rows, 4 << 20),
        )(
            *in_smem(starts),
            *in_vmem(main, *edges[2 * i : 2 * i + 2], *(edges[:2] if i else [])),
            *in_vmem(taper, t_odd, t_even, send_rows, *late_out),
        )
        whites = whites + list(result[:2])
        late_out = result[2:]
    late_in = exchange(late_out)
    early, first, hot = pl.pallas_call(
        functools.partial(early_kernel, groups, len(buffers), n_chunks, scale),
        out_shape=[
            pltpu.VMEM((pairs, 2 * NF), F32),
            pltpu.VMEM((2, pairs, 2 * NF), F32),
            pltpu.VMEM((pairs, width), BF16),
        ],
        in_specs=[VMEM] * (4 + 2 * n_chunks + len(buffers)),
        out_specs=[VMEM] * 3,
        scratch_shapes=pair_scratch,
        compiler_params=params(16),
        cost_estimate=cost(2 * 2 * pairs * (2 * stations + width) * 2 * NF, 4 << 20),
        name="early_pairs",
    )(first_row, slot_row, *in_vmem(white0, white3, *whites, *early_in))

    lag_rows = NL // n_tm
    half = pairs // 2

    def late(h, orders):
        return pl.pallas_call(
            functools.partial(late_kernel, groups, len(buffers), n_tm, orders, h * half),
            out_shape=[
                pltpu.VMEM((len(o) * lag_rows, half), F32 if 0 in o else BF16) for o in orders
            ],
            in_specs=[VMEM] * (5 + len(buffers)),
            out_specs=[VMEM] * len(orders),
            scratch_shapes=[
                pltpu.VMEM((2, width, 2 * NF), BF16),
                pltpu.VMEM((2, half, 2 * NF), F32),
                pltpu.VMEM((half, NF), BF16),
                pltpu.VMEM((half, NF), BF16),
            ],
            compiler_params=params(10),
            cost_estimate=cost(2 * 2 * half * width * 2 * NF + 2 * NL * half * 2 * NF, 3 << 20),
        )(*in_vmem(early, first, hot, t_odd, t_even, *late_in))

    def swapped(x, r):
        return lax.ppermute(x, "tm", [(i, i ^ r) for i in range(n_tm)])

    def halving(h):
        send, keep = late(h, [list(range(1, n_tm, 2)), list(range(0, n_tm, 2))])
        step = 1
        while True:
            received = swapped(send, step)
            if keep.shape[0] == lag_rows:
                return [keep, received]
            rows = keep.shape[0] // 2
            send, keep = pl.pallas_call(
                functools.partial(merge_kernel, lag_rows),
                out_shape=[pltpu.VMEM((rows, half), BF16), pltpu.VMEM((rows, half), F32)],
                in_specs=[VMEM] * 2,
                out_specs=[VMEM] * 2,
                compiler_params=params(1),
                cost_estimate=cost(rows * half, 1 << 20),
            )(*in_vmem(keep, received))
            step *= 2

    def direct(h):
        order = [r for r in (3, 2, 1, 0)]
        outs = late(h, [[r] for r in order])
        got = [swapped(x, r) for r, x in zip(order[:-1], outs)]
        return [outs[-1]] + got

    pieces = [halving(0), direct(1) if n_tm == 4 else halving(1)]
    done = [x for piece in pieces for x in piece]
    return pl.pallas_call(
        functools.partial(finish_kernel, tuple(len(piece) for piece in pieces)),
        out_shape=jax.ShapeDtypeStruct((lag_rows, pairs), F32),
        in_specs=[VMEM] * len(done),
        out_specs=VMEM,
        compiler_params=params(2),
        cost_estimate=cost(lag_rows * pairs, 1 << 20),
        name="finish",
    )(*in_vmem(*done))


def solution(mesh):
    in_specs = (P("sta", ("day", "tm")), P(("day", "tm")), P("sta"), P("sta"), P("sta", None))
    out_specs = P(("day", "tm"), "sta")
    return jax.shard_map(
        on_device, mesh=mesh, in_specs=in_specs, out_specs=out_specs, check_vma=False
    )
```
